32 devices in a mesh: grp: 2 (over y), dep: 4 (over z), hgt: 2 (over x), wid: 2 (over core).
Axes of the slice: x: 2, y: 2, z: 4, core: 2. Of those that a mesh axis runs over, the one named last changes fastest.
Arguments:
- features: bfloat16 [64, 8, 16, 256], P('grp', 'wid', 'dep', 'hgt'), parts along dimension 0, may hold values from -6 to 6
- cotangent: bfloat16 [64, 8, 16, 256], P('grp', 'wid', 'dep', 'hgt'), parts along dimension 0, may hold values from -6 to 6
- w_stem: bfloat16 [3, 3, 3, 32, 32], replicated, may hold values from -0.21875 to 0.21875
- w_middle: bfloat16 [3, 3, 3, 32, 64], replicated, may hold values from -0.21875 to 0.21875
- w_bottom: bfloat16 [3, 3, 3, 64, 128], replicated, may hold values from -0.15625 to 0.15625
- w_rise: bfloat16 [3, 3, 3, 192, 64], replicated, may hold values from -0.078125 to 0.078125
- w_final: bfloat16 [3, 3, 3, 96, 32], replicated, may hold values from -0.125 to 0.125
Outputs:
- output: bfloat16 [64, 8, 16, 256], P('grp', 'wid', 'dep', 'hgt'), parts along dimension 0
- grad_stem: float32 [6, 3, 3, 32, 32], P('grp'), parts along dimension 0
- grad_middle: float32 [6, 3, 3, 32, 64], P('grp'), parts along dimension 0
- grad_bottom: float32 [6, 3, 3, 64, 128], P('grp'), parts along dimension 0
- grad_rise: float32 [6, 3, 3, 192, 64], P('grp'), parts along dimension 0
- grad_final: float32 [6, 3, 3, 96, 32], P('grp'), parts along dimension 0
- half_grad: float32 [64, 4, 8, 128], P('grp', 'wid', 'dep', 'hgt'), parts along dimension 0
The draws below stay inside these ranges and needn't reach their ends.
There are 2 independent parts, one for each index of `grp`. The reference program is written for one: setup_inputs(seed, part) draws one part's arguments, and reference() takes and returns one part's arrays. A program takes and returns all parts, laid end to end along the dimension named above; an argument that names none is the same for every part. Nothing has to cross between parts.
All inputs are finite; a program needn't handle non-finite values.
Results may differ from the reference program's by a relative error of at most 0.012.
Values may be sent and summed in bfloat16 or wider, within the bound.
A program may use at most 128 MiB of HBM per device.

```python
import math
import jax
import jax.numpy as jnp
from jax import lax

F0 = 32
F1 = 64
F2 = 128
NW = 8
ND = 16
NH = 256


def block_scale(own_key, dims, split, least, top_value):
    factor_of, own = 1.0, jax.random.fold_in(own_key, 6)
    for axis_at, parts in split:
        draws = jnp.exp(jax.random.uniform(jax.random.fold_in(own, axis_at), (parts,), jnp.float32, least / len(split), top_value / len(split)))
        factor_of = factor_of * jnp.repeat(draws, dims[axis_at] // parts).reshape([-1 if axis == axis_at else 1 for axis in range(len(dims))])
    return factor_of


def gaussian(stream_key, dims, scale, limit, shards=(), held_as=jnp.bfloat16):
    gain = block_scale(stream_key, dims, shards, -0.22, 0.18) if shards else 1.0
    drawn = jax.random.normal(stream_key, dims, jnp.float32) * scale * gain
    return jnp.minimum(jnp.maximum(drawn, -limit), limit).astype(held_as)


def setup_inputs(seed: int = 0, part: int = 0) -> dict:
    keys = jax.random.split(jax.random.key(seed), 8)
    part_keys = jax.random.split(jax.random.fold_in(keys[7], part), 8)
    return {
        "features": gaussian(part_keys[0], (F0, NW, ND, NH), 1.0, 6.0, ((1, 2), (2, 4), (3, 2))),
        "cotangent": gaussian(part_keys[1], (F0, NW, ND, NH), 1.0, 6.0, ((1, 2), (2, 4), (3, 2))),
        "w_stem": gaussian(keys[2], (3, 3, 3, F0, F0), (27 * F0) ** -0.5, 0.21875),
        "w_middle": gaussian(keys[3], (3, 3, 3, F0, F1), (27 * F0) ** -0.5, 0.21875),
        "w_bottom": gaussian(keys[4], (3, 3, 3, F1, F2), (27 * F1) ** -0.5, 0.15625),
        "w_rise": gaussian(keys[5], (3, 3, 3, F2 + F1, F1), (27 * (F2 + F1)) ** -0.5, 0.078125),
        "w_final": gaussian(keys[6], (3, 3, 3, F1 + F0, F0), (27 * (F1 + F0)) ** -0.5, 0.125),
    }


def conv_valid(padded, weight):
    result = lax.conv_general_dilated(padded[None], weight, (1, 1, 1), 'VALID', dimension_numbers=('NCDHW', 'DHWIO', 'NCDHW'), preferred_element_type=jnp.float32)
    return result[0]

def conv_back(padded_grad, weight):
    flipped = jnp.swapaxes(weight[::-1, ::-1, ::-1], 3, 4)
    return conv_valid(padded_grad, flipped)

def weight_grad(padded, grad):
    span_w, span_d, span_h = (grad.shape[1], grad.shape[2], grad.shape[3])
    flat_grad = grad.reshape(grad.shape[0], -1)
    blocks = []
    for offset_a in range(3):
        for offset_b in range(3):
            for offset_c in range(3):
                window = padded[:, offset_a:offset_a + span_w, offset_b:offset_b + span_d, offset_c:offset_c + span_h]
                window = window.reshape(padded.shape[0], -1)
                blocks.append(lax.dot_general(window, flat_grad, (((1,), (1,)), ((), ())), preferred_element_type=jnp.float32))
    return jnp.stack(blocks).reshape(3, 3, 3, padded.shape[0], grad.shape[0])

def silu_act(value):
    return value * jax.nn.sigmoid(value)

def silu_slope(value):
    gating = jax.nn.sigmoid(value)
    return gating * (1.0 + value * (1.0 - gating))

def pool_mean(value):
    count_c, count_w, count_d, count_h = value.shape
    blocks = value.astype(jnp.float32).reshape(count_c, count_w // 2, 2, count_d // 2, 2, count_h // 2, 2)
    return lax.optimization_barrier(jnp.mean(blocks, axis=(2, 4, 6))).astype(jnp.bfloat16)

def pool_sum(value):
    count_c, count_w, count_d, count_h = value.shape
    return lax.optimization_barrier(jnp.sum(value.reshape(count_c, count_w // 2, 2, count_d // 2, 2, count_h // 2, 2), axis=(2, 4, 6)))

def upsample(value):
    count_c, count_w, count_d, count_h = value.shape
    spread = jnp.broadcast_to(value[:, :, None, :, None, :, None], (count_c, count_w, 2, count_d, 2, count_h, 2))
    return spread.reshape(count_c, 2 * count_w, 2 * count_d, 2 * count_h)

def pad_cells(value):
    return jnp.pad(value, ((0, 0), (1, 1), (1, 1), (1, 1)))

def reference(features, cotangent, w_stem, w_middle, w_bottom, w_rise, w_final):
    mid_width = w_middle.shape[4]
    top_width = w_bottom.shape[4]
    input_pad = pad_cells(features)
    stem_pre = conv_valid(input_pad, w_stem)
    stem_act = silu_act(stem_pre).astype(jnp.bfloat16)
    half = pool_mean(stem_act)
    half_pad = pad_cells(half)
    mid_pre = conv_valid(half_pad, w_middle)
    mid_act = silu_act(mid_pre).astype(jnp.bfloat16)
    quarter = pool_mean(mid_act)
    quarter_pad = pad_cells(quarter)
    deep_pre = conv_valid(quarter_pad, w_bottom)
    deep_act = silu_act(deep_pre).astype(jnp.bfloat16)
    rise_pad = pad_cells(jnp.concatenate([upsample(deep_act), mid_act], 0))
    rise_pre = conv_valid(rise_pad, w_rise)
    rise_act = silu_act(rise_pre).astype(jnp.bfloat16)
    final_pad = pad_cells(jnp.concatenate([upsample(rise_act), stem_act], 0))
    output = conv_valid(final_pad, w_final).astype(jnp.bfloat16)
    grad_final = weight_grad(final_pad, cotangent)
    final_back = conv_back(pad_cells(cotangent), w_final)
    rise_grad = (pool_sum(final_back[:mid_width]) * silu_slope(rise_pre)).astype(jnp.bfloat16)
    grad_rise = weight_grad(rise_pad, rise_grad)
    rise_back = conv_back(pad_cells(rise_grad), w_rise)
    deep_grad = (pool_sum(rise_back[:top_width]) * silu_slope(deep_pre)).astype(jnp.bfloat16)
    grad_bottom = weight_grad(quarter_pad, deep_grad)
    quarter_back = conv_back(pad_cells(deep_grad), w_bottom)
    mid_grad = ((rise_back[top_width:] + upsample(quarter_back) / 8.0) * silu_slope(mid_pre)).astype(jnp.bfloat16)
    grad_middle = weight_grad(half_pad, mid_grad)
    half_back = conv_back(pad_cells(mid_grad), w_middle)
    stem_grad = ((final_back[mid_width:] + upsample(half_back) / 8.0) * silu_slope(stem_pre)).astype(jnp.bfloat16)
    grad_stem = weight_grad(input_pad, stem_grad)
    cell_count = features.shape[1] * features.shape[2] * features.shape[3]
    fine_scale = 1.0 / math.sqrt(cell_count)
    half_scale = 1.0 / math.sqrt(cell_count / 8.0)
    deep_scale = 1.0 / math.sqrt(cell_count / 64.0)
    return (output, grad_stem * fine_scale, grad_middle * half_scale, grad_bottom * deep_scale, grad_rise * half_scale, grad_final * fine_scale, half_back)
```

```python
import functools
import math

import jax
import jax.numpy as jnp
from jax import lax
from jax.experimental import pallas as pl
from jax.experimental.pallas import tpu as pltpu
from jax.sharding import PartitionSpec as P

BF, F32 = jnp.bfloat16, jnp.float32
AXES = ("grp", "dep", "hgt", "wid")
GROUP = ("wid", "hgt", "dep")
TILE = 16


class Names(dict):
    __getattr__ = dict.__getitem__


def spread_out(tree):
    if not isinstance(tree, dict):
        return [tree], lambda leaves: next(leaves)
    parts = {k: spread_out(v) for k, v in tree.items()}
    leaves = [leaf for some, _ in parts.values() for leaf in some]
    return leaves, lambda leaves: Names({k: back(leaves) for k, (_, back) in parts.items()})


def mm(a, b):
    return lax.dot_general(a, b, (((1,), (0,)), ((), ())), preferred_element_type=F32)


def mm_nt(a, b):
    return lax.dot_general(a, b, (((1,), (1,)), ((), ())), preferred_element_type=F32)


def mm_split(a, b):
    high = a.astype(BF)
    low = (a - high.astype(F32)).astype(BF)
    return mm(high, b) + mm(low, b)


def silu(v):
    return v * jax.nn.sigmoid(v)


def slope(v):
    g = jax.nn.sigmoid(v)
    return g * (1.0 + v * (1.0 - g))


def pattern(lanes, test):
    row = lax.broadcasted_iota(jnp.int32, (lanes, lanes), 0)
    col = lax.broadcasted_iota(jnp.int32, (lanes, lanes), 1)
    return jnp.where(test(row, col), 1.0, 0.0)


def neighbours():
    count = 1
    for name in GROUP:
        count *= min(lax.axis_size(name), 3)
    return count - 1


def edge_rows(channels, rows, lanes):
    size = TILE
    while channels % size or rows * (channels // size) > lanes // 2:
        size += TILE
    return size


class Halo:
    def __init__(self, group, rows, edges, own, span, sems):
        self.rows, self.edges, self.own = rows, edges, own
        self.base = group * neighbours()
        self.w, self.d, self.h = span
        self.send, self.recv = sems
        self.before = None
        self.unsent = False
        self.side = own.shape[1] // 2
        self.tall = own.shape[0]
        self.per = rows.shape[2] // self.tall

    def clear(self):
        blank = jnp.zeros(self.rows.shape[2:], BF)
        for a in range(self.w + 2):
            for b in range(self.d + 2):
                if a in (0, self.w + 1) or b in (0, self.d + 1):
                    self.rows[a, b] = blank
        self.edges[...] = jnp.zeros(self.edges.shape, BF)

    def fill_edges(self):
        lane = lax.broadcasted_iota(jnp.int32, self.own.shape, 1)
        tile = jnp.zeros(self.own.shape, F32)
        for a in range(self.w):
            for b in range(self.d):
                row = self.rows[a + 1, b + 1].astype(F32)
                for g in range(self.per):
                    r = (a * self.d + b) * self.per + g
                    part_of = row[g * self.tall : (g + 1) * self.tall]
                    tile = jnp.where(lane == r, part_of[:, 0:1], tile)
                    tile = jnp.where(lane == self.side + r, part_of[:, self.h - 1 : self.h], tile)
        self.own[...] = tile.astype(BF)

    def copies(self):
        place = {name: lax.axis_index(name) for name in AXES}
        size = {name: lax.axis_size(name) for name in AXES}

        def choices(name):
            i, n = place[name], size[name]
            if n == 1:
                return [(0, 0, True, True)]
            if n == 2:
                return [(0, 0, True, True), (1, 1 - 2 * i, True, True)]
            return [(0, 0, True, True), (1, 1, i < n - 1, i > 0), (2, -1, i > 0, i < n - 1)]

        def cells(step, code, count):
            if code == 0:
                return pl.ds(1, count), pl.ds(1, count)
            up = (1 + step) // 2
            return pl.ds(1 + (count - 1) * up, 1), pl.ds((count + 1) * (1 - up), 1)

        out = []
        for cw, sw, ow, iw in choices("wid"):
            for cd, sd, od, id_ in choices("dep"):
                for ch, sh, oh, ih in choices("hgt"):
                    if cw == 0 and cd == 0 and ch == 0:
                        continue
                    slot = self.base + len(out)
                    target = {"wid": place["wid"] + sw, "dep": place["dep"] + sd, "hgt": place["hgt"] + sh}
                    if ch == 0:
                        from_w, to_w = cells(sw, cw, self.w)
                        from_d, to_d = cells(sd, cd, self.d)
                        source = self.rows.at[from_w, from_d]
                        dest = self.rows.at[to_w, to_d]
                    else:
                        source = self.own
                        dest = self.edges.at[(1 - sh) // 2, 1 - sw, 1 - sd]
                    copy = pltpu.make_async_remote_copy(
                        src_ref=source,
                        dst_ref=dest,
                        send_sem=self.send.at[slot],
                        recv_sem=self.recv.at[slot],
                        device_id=target,
                        device_id_type=pl.DeviceIdType.MESH,
                    )
                    out.append((copy, [c for c in (ow, od, oh) if c is not True], [c for c in (iw, id_, ih) if c is not True]))
        return out

    @staticmethod
    def guarded(conditions, action):
        if not conditions:
            action()
        else:
            pl.when(functools.reduce(jnp.logical_and, conditions))(action)

    def start(self):
        if self.before is not None:
            self.before.finish()
        self.fill_edges()
        for copy, can_send, _ in self.copies():
            self.guarded(can_send, copy.start)
        self.unsent = True

    def wait(self):
        for copy, _, can_take in self.copies():
            self.guarded(can_take, copy.wait_recv)

    def finish(self):
        if self.unsent:
            for copy, can_send, _ in self.copies():
                self.guarded(can_send, copy.wait_send)
        self.unsent = False

    def shifted(self, a, b, spread=None):
        lanes = self.own.shape[1]
        h = self.h if spread is None else 2 * self.h
        row = self.rows[a, b]
        if spread is not None:
            row = mm(row, spread).astype(BF)
        dw = 0 if a == 0 else 2 if a == self.w + 1 else 1
        dd = 0 if b == 0 else 2 if b == self.d + 1 else 1
        r = ((self.w - 1, a - 1, 0)[dw] * self.d + (self.d - 1, b - 1, 0)[dd]) * self.per

        lane = lax.broadcasted_iota(jnp.int32, (self.tall, lanes), 1)
        low, high = self.edges[0, dw, dd].astype(F32), self.edges[1, dw, dd].astype(F32)
        wide = row.astype(F32)
        befores, afters = [], []
        for g in range(self.per):
            here = wide[g * self.tall : (g + 1) * self.tall]
            left = low[:, self.side + r + g : self.side + r + g + 1]
            right = high[:, r + g : r + g + 1]
            before = jnp.where(lane == 0, left, pltpu.roll(here, 1, 1))
            after = jnp.where(lane == h - 1, right, pltpu.roll(here, lanes - 1, 1))
            if h < lanes:
                before = jnp.where(lane < h, before, 0.0)
                after = jnp.where(lane < h, after, 0.0)
            befores.append(before.astype(BF))
            afters.append(after.astype(BF))
        if self.per == 1:
            return befores[0], row, afters[0]
        return jnp.concatenate(befores, axis=0), row, jnp.concatenate(afters, axis=0)


def part(i, m):
    return pl.ds(pl.multiple_of(i * m, TILE), m)


def position(axes):
    place, count = 0, 1
    for axis in axes:
        place = place * lax.axis_size(axis) + lax.axis_index(axis)
        count *= lax.axis_size(axis)
    return place, count


def device_at(axes, place):
    where = {name: lax.axis_index(name) for name in GROUP}
    for axis in axes[::-1]:
        n = lax.axis_size(axis)
        where[axis] = place if axis == axes[0] else lax.rem(place, n)
        place = lax.div(place, n)
    return where


class Summed:
    def __init__(self, order, full, buffers, send, recv):
        self.order, self.full = order, full
        self.levels = [buffers[3 * i : 3 * i + 3] for i in range(len(order))]
        self.total = buffers[0]
        self.send, self.recv = send, recv
        self.stage, self.open, self.sent = 0, None, []

    def copy(self, stage, axes, source, dest, to):
        return pltpu.make_async_remote_copy(
            src_ref=source,
            dst_ref=dest,
            send_sem=self.send.at[stage],
            recv_sem=self.recv.at[stage],
            device_id=device_at(axes, to),
            device_id_type=pl.DeviceIdType.MESH,
        )

    def exchange(self, stage, axes, pieces, whole, m):
        i, n = position(axes)
        if n == 1:
            return
        for k in range(1, n):
            to = lax.rem(i + k, n)
            source, dest = pieces(to, i)
            self.copy(stage, axes, source, dest, to).start()
        every = whole.at[pl.ds(0, (n - 1) * m)]
        self.open = self.copy(stage, axes, every, every, lax.rem(i + 1, n))
        self.sent.append(self.open)

    def step(self):
        stage, deep = self.stage, len(self.order)
        self.stage += 1
        if self.open is not None:
            self.open.wait_recv()
            self.open = None
        if 0 < stage <= deep:
            i, n = position(self.order[stage - 1])
            held, _, came = self.levels[stage - 1]
            m = held.shape[0] // n
            value = held[part(i, m)]
            for k in range(1, n):
                value = value + came[part(lax.rem(i + k, n), m)].astype(F32)
            if stage < deep:
                self.levels[stage][0][...] = value
            else:
                place, _ = position([axis for axes in self.order for axis in axes])
                self.full[part(place, m)] = value.astype(BF)
        if stage < deep:
            held, wire, came = self.levels[stage]
            i, n = position(self.order[stage])
            m = held.shape[0] // n
            for k in range(1, n):
                there = part(lax.rem(i + k, n), m)
                wire[there] = held[there].astype(BF)
            self.exchange(stage, self.order[stage], lambda to, me: (wire.at[part(to, m)], came.at[part(me, m)]), came, m)
        elif stage < 2 * deep:
            depth = 2 * deep - stage
            place, count = position([axis for axes in self.order[:depth] for axis in axes])
            m = self.full.shape[0] // count
            piece = self.full.at[part(place, m)]
            self.exchange(stage, self.order[depth - 1], lambda to, me: (piece, piece), self.full, m)

    def finish(self):
        while self.stage <= 2 * len(self.order):
            self.step()
        for copy in self.sent:
            copy.wait_send()


HALOS = dict(
    feat=(0, 0, 0), half=(0, 1, 1), quarter=(1, 2, 0), deep=(2, 2, 1), rg=(1, 1, 0), dg=(2, 2, 1),
    mg=(1, 1, 0), cot=(0, 0, 2), mid=(1, 1, 2), stem=(0, 0, 3), ra=(1, 1, 3),
)
STACKS = dict(
    feat=(0, 0), cot=(0, 0), half=(0, 1), quarter=(1, 2), up2=(2, 1), mid=(1, 1), up1=(1, 0),
    stem=(0, 0), rg=(1, 1), dg=(2, 2), mg=(1, 1),
)


def blocks(size, lanes):
    return -(-size // lanes)


def segments(f, lanes):
    f0, f1, f2 = f
    return dict(
        low=[(f1, blocks(27 * f1, lanes))],
        up=[(f1, blocks(27 * f2, lanes))],
        bot=[(27 * f1, blocks(f2, lanes))],
        fin=[(3 * f0, blocks(9 * f1, lanes)), (3 * f0, blocks(9 * f0, lanes))],
        mid=[(f1, blocks(27 * f0, lanes))],
        stem=[(f0, blocks(27 * f0, lanes))],
    )


STAGED = (("wid",), ("hgt",), ("dep",))


def orders():
    whole = math.prod(lax.axis_size(axis) for axis in GROUP)
    near = (GROUP,) if whole <= 16 else STAGED
    return dict(low=STAGED, up=STAGED, bot=STAGED, fin=STAGED, mid=near, stem=near)


def step_kernel(cfg, back, *refs):
    (f0, f1, f2, w, d, h) = cfg
    ref = back(iter(refs))
    spans = {0: (w, d, h), 1: (w // 2, d // 2, h // 2), 2: (w // 4, d // 4, h // 4)}
    lanes = h
    halo = Names()
    last = {}
    for name, (_, level, group) in HALOS.items():
        own = ref.halos[name]
        halo[name] = Halo(group, own.rows, own.edges, own.own, spans[level], (ref.send, ref.recv))
        halo[name].before = last.get(group)
        last[group] = halo[name]
    stacks = ref.stacks
    sums = Names()
    for name, order in orders().items():
        own = ref.sums[name]
        sums[name] = Summed(order, ref.outs[name], list(own.levels.values()), own.send, own.recv)

    loads = Names()
    for i, name in enumerate(ref.ins):
        loads[name] = pltpu.make_async_copy(ref.ins[name], ref.inside[name], ref.load.at[i])
        loads[name].start()
    for item in halo.values():
        item.clear()

    def take(load, source, item):
        load.wait()
        ref.wide[...] = source[...].astype(F32)
        for a in range(w):
            for b in range(d):
                item.rows[a + 1, b + 1] = ref.wide[pl.ds(a * d + b, f0, stride=w * d), :].astype(BF)

    take(loads.feat, ref.inside.feat, halo.feat)
    barrier = pltpu.get_barrier_semaphore()
    me, everyone = position(GROUP)
    for k in range(1, everyone):
        pl.semaphore_signal(
            barrier, 1, device_id=device_at(GROUP, lax.rem(me + k, everyone)), device_id_type=pl.DeviceIdType.MESH
        )
    pl.semaphore_wait(barrier, everyone - 1)

    halo.feat.start()
    take(loads.cot, ref.inside.cot, halo.cot)
    halo.cot.start()
    pool = pattern(lanes, lambda r, c: r // 2 == c)
    pool_mean = (pool / 8.0).astype(BF)
    pool_sum = pool.astype(BF)
    spread = pattern(lanes, lambda r, c: c // 2 == r)
    spread_mean = (spread / 8.0).astype(BF)
    spread = spread.astype(BF)

    def forward(raw, target):
        target[...] = raw[...].reshape(-1, raw.shape[2]).T

    def side_by_side(raw, target, low, high):
        width = high - low
        for k in range(raw.shape[0]):
            target[:, k * width : (k + 1) * width] = raw[k][:, low:high]

    loads.stem.wait()
    forward(ref.inside.stem, ref.w_stem)
    loads.fin.wait()
    forward(ref.inside.fin, ref.b_fin)
    side_by_side(ref.inside.fin, ref.w_fin_up, 0, f1)
    side_by_side(ref.inside.fin, ref.w_fin_low, f1, f1 + f0)
    loads.mid.wait()
    forward(ref.inside.mid, ref.w_mid)
    side_by_side(ref.inside.mid, ref.b_mid, 0, f1)
    loads.bot.wait()
    forward(ref.inside.bot, ref.w_bot)
    side_by_side(ref.inside.bot, ref.b_bot, 0, f2)
    loads.rise.wait()
    forward(ref.inside.rise, ref.b_rise)
    side_by_side(ref.inside.rise, ref.w_rise_up, 0, f2)
    side_by_side(ref.inside.rise, ref.w_rise_low, f2, f2 + f1)

    def stack(item, target, back=False):
        for a in range(item.w + 2):
            for b in range(item.d + 2):
                parts = item.shifted(a, b)
                target[a, b] = jnp.concatenate(parts[::-1] if back else parts, axis=0)

    def stack_up(up, target):
        for a in range(target.shape[0]):
            for b in range(target.shape[1]):
                target[a, b] = jnp.concatenate(up.shifted((a + 1) // 2, (b + 1) // 2, spread), axis=0)

    def patch(source, a, b, pair, back=False, middle=False):
        third = source.shape[2] // 3
        rows = slice(third, 2 * third) if middle else slice(0, 3 * third)
        parts = []
        for q in range(pair):
            taps = [(ka, kb) for ka in range(3) for kb in range(3)]
            parts.append(
                jnp.concatenate([source[a + ka, b + kb + q, rows] for ka, kb in (taps[::-1] if back else taps)], axis=0)
            )
        return parts[0] if pair == 1 else jnp.concatenate(parts, axis=1)

    def over_rows(span, body):
        pair = 4 if span[1] % 4 == 0 else 2 if span[1] % 2 == 0 else 1
        across = span[1] // pair

        def trip(i, _):
            body(i // across, (i % across) * pair, pair)
            return 0

        count = span[0] * across
        if count <= 2:
            for i in range(count):
                trip(i, 0)
        else:
            lax.fori_loop(0, count, trip, 0)

    def conv(source, weight, span, store, back=False):
        def body(a, b, pair):
            result = mm(weight[...], patch(source, a, b, pair, back))
            for q in range(pair):
                store(a, b + q, result[:, q * lanes : (q + 1) * lanes])

        over_rows(span, body)

    def put_blocks(where, base, value):
        rows, width = value.shape
        count = blocks(width, lanes)
        if count * lanes > width:
            value = jnp.concatenate([value, jnp.zeros((rows, count * lanes - width), value.dtype)], axis=1)
        for j in range(count):
            where[base + j * rows : base + (j + 1) * rows] = value[:, j * lanes : (j + 1) * lanes]

    def beside(span, pick):
        return jnp.concatenate([pick(a, b) for a in range(span[0]) for b in range(span[1])], axis=1)

    halo.feat.wait()
    stack(halo.feat, stacks.feat)

    def stem_store(a, b, value):
        ref.stem_pre[a, b] = value
        halo.stem.rows[a + 1, b + 1] = silu(value).astype(BF)

    conv(stacks.feat, ref.w_stem, spans[0], stem_store)

    def pooled(fine, coarse):
        low, up = fine, coarse
        for a in range(up.w):
            for b in range(up.d):
                cat = [low.rows[2 * a + 1 + i, 2 * b + 1 + j] for i in range(2) for j in range(2)]
                total = mm(cat[0], pool_mean) + mm(cat[1], pool_mean) + mm(cat[2], pool_mean) + mm(cat[3], pool_mean)
                up.rows[a + 1, b + 1] = total.astype(BF)

    pooled(halo.stem, halo.half)
    halo.cot.wait()
    halo.half.start()
    halo.stem.start()
    stack(halo.cot, stacks.cot, back=True)
    ref.fb_pool[...] = jnp.zeros(ref.fb_pool.shape, F32)

    def back_store(a, b, value):
        ref.fb_pool[a // 2, b // 2] += value[:f1]
        ref.fb_skip[a, b] = value[f1:]

    conv(stacks.cot, ref.b_fin, spans[0], back_store, back=True)
    for a in range(spans[1][0]):
        for b in range(spans[1][1]):
            ref.fb_pool[a, b] = mm_split(ref.fb_pool[a, b], pool_sum)
    halo.half.wait()
    stack(halo.half, stacks.half)

    def mid_store(a, b, value):
        ref.mid_pre[a, b] = value
        halo.mid.rows[a + 1, b + 1] = silu(value).astype(BF)

    conv(stacks.half, ref.w_mid, spans[1], mid_store)
    pooled(halo.mid, halo.quarter)
    halo.quarter.start()
    halo.mid.start()
    halo.stem.wait()
    stack(halo.stem, stacks.stem)

    def final_low(a, b, value):
        ref.fin_part[a, b] = value

    conv(stacks.stem, ref.w_fin_low, spans[0], final_low)
    cot_cells = lambda: beside(spans[0], lambda a, b: stacks.cot[a + 1, b + 1])
    low_cells = beside(spans[0], lambda a, b: patch(stacks.stem, a, b, 1, middle=True))
    put_blocks(sums.fin.total, 3 * f0 * blocks(9 * f1, lanes), mm_nt(cot_cells(), low_cells))
    halo.quarter.wait()
    stack(halo.quarter, stacks.quarter)

    def deep_store(a, b, value):
        ref.deep_pre[a, b] = value
        halo.deep.rows[a + 1, b + 1] = silu(value).astype(BF)

    conv(stacks.quarter, ref.w_bot, spans[2], deep_store)
    halo.deep.start()
    halo.mid.wait()
    stack(halo.mid, stacks.mid)

    def rise_low(a, b, value):
        ref.rise_pre[a, b] = value

    conv(stacks.mid, ref.w_rise_low, spans[1], rise_low)
    halo.deep.wait()
    stack_up(halo.deep, stacks.up2)

    def rise_store(a, b, value):
        value = value + ref.rise_pre[a, b]
        halo.ra.rows[a + 1, b + 1] = silu(value).astype(BF)
        grad = ref.fb_pool[a, b] * slope(value)
        halo.rg.rows[a + 1, b + 1] = grad.astype(BF)

    conv(stacks.up2, ref.w_rise_up, spans[1], rise_store)
    halo.rg.start()
    halo.ra.start()

    grad1 = lambda item: beside(spans[1], lambda a, b: item.rows[a + 1, b + 1])

    def wide_wgrad(segment, grad, source, span):
        cells = beside(span, lambda a, b: patch(source, a, b, 1))
        put_blocks(segment.total, 0, mm_nt(grad, cells))

    wide_wgrad(sums.low, grad1(halo.rg), stacks.mid, spans[1])
    sums.low.step()
    wide_wgrad(sums.up, grad1(halo.rg), stacks.up2, spans[1])
    sums.up.step()
    sums.low.step()
    halo.rg.wait()
    stack(halo.rg, stacks.rg, back=True)
    deep_sum = [[None] * spans[2][1] for _ in range(spans[2][0])]
    pair1 = 2 if spans[1][1] % 2 == 0 else 1
    for a in range(spans[1][0]):
        for b in range(0, spans[1][1], pair1):
            result = mm(ref.b_rise[...], patch(stacks.rg, a, b, pair1, back=True))
            for q in range(pair1):
                value = result[:, q * lanes : (q + 1) * lanes]
                ref.rb_skip[a, b + q] = value[f2:]
                ap, bt = a // 2, (b + q) // 2
                old = deep_sum[ap][bt]
                deep_sum[ap][bt] = value[:f2] if old is None else old + value[:f2]
    for a in range(spans[2][0]):
        for b in range(spans[2][1]):
            grad = mm_split(deep_sum[a][b], pool_sum) * slope(ref.deep_pre[a, b])
            halo.dg.rows[a + 1, b + 1] = grad.astype(BF)
    halo.dg.start()
    sums.up.step()
    cells2 = beside(spans[2], lambda a, b: patch(stacks.quarter, a, b, 1))
    grad2 = beside(spans[2], lambda a, b: halo.dg.rows[a + 1, b + 1])
    bot = mm_nt(cells2, grad2)
    put_blocks(sums.bot.total, 0, bot)
    sums.bot.step()
    halo.ra.wait()
    stack_up(halo.ra, stacks.up1)
    sums.low.step()
    up_cells = beside(spans[0], lambda a, b: patch(stacks.up1, a, b, 1, middle=True))
    put_blocks(sums.fin.total, 0, mm_nt(cot_cells(), up_cells))
    sums.fin.step()
    halo.dg.wait()
    stack(halo.dg, stacks.dg, back=True)

    def quarter_store(a, b, value):
        wide = mm_split(value, spread_mean)
        for i in range(2):
            for j in range(2):
                at_, bt = 2 * a + i, 2 * b + j
                grad = (ref.rb_skip[at_, bt] + wide) * slope(ref.mid_pre[at_, bt])
                halo.mg.rows[at_ + 1, bt + 1] = grad.astype(BF)

    conv(stacks.dg, ref.b_bot, spans[2], quarter_store, back=True)
    halo.mg.start()
    wide_wgrad(sums.mid, grad1(halo.mg), stacks.half, spans[1])
    sums.mid.step()
    sums.up.step()
    sums.bot.step()
    sums.fin.step()
    sums.low.step()
    halo.mg.wait()
    stack(halo.mg, stacks.mg, back=True)

    def half_store(a, b, value):
        ref.half_wide[pl.ds(a * spans[1][1] + b, f0, stride=spans[1][0] * spans[1][1]), :] = value
        wide = mm_split(value, spread_mean)
        for i in range(2):
            for j in range(2):
                at_, bt = 2 * a + i, 2 * b + j
                grad = (ref.fb_skip[at_, bt] + wide) * slope(ref.stem_pre[at_, bt])
                ref.stem_grad[at_, bt] = grad.astype(BF)

    conv(stacks.mg, ref.b_mid, spans[1], half_store, back=True)
    ref.outs.half[...] = ref.half_wide[...]
    wide_wgrad(sums.stem, beside(spans[0], lambda a, b: ref.stem_grad[a, b]), stacks.feat, spans[0])
    sums.stem.step()
    sums.up.step()
    sums.bot.step()
    sums.fin.step()
    sums.low.step()
    sums.mid.step()

    def final_store(a, b, value):
        ref.wide[pl.ds(a * d + b, f0, stride=w * d), :] = ref.fin_part[a, b] + value

    conv(stacks.up1, ref.w_fin_up, spans[0], final_store)
    ref.outs.output[...] = ref.wide[...].astype(BF)
    sums.stem.step()
    sums.up.step()
    sums.bot.step()
    sums.fin.step()
    sums.low.step()
    sums.mid.step()
    sums.up.step()
    sums.stem.step()
    sums.bot.step()
    sums.fin.step()
    sums.low.step()
    sums.up.step()
    sums.bot.step()
    sums.fin.step()
    for item in sums.values():
        item.finish()
    for item in halo.values():
        item.finish()


def unpack_kernel(cfg, back, *refs):
    (f0, f1, f2, lanes, scales) = cfg
    ref = back(iter(refs))
    loads = Names()
    for i, name in enumerate(ref.ins):
        loads[name] = pltpu.make_async_copy(ref.ins[name], ref.inside[name], ref.load.at[i])
        loads[name].start()
    stores = []

    def send(source, target):
        copy = pltpu.make_async_copy(source, target, ref.store.at[len(stores)])
        copy.start()
        stores.append(copy)

    def side(source, base, rows, width, scale):
        count = blocks(width, lanes)
        value = [source[base + j * rows : base + (j + 1) * rows].astype(F32) * scale for j in range(count)]
        return jnp.concatenate(value, axis=1)

    loads.output.wait()
    send(ref.inside.output, ref.outs.output)
    loads.half.wait()
    ref.ready.half[...] = ref.inside.half[:, : lanes // 2]
    send(ref.ready.half, ref.outs.half)
    loads.low.wait()
    loads.up.wait()
    low = side(ref.inside.low, 0, f1, 27 * f1, scales.rise)
    up = side(ref.inside.up, 0, f1, 27 * f2, scales.rise)
    for k in range(27):
        ref.ready.rise[k] = jnp.concatenate([up[:, k * f2 : (k + 1) * f2], low[:, k * f1 : (k + 1) * f1]], axis=1)
    send(ref.ready.rise, ref.outs.rise)
    loads.bot.wait()
    ref.ready.bot[...] = side(ref.inside.bot, 0, 27 * f1, f2, scales.bot)[:, :f2]
    send(ref.ready.bot, ref.outs.bot)
    loads.fin.wait()
    up = side(ref.inside.fin, 0, 3 * f0, 9 * f1, scales.fin)
    low = side(ref.inside.fin, 3 * f0 * blocks(9 * f1, lanes), 3 * f0, 9 * f0, scales.fin)
    for k in range(27):
        at_, rows = k // 3, slice((k % 3) * f0, (k % 3 + 1) * f0)
        ref.ready.fin[k] = jnp.concatenate([up[rows, at_ * f1 : (at_ + 1) * f1], low[rows, at_ * f0 : (at_ + 1) * f0]], axis=1)
    send(ref.ready.fin, ref.outs.fin)
    for load, source, target, out, scale in (
        (loads.mid, ref.inside.mid, ref.ready.mid, ref.outs.mid, scales.mid),
        (loads.stem, ref.inside.stem, ref.ready.stem, ref.outs.stem, scales.stem),
    ):
        load.wait()
        width = target.shape[1]
        for j in range(blocks(27 * f0, lanes)):
            value = (source[j * width : (j + 1) * width].astype(F32) * scale).T
            rows = min(lanes, 27 * f0 - j * lanes)
            target[j * lanes : j * lanes + rows] = value[:rows]
        send(target, out)
    for copy in stores:
        copy.wait()


def local(features, cotangent, w_stem, w_middle, w_bottom, w_rise, w_final):
    f0, w, d, h = features.shape
    f1, f2 = w_middle.shape[4], w_bottom.shape[4]
    f = (f0, f1, f2)
    spans = {0: (w, d), 1: (w // 2, d // 2), 2: (w // 4, d // 4)}
    near = neighbours()
    sets = 1 + max(group for _, _, group in HALOS.values())
    flat = w * d * f0
    inputs = dict(
        feat=features.reshape(flat, h),
        cot=cotangent.reshape(flat, h),
        stem=w_stem.reshape(27, f0, f0),
        fin=w_final.transpose(0, 1, 2, 4, 3).reshape(27, f0, f1 + f0),
        mid=w_middle.reshape(27, f0, f1),
        bot=w_bottom.reshape(27, f1, f2),
        rise=w_rise.transpose(0, 1, 2, 4, 3).reshape(27, f1, f2 + f1),
    )
    outs = dict(output=jax.ShapeDtypeStruct((flat, h), BF), half=jax.ShapeDtypeStruct((flat // 4, h), F32))
    halos, sums = {}, {}
    for name, (c, level, _) in HALOS.items():
        a, b = spans[level]
        tall = edge_rows(f[c], a * b, h)
        halos[name] = dict(
            rows=pltpu.VMEM((a + 2, b + 2, f[c], h), BF),
            edges=pltpu.VMEM((2, 3, 3, tall, h), BF),
            own=pltpu.VMEM((tall, h), BF),
        )
    place = segments(f, h)
    for name, order in orders().items():
        unit = TILE * math.prod(lax.axis_size(axis) for axis in GROUP)
        rows = -(-sum(a * b for a, b in place[name]) // unit) * unit
        outs[name] = jax.ShapeDtypeStruct((rows, h), BF)
        levels = {}
        for i, axes in enumerate(order):
            for j, kind in enumerate((F32, BF, BF)):
                levels[3 * i + j] = pltpu.VMEM((rows, h), kind)
            rows //= math.prod(lax.axis_size(axis) for axis in axes)
        several = pltpu.SemaphoreType.DMA((2 * len(order),))
        sums[name] = dict(levels=levels, send=several, recv=several)

    def cells_of(c, level, kind=F32):
        return pltpu.VMEM((*spans[level], c, h), kind)

    def taps(a, b):
        return pltpu.VMEM((a, 27 * b), BF)

    scratch = dict(
        send=pltpu.SemaphoreType.DMA((sets * near,)),
        recv=pltpu.SemaphoreType.DMA((sets * near,)),
        load=pltpu.SemaphoreType.DMA((len(inputs),)),
        inside={name: pltpu.VMEM(v.shape, BF) for name, v in inputs.items()},
        halos=halos,
        sums=sums,
        stacks={
            name: pltpu.VMEM((spans[level][0] + 2, spans[level][1] + 2, 3 * f[c], h), BF)
            for name, (c, level) in STACKS.items()
        },
        stem_pre=cells_of(f0, 0), mid_pre=cells_of(f1, 1), deep_pre=cells_of(f2, 2), rise_pre=cells_of(f1, 1),
        fb_pool=cells_of(f1, 1), fb_skip=cells_of(f0, 0), rb_skip=cells_of(f1, 1), fin_part=cells_of(f0, 0),
        stem_grad=cells_of(f0, 0, BF),
        wide=pltpu.VMEM((flat, h), F32), half_wide=pltpu.VMEM((flat // 4, h), F32),
        w_stem=taps(f0, f0), w_mid=taps(f1, f0), w_bot=taps(f2, f1), w_rise_up=taps(f1, f2), w_rise_low=taps(f1, f1),
        w_fin_up=taps(f0, f1), w_fin_low=taps(f0, f0), b_mid=taps(f0, f1), b_bot=taps(f1, f2),
        b_rise=taps(f2 + f1, f1), b_fin=taps(f1 + f0, f0),
    )
    vmem = pl.BlockSpec(memory_space=pltpu.VMEM)
    anywhere = pl.BlockSpec(memory_space=pl.ANY)
    leaves, back = spread_out(dict(ins=inputs, outs=outs, **scratch))
    done = pl.pallas_call(
        functools.partial(step_kernel, (f0, f1, f2, w, d, h), back),
        out_shape=tuple(outs.values()),
        in_specs=[anywhere] * len(inputs),
        out_specs=(vmem,) * len(outs),
        scratch_shapes=leaves[len(inputs) + len(outs) :],
        compiler_params=pltpu.CompilerParams(collective_id=0, has_side_effects=True, vmem_limit_bytes=60 << 20),
        name="unet_step",
    )(*inputs.values())
    packed = dict(zip(outs, done))
    cells = w * d * h * math.prod(lax.axis_size(axis) for axis in GROUP)
    fine, mid, deep = (1.0 / math.sqrt(cells / k) for k in (1.0, 8.0, 64.0))
    scales = Names(stem=fine, mid=mid, bot=deep, rise=mid, fin=fine)

    results = dict(
        output=jax.ShapeDtypeStruct((flat, h), BF),
        stem=jax.ShapeDtypeStruct((27 * f0, f0), F32),
        mid=jax.ShapeDtypeStruct((27 * f0, f1), F32),
        bot=jax.ShapeDtypeStruct((27 * f1, f2), F32),
        rise=jax.ShapeDtypeStruct((27, f1, f2 + f1), F32),
        fin=jax.ShapeDtypeStruct((27, f0, f1 + f0), F32),
        half=jax.ShapeDtypeStruct((flat // 4, h // 2), F32),
    )
    hold = dict(
        inside={n: pltpu.VMEM(v.shape, v.dtype) for n, v in packed.items()},
        ready={n: pltpu.VMEM(v.shape, v.dtype) for n, v in results.items()},
        load=pltpu.SemaphoreType.DMA((len(packed),)),
        store=pltpu.SemaphoreType.DMA((len(results),)),
    )
    leaves, back = spread_out(dict(ins=packed, outs=results, **hold))
    final = pl.pallas_call(
        functools.partial(unpack_kernel, (f0, f1, f2, h, scales), back),
        out_shape=tuple(results.values()),
        in_specs=[anywhere] * len(packed),
        out_specs=(anywhere,) * len(results),
        scratch_shapes=leaves[len(packed) + len(results) :],
        compiler_params=pltpu.CompilerParams(vmem_limit_bytes=60 << 20),
        name="unpack",
    )(*packed.values())
    final = Names(zip(results, final))
    return (
        final.output.reshape(f0, w, d, h),
        final.stem.reshape(w_stem.shape),
        final.mid.reshape(w_middle.shape),
        final.bot.reshape(w_bottom.shape),
        final.rise.reshape(3, 3, 3, f1, f2 + f1).transpose(0, 1, 2, 4, 3),
        final.fin.reshape(3, 3, 3, f0, f1 + f0).transpose(0, 1, 2, 4, 3),
        final.half.reshape(f0, w // 2, d // 2, h // 2),
    )


def solution(mesh):
    placed = (P("grp", "wid", "dep", "hgt"), P("grp", "wid", "dep", "hgt"), P(), P(), P(), P(), P())
    grad = P("grp", None, None, None, None)
    return jax.shard_map(
        local,
        mesh=mesh,
        in_specs=placed,
        out_specs=(P("grp", "wid", "dep", "hgt"), grad, grad, grad, grad, grad, P("grp", "wid", "dep", "hgt")),
        check_vma=False,
    )
```

```python
import functools
import math

import jax
import jax.numpy as jnp
from jax import lax
from jax.experimental import pallas as pl
from jax.experimental.pallas import tpu as pltpu
from jax.sharding import PartitionSpec as P

BF, F32 = jnp.bfloat16, jnp.float32
AXES = ("grp", "dep", "hgt", "wid")
GROUP = ("wid", "hgt", "dep")
TILE = 16


class Names(dict):
    __getattr__ = dict.__getitem__


def spread_out(tree):
    if not isinstance(tree, dict):
        return [tree], lambda leaves: next(leaves)
    parts = {k: spread_out(v) for k, v in tree.items()}
    leaves = [leaf for some, _ in parts.values() for leaf in some]
    return leaves, lambda leaves: Names({k: back(leaves) for k, (_, back) in parts.items()})


def mm(a, b):
    return lax.dot_general(a, b, (((1,), (0,)), ((), ())), preferred_element_type=F32)


def mm_nt(a, b):
    return lax.dot_general(a, b, (((1,), (1,)), ((), ())), preferred_element_type=F32)


def mm_split(a, b):
    high = a.astype(BF)
    low = (a - high.astype(F32)).astype(BF)
    return mm(high, b) + mm(low, b)


def silu(v):
    return v * jax.nn.sigmoid(v)


def slope(v):
    g = jax.nn.sigmoid(v)
    return g * (1.0 + v * (1.0 - g))


def pattern(lanes, test):
    row = lax.broadcasted_iota(jnp.int32, (lanes, lanes), 0)
    col = lax.broadcasted_iota(jnp.int32, (lanes, lanes), 1)
    return jnp.where(test(row, col), 1.0, 0.0)


def neighbours():
    count = 1
    for name in GROUP:
        count *= min(lax.axis_size(name), 3)
    return count - 1


def edge_rows(channels, rows, lanes):
    size = TILE
    while channels % size or rows * (channels // size) > lanes // 2:
        size += TILE
    return size


def lane_parts(channels, tall, h, lanes):
    count = lanes // h
    while channels % (tall * count):
        count -= 1
    return count


class Halo:
    def __init__(self, group, rows, packed, edges, own, span, sems):
        self.rows, self.edges, self.own = rows, edges, own
        self.packed = packed
        self.fold = rows.shape[2] // packed.shape[2]
        self.base = group * neighbours()
        self.w, self.d, self.h = span
        self.send, self.recv = sems
        self.before = None
        self.unsent = False
        self.side = own.shape[1] // 2
        self.tall = own.shape[0]
        self.per = rows.shape[2] // self.tall

    def outer(self, a, b):
        return a in (0, self.w + 1) or b in (0, self.d + 1)

    def clear(self):
        moving = self.rows if self.fold == 1 else self.packed
        blank = jnp.zeros(moving.shape[2:], BF)
        for a in range(self.w + 2):
            for b in range(self.d + 2):
                if self.outer(a, b):
                    moving[a, b] = blank
        self.edges[...] = jnp.zeros(self.edges.shape, BF)

    def fill_edges(self):
        lane = lax.broadcasted_iota(jnp.int32, self.own.shape, 1)
        tile = jnp.zeros(self.own.shape, F32)
        for a in range(self.w):
            for b in range(self.d):
                row = self.rows[a + 1, b + 1].astype(F32)
                for g in range(self.per):
                    r = (a * self.d + b) * self.per + g
                    part_of = row[g * self.tall : (g + 1) * self.tall]
                    tile = jnp.where(lane == r, part_of[:, 0:1], tile)
                    tile = jnp.where(lane == self.side + r, part_of[:, self.h - 1 : self.h], tile)
        self.own[...] = tile.astype(BF)

    def pack(self):
        tall = self.packed.shape[2]
        for a in range(1, self.w + 1):
            for b in range(1, self.d + 1):
                wide = self.rows[a, b].astype(F32)
                total = wide[:tall]
                for g in range(1, self.fold):
                    total = total + pltpu.roll(wide[g * tall : (g + 1) * tall], g * self.h, 1)
                self.packed[a, b] = total.astype(BF)

    def copies(self):
        moving = self.rows if self.fold == 1 else self.packed
        place = {name: lax.axis_index(name) for name in AXES}
        size = {name: lax.axis_size(name) for name in AXES}

        def choices(name):
            i, n = place[name], size[name]
            if n == 1:
                return [(0, 0, True, True)]
            if n == 2:
                return [(0, 0, True, True), (1, 1 - 2 * i, True, True)]
            return [(0, 0, True, True), (1, 1, i < n - 1, i > 0), (2, -1, i > 0, i < n - 1)]

        def cells(step, code, count):
            if code == 0:
                return pl.ds(1, count), pl.ds(1, count)
            up = (1 + step) // 2
            return pl.ds(1 + (count - 1) * up, 1), pl.ds((count + 1) * (1 - up), 1)

        out = []
        for cw, sw, ow, iw in choices("wid"):
            for cd, sd, od, id_ in choices("dep"):
                for ch, sh, oh, ih in choices("hgt"):
                    if cw == 0 and cd == 0 and ch == 0:
                        continue
                    slot = self.base + len(out)
                    target = {"wid": place["wid"] + sw, "dep": place["dep"] + sd, "hgt": place["hgt"] + sh}
                    if ch == 0:
                        from_w, to_w = cells(sw, cw, self.w)
                        from_d, to_d = cells(sd, cd, self.d)
                        source = moving.at[from_w, from_d]
                        dest = moving.at[to_w, to_d]
                    else:
                        source = self.own
                        dest = self.edges.at[(1 - sh) // 2, 1 - sw, 1 - sd]
                    copy = pltpu.make_async_remote_copy(
                        src_ref=source,
                        dst_ref=dest,
                        send_sem=self.send.at[slot],
                        recv_sem=self.recv.at[slot],
                        device_id=target,
                        device_id_type=pl.DeviceIdType.MESH,
                    )
                    out.append((copy, [c for c in (ow, od, oh) if c is not True], [c for c in (iw, id_, ih) if c is not True]))
        return out

    @staticmethod
    def guarded(conditions, action):
        if not conditions:
            action()
        else:
            pl.when(functools.reduce(jnp.logical_and, conditions))(action)

    def start(self):
        if self.before is not None:
            self.before.finish()
        self.fill_edges()
        if self.fold > 1:
            self.pack()
        for copy, can_send, _ in self.copies():
            self.guarded(can_send, copy.start)
        self.unsent = True

    def wait(self):
        for copy, _, can_take in self.copies():
            self.guarded(can_take, copy.wait_recv)

    def finish(self):
        if self.unsent:
            for copy, can_send, _ in self.copies():
                self.guarded(can_send, copy.wait_send)
        self.unsent = False

    def shifted(self, a, b, spread=None):
        lanes = self.own.shape[1]
        h = self.h if spread is None else 2 * self.h
        folded = self.fold > 1 and self.outer(a, b)
        tall = self.packed.shape[2] if folded else self.rows.shape[2]
        row = self.packed[a, b] if folded else self.rows[a, b]
        if spread is not None:
            pieces = [mm(row, spread[g]) for g in range(self.fold if folded else 1)]
            wide = pieces[0] if len(pieces) == 1 else jnp.concatenate(pieces, axis=0)
            row = wide.astype(BF)
            folded = False
        else:
            wide = row.astype(F32)
        dw = 0 if a == 0 else 2 if a == self.w + 1 else 1
        dd = 0 if b == 0 else 2 if b == self.d + 1 else 1
        r = ((self.w - 1, a - 1, 0)[dw] * self.d + (self.d - 1, b - 1, 0)[dd]) * self.per
        lane = lax.broadcasted_iota(jnp.int32, (self.tall, lanes), 1)
        low, high = self.edges[0, dw, dd].astype(F32), self.edges[1, dw, dd].astype(F32)
        befores, centres, afters = [], [], []
        for g in range(self.per):
            turn, from_row = divmod(g * self.tall, tall) if folded else (0, g * self.tall)
            here = wide[from_row : from_row + self.tall]
            left = low[:, self.side + r + g : self.side + r + g + 1]
            right = high[:, r + g : r + g + 1]
            before = jnp.where(lane == 0, left, pltpu.roll(here, (lanes + 1 - turn * h) % lanes, 1))
            after = jnp.where(lane == h - 1, right, pltpu.roll(here, lanes - 1 - turn * h, 1))
            if h < lanes:
                before = jnp.where(lane < h, before, 0.0)
                after = jnp.where(lane < h, after, 0.0)
            befores.append(before.astype(BF))
            afters.append(after.astype(BF))
            if folded:
                centre = pltpu.roll(here, lanes - turn * h, 1) if turn else here
                centres.append(jnp.where(lane < h, centre, 0.0).astype(BF))
        if folded:
            row = jnp.concatenate(centres, axis=0)
        return jnp.concatenate(befores, axis=0), row, jnp.concatenate(afters, axis=0)


def part(i, m):
    return pl.ds(pl.multiple_of(i * m, TILE), m)


def position(axes):
    place, count = 0, 1
    for axis in axes:
        place = place * lax.axis_size(axis) + lax.axis_index(axis)
        count *= lax.axis_size(axis)
    return place, count


def device_at(axes, place):
    where = {name: lax.axis_index(name) for name in GROUP}
    for axis in axes[::-1]:
        n = lax.axis_size(axis)
        where[axis] = place if axis == axes[0] else lax.rem(place, n)
        place = lax.div(place, n)
    return where


class Summed:
    def __init__(self, order, full, buffers, send, recv):
        self.order, self.full = order, full
        self.levels = [buffers[3 * i : 3 * i + 3] for i in range(len(order))]
        self.total = buffers[0]
        self.send, self.recv = send, recv
        self.stage, self.open, self.sent = 0, None, []

    def copy(self, stage, axes, source, dest, to):
        return pltpu.make_async_remote_copy(
            src_ref=source,
            dst_ref=dest,
            send_sem=self.send.at[stage],
            recv_sem=self.recv.at[stage],
            device_id=device_at(axes, to),
            device_id_type=pl.DeviceIdType.MESH,
        )

    def exchange(self, stage, axes, pieces, whole, m):
        i, n = position(axes)
        if n == 1:
            return
        for k in range(1, n):
            to = lax.rem(i + k, n)
            source, dest = pieces(to, i)
            self.copy(stage, axes, source, dest, to).start()
        every = whole.at[pl.ds(0, (n - 1) * m)]
        self.open = self.copy(stage, axes, every, every, lax.rem(i + 1, n))
        self.sent.append(self.open)

    def step(self):
        stage, deep = self.stage, len(self.order)
        self.stage += 1
        if self.open is not None:
            self.open.wait_recv()
            self.open = None
        if 0 < stage <= deep:
            i, n = position(self.order[stage - 1])
            held, _, came = self.levels[stage - 1]
            m = held.shape[0] // n
            value = held[part(i, m)]
            for k in range(1, n):
                value = value + came[part(lax.rem(i + k, n), m)].astype(F32)
            if stage < deep:
                self.levels[stage][0][...] = value
            else:
                place, _ = position([axis for axes in self.order for axis in axes])
                self.full[part(place, m)] = value.astype(BF)
        if stage < deep:
            held, wire, came = self.levels[stage]
            i, n = position(self.order[stage])
            m = held.shape[0] // n
            for k in range(1, n):
                there = part(lax.rem(i + k, n), m)
                wire[there] = held[there].astype(BF)
            self.exchange(stage, self.order[stage], lambda to, me: (wire.at[part(to, m)], came.at[part(me, m)]), came, m)
        elif stage < 2 * deep:
            depth = 2 * deep - stage
            place, count = position([axis for axes in self.order[:depth] for axis in axes])
            m = self.full.shape[0] // count
            piece = self.full.at[part(place, m)]
            self.exchange(stage, self.order[depth - 1], lambda to, me: (piece, piece), self.full, m)

    def finish(self):
        while self.stage <= 2 * len(self.order):
            self.step()
        for copy in self.sent:
            copy.wait_send()


HALOS = dict(
    feat=(0, 0, 0), half=(0, 1, 1), quarter=(1, 2, 0), deep=(2, 2, 1), rg=(1, 1, 0), dg=(2, 2, 1),
    mg=(1, 1, 0), cot=(0, 0, 2), mid=(1, 1, 2), stem=(0, 0, 3), ra=(1, 1, 3),
)
STACKS = dict(
    feat=(0, 0), cot=(0, 0), half=(0, 1), quarter=(1, 2), up2=(2, 1), mid=(1, 1), up1=(1, 0),
    stem=(0, 0), rg=(1, 1), dg=(2, 2), mg=(1, 1),
)


def blocks(size, lanes):
    return -(-size // lanes)


def segments(f, lanes):
    f0, f1, f2 = f
    return dict(
        low=[(f1, blocks(27 * f1, lanes))],
        up=[(f1, blocks(27 * f2, lanes))],
        bot=[(27 * f1, blocks(f2, lanes))],
        early=[(3 * f0, blocks(9 * f0, lanes))],
        fin=[(3 * f0, blocks(9 * f1, lanes))],
        mid=[(f1, blocks(27 * f0, lanes))],
        stem=[(f0, blocks(27 * f0, lanes))],
    )


STAGED = (("wid",), ("hgt",), ("dep",))


def orders():
    whole = math.prod(lax.axis_size(axis) for axis in GROUP)
    near = (GROUP[:1], GROUP[1:]) if whole <= 16 else STAGED
    return dict(low=STAGED, up=STAGED, bot=STAGED, early=STAGED, fin=STAGED, mid=STAGED, stem=near)


def step_kernel(cfg, back, *refs):
    (f0, f1, f2, w, d, h) = cfg
    ref = back(iter(refs))
    spans = {0: (w, d, h), 1: (w // 2, d // 2, h // 2), 2: (w // 4, d // 4, h // 4)}
    lanes = h
    halo = Names()
    last = {}
    for name, (_, level, group) in HALOS.items():
        own = ref.halos[name]
        halo[name] = Halo(group, own.rows, own.get(0, own.rows), own.edges, own.own, spans[level], (ref.send, ref.recv))
        halo[name].before = last.get(group)
        last[group] = halo[name]
    stacks = ref.stacks
    sums = Names()
    for name, order in orders().items():
        own = ref.sums[name]
        sums[name] = Summed(order, ref.outs[name], list(own.levels.values()), own.send, own.recv)

    loads = Names()
    for i, name in enumerate(ref.ins):
        loads[name] = pltpu.make_async_copy(ref.ins[name], ref.inside[name], ref.load.at[i])
        loads[name].start()
    halo.feat.clear()
    halo.cot.clear()

    def take(load, source, item):
        load.wait()
        ref.wide[...] = source[...].astype(F32)
        for a in range(w):
            for b in range(d):
                item.rows[a + 1, b + 1] = ref.wide[pl.ds(a * d + b, f0, stride=w * d), :].astype(BF)

    barrier = pltpu.get_barrier_semaphore()
    me, everyone = position(GROUP)
    for k in range(1, everyone):
        pl.semaphore_signal(
            barrier, 1, device_id=device_at(GROUP, lax.rem(me + k, everyone)), device_id_type=pl.DeviceIdType.MESH
        )
    take(loads.feat, ref.inside.feat, halo.feat)
    halo.half.clear()
    halo.stem.clear()
    pl.semaphore_wait(barrier, everyone - 1)

    halo.feat.start()
    take(loads.cot, ref.inside.cot, halo.cot)
    halo.cot.start()
    for item in (halo.quarter, halo.deep, halo.rg, halo.dg, halo.mg, halo.mid, halo.ra):
        item.clear()
    pool = pattern(lanes, lambda r, c: r // 2 == c)
    pool_mean = (pool / 8.0).astype(BF)
    pool_sum = pool.astype(BF)
    spread = pattern(lanes, lambda r, c: c // 2 == r)
    spread_mean = (spread / 8.0).astype(BF)

    def spreads(item):
        full = 2 * item.h
        each = [pattern(lanes, lambda r, c: (c < full) & (c // 2 == r - g * item.h)) for g in range(item.fold)]
        return [v.astype(BF) for v in each]

    def forward(raw, target):
        target[...] = raw[...].reshape(-1, raw.shape[2]).T

    def side_by_side(raw, target, low, high):
        width = high - low
        for k in range(raw.shape[0]):
            target[:, k * width : (k + 1) * width] = raw[k][:, low:high]

    loads.stem.wait()
    forward(ref.inside.stem, ref.w_stem)
    loads.fin.wait()
    forward(ref.inside.fin, ref.b_fin)
    side_by_side(ref.inside.fin, ref.w_fin_up, 0, f1)
    side_by_side(ref.inside.fin, ref.w_fin_low, f1, f1 + f0)
    loads.mid.wait()
    forward(ref.inside.mid, ref.w_mid)
    side_by_side(ref.inside.mid, ref.b_mid, 0, f1)
    loads.bot.wait()
    forward(ref.inside.bot, ref.w_bot)
    side_by_side(ref.inside.bot, ref.b_bot, 0, f2)
    loads.rise.wait()
    forward(ref.inside.rise, ref.b_rise)
    side_by_side(ref.inside.rise, ref.w_rise_up, 0, f2)
    side_by_side(ref.inside.rise, ref.w_rise_low, f2, f2 + f1)

    def stack(item, target, back=False):
        for a in range(item.w + 2):
            for b in range(item.d + 2):
                parts = item.shifted(a, b)
                target[a, b] = jnp.concatenate(parts[::-1] if back else parts, axis=0)

    def stack_up(up, target):
        spread = spreads(up)
        for i in range(up.w + 2):
            for j in range(up.d + 2):
                value = jnp.concatenate(up.shifted(i, j, spread), axis=0)
                for a in range(max(2 * i - 1, 0), min(2 * i + 1, target.shape[0])):
                    for b in range(max(2 * j - 1, 0), min(2 * j + 1, target.shape[1])):
                        target[a, b] = value

    def patch(source, a, b, pair, back=False, middle=False):
        third = source.shape[2] // 3
        rows = slice(third, 2 * third) if middle else slice(0, 3 * third)
        parts = []
        for q in range(pair):
            taps = [(ka, kb) for ka in range(3) for kb in range(3)]
            parts.append(
                jnp.concatenate([source[a + ka, b + kb + q, rows] for ka, kb in (taps[::-1] if back else taps)], axis=0)
            )
        return parts[0] if pair == 1 else jnp.concatenate(parts, axis=1)

    def over_rows(span, body):
        pair = 4 if span[1] % 4 == 0 else 2 if span[1] % 2 == 0 else 1
        across = span[1] // pair

        def trip(i, _):
            body(i // across, (i % across) * pair, pair)
            return 0

        count = span[0] * across
        if count <= 2:
            for i in range(count):
                trip(i, 0)
        else:
            lax.fori_loop(0, count, trip, 0)

    def conv(source, weight, span, store, back=False):
        def body(a, b, pair):
            result = mm(weight[...], patch(source, a, b, pair, back))
            for q in range(pair):
                store(a, b + q, result[:, q * lanes : (q + 1) * lanes])

        over_rows(span, body)

    def put_blocks(where, base, value):
        rows, width = value.shape
        count = blocks(width, lanes)
        if count * lanes > width:
            value = jnp.concatenate([value, jnp.zeros((rows, count * lanes - width), value.dtype)], axis=1)
        for j in range(count):
            where[base + j * rows : base + (j + 1) * rows] = value[:, j * lanes : (j + 1) * lanes]

    def beside(span, pick):
        return jnp.concatenate([pick(a, b) for a in range(span[0]) for b in range(span[1])], axis=1)

    halo.feat.wait()
    stack(halo.feat, stacks.feat)

    def stem_store(a, b, value):
        ref.stem_pre[a, b] = value
        halo.stem.rows[a + 1, b + 1] = silu(value).astype(BF)

    conv(stacks.feat, ref.w_stem, spans[0], stem_store)

    def pooled(fine, coarse):
        low, up = fine, coarse
        for a in range(up.w):
            for b in range(up.d):
                cat = [low.rows[2 * a + 1 + i, 2 * b + 1 + j] for i in range(2) for j in range(2)]
                total = mm(cat[0], pool_mean) + mm(cat[1], pool_mean) + mm(cat[2], pool_mean) + mm(cat[3], pool_mean)
                up.rows[a + 1, b + 1] = total.astype(BF)

    pooled(halo.stem, halo.half)
    halo.cot.wait()
    halo.half.start()
    halo.stem.start()
    stack(halo.cot, stacks.cot, back=True)
    ref.fb_pool[...] = jnp.zeros(ref.fb_pool.shape, F32)

    def back_store(a, b, value):
        ref.fb_pool[a // 2, b // 2] += value[:f1]
        ref.fb_skip[a, b] = value[f1:]

    conv(stacks.cot, ref.b_fin, spans[0], back_store, back=True)
    for a in range(spans[1][0]):
        for b in range(spans[1][1]):
            ref.fb_pool[a, b] = mm_split(ref.fb_pool[a, b], pool_sum)
    halo.half.wait()
    stack(halo.half, stacks.half)

    def mid_store(a, b, value):
        ref.mid_pre[a, b] = value
        halo.mid.rows[a + 1, b + 1] = silu(value).astype(BF)

    conv(stacks.half, ref.w_mid, spans[1], mid_store)
    pooled(halo.mid, halo.quarter)
    halo.quarter.start()
    halo.mid.start()
    halo.stem.wait()
    stack(halo.stem, stacks.stem)

    def final_low(a, b, value):
        ref.fin_part[a, b] = value

    conv(stacks.stem, ref.w_fin_low, spans[0], final_low)
    cot_cells = lambda: beside(spans[0], lambda a, b: stacks.cot[a + 1, b + 1])
    low_cells = beside(spans[0], lambda a, b: patch(stacks.stem, a, b, 1, middle=True))
    put_blocks(sums.early.total, 0, mm_nt(cot_cells(), low_cells))
    sums.early.step()
    halo.quarter.wait()
    stack(halo.quarter, stacks.quarter)

    def deep_store(a, b, value):
        ref.deep_pre[a, b] = value
        halo.deep.rows[a + 1, b + 1] = silu(value).astype(BF)

    conv(stacks.quarter, ref.w_bot, spans[2], deep_store)
    halo.deep.start()
    halo.mid.wait()
    stack(halo.mid, stacks.mid)

    def rise_low(a, b, value):
        ref.rise_pre[a, b] = value

    conv(stacks.mid, ref.w_rise_low, spans[1], rise_low)
    sums.early.step()
    halo.deep.wait()
    stack_up(halo.deep, stacks.up2)

    def rise_store(a, b, value):
        value = value + ref.rise_pre[a, b]
        halo.ra.rows[a + 1, b + 1] = silu(value).astype(BF)
        grad = ref.fb_pool[a, b] * slope(value)
        halo.rg.rows[a + 1, b + 1] = grad.astype(BF)

    conv(stacks.up2, ref.w_rise_up, spans[1], rise_store)
    halo.rg.start()
    halo.ra.start()

    sums.early.step()
    grad1 = lambda item: beside(spans[1], lambda a, b: item.rows[a + 1, b + 1])

    def wide_wgrad(segment, grad, source, span):
        cells = beside(span, lambda a, b: patch(source, a, b, 1))
        put_blocks(segment.total, 0, mm_nt(grad, cells))

    wide_wgrad(sums.low, grad1(halo.rg), stacks.mid, spans[1])
    sums.low.step()
    wide_wgrad(sums.up, grad1(halo.rg), stacks.up2, spans[1])
    sums.up.step()
    sums.low.step()
    halo.rg.wait()
    stack(halo.rg, stacks.rg, back=True)
    deep_sum = [[None] * spans[2][1] for _ in range(spans[2][0])]
    pair1 = 2 if spans[1][1] % 2 == 0 else 1
    for a in range(spans[1][0]):
        for b in range(0, spans[1][1], pair1):
            result = mm(ref.b_rise[...], patch(stacks.rg, a, b, pair1, back=True))
            for q in range(pair1):
                value = result[:, q * lanes : (q + 1) * lanes]
                ref.rb_skip[a, b + q] = value[f2:]
                ap, bt = a // 2, (b + q) // 2
                old = deep_sum[ap][bt]
                deep_sum[ap][bt] = value[:f2] if old is None else old + value[:f2]
    for a in range(spans[2][0]):
        for b in range(spans[2][1]):
            grad = mm_split(deep_sum[a][b], pool_sum) * slope(ref.deep_pre[a, b])
            halo.dg.rows[a + 1, b + 1] = grad.astype(BF)
    halo.dg.start()
    sums.up.step()
    sums.early.step()
    cells2 = beside(spans[2], lambda a, b: patch(stacks.quarter, a, b, 1))
    grad2 = beside(spans[2], lambda a, b: halo.dg.rows[a + 1, b + 1])
    bot = mm_nt(cells2, grad2)
    put_blocks(sums.bot.total, 0, bot)
    sums.bot.step()
    halo.ra.wait()
    stack_up(halo.ra, stacks.up1)
    sums.low.step()
    up_cells = beside(spans[0], lambda a, b: patch(stacks.up1, a, b, 1, middle=True))
    put_blocks(sums.fin.total, 0, mm_nt(cot_cells(), up_cells))
    sums.fin.step()
    sums.bot.step()
    halo.dg.wait()
    stack(halo.dg, stacks.dg, back=True)

    def quarter_store(a, b, value):
        wide = mm_split(value, spread_mean)
        for i in range(2):
            for j in range(2):
                at_, bt = 2 * a + i, 2 * b + j
                grad = (ref.rb_skip[at_, bt] + wide) * slope(ref.mid_pre[at_, bt])
                halo.mg.rows[at_ + 1, bt + 1] = grad.astype(BF)

    conv(stacks.dg, ref.b_bot, spans[2], quarter_store, back=True)
    halo.mg.start()
    sums.up.step()
    sums.fin.step()
    sums.early.step()
    wide_wgrad(sums.mid, grad1(halo.mg), stacks.half, spans[1])
    sums.mid.step()
    def final_store(a, b, value):
        ref.wide[pl.ds(a * d + b, f0, stride=w * d), :] = ref.fin_part[a, b] + value

    conv(stacks.up1, ref.w_fin_up, spans[0], final_store)
    ref.outs.output[...] = ref.wide[...].astype(BF)
    sums.low.step()
    sums.mid.step()
    sums.early.step()
    halo.mg.wait()
    stack(halo.mg, stacks.mg, back=True)

    def half_store(a, b, value):
        ref.half_wide[pl.ds(a * spans[1][1] + b, f0, stride=spans[1][0] * spans[1][1]), :] = value
        wide = mm_split(value, spread_mean)
        for i in range(2):
            for j in range(2):
                at_, bt = 2 * a + i, 2 * b + j
                grad = (ref.fb_skip[at_, bt] + wide) * slope(ref.stem_pre[at_, bt])
                ref.stem_grad[at_, bt] = grad.astype(BF)

    conv(stacks.mg, ref.b_mid, spans[1], half_store, back=True)
    ref.outs.half[...] = ref.half_wide[...]
    wide_wgrad(sums.stem, beside(spans[0], lambda a, b: ref.stem_grad[a, b]), stacks.feat, spans[0])

    sums.stem.step()
    sums.bot.step()
    sums.fin.step()
    sums.up.step()
    sums.mid.step()
    sums.low.step()
    sums.stem.step()
    sums.bot.step()
    sums.fin.step()
    sums.low.step()
    sums.up.step()
    sums.mid.step()
    sums.low.step()
    sums.stem.step()
    sums.bot.step()
    sums.up.step()
    sums.fin.step()
    sums.mid.step()
    sums.up.step()
    sums.stem.step()
    sums.stem.step()
    sums.bot.step()
    sums.fin.step()
    sums.mid.step()
    sums.bot.step()
    sums.fin.step()
    sums.mid.step()
    sums.early.step()
    for item in sums.values():
        item.finish()
    for item in halo.values():
        item.finish()


def unpack_kernel(cfg, back, *refs):
    (f0, f1, f2, lanes, scales) = cfg
    ref = back(iter(refs))
    loads = Names()
    for i, name in enumerate(ref.ins):
        loads[name] = pltpu.make_async_copy(ref.ins[name], ref.inside[name], ref.load.at[i])
        loads[name].start()
    stores = []

    def send(source, target):
        copy = pltpu.make_async_copy(source, target, ref.store.at[len(stores)])
        copy.start()
        stores.append(copy)

    def side(source, base, rows, width, scale):
        count = blocks(width, lanes)
        value = [source[base + j * rows : base + (j + 1) * rows].astype(F32) * scale for j in range(count)]
        return jnp.concatenate(value, axis=1)

    loads.output.wait()
    send(ref.inside.output, ref.outs.output)
    loads.half.wait()
    ref.ready.half[...] = ref.inside.half[:, : lanes // 2]
    send(ref.ready.half, ref.outs.half)
    loads.low.wait()
    loads.up.wait()
    low = side(ref.inside.low, 0, f1, 27 * f1, scales.rise)
    up = side(ref.inside.up, 0, f1, 27 * f2, scales.rise)
    for k in range(27):
        ref.ready.rise[k] = jnp.concatenate([up[:, k * f2 : (k + 1) * f2], low[:, k * f1 : (k + 1) * f1]], axis=1)
    send(ref.ready.rise, ref.outs.rise)
    loads.bot.wait()
    ref.ready.bot[...] = side(ref.inside.bot, 0, 27 * f1, f2, scales.bot)[:, :f2]
    send(ref.ready.bot, ref.outs.bot)
    loads.fin.wait()
    loads.early.wait()
    up = side(ref.inside.fin, 0, 3 * f0, 9 * f1, scales.fin)
    low = side(ref.inside.early, 0, 3 * f0, 9 * f0, scales.fin)
    for k in range(27):
        at_, rows = k // 3, slice((k % 3) * f0, (k % 3 + 1) * f0)
        ref.ready.fin[k] = jnp.concatenate([up[rows, at_ * f1 : (at_ + 1) * f1], low[rows, at_ * f0 : (at_ + 1) * f0]], axis=1)
    send(ref.ready.fin, ref.outs.fin)
    for load, source, target, out, scale in (
        (loads.mid, ref.inside.mid, ref.ready.mid, ref.outs.mid, scales.mid),
        (loads.stem, ref.inside.stem, ref.ready.stem, ref.outs.stem, scales.stem),
    ):
        load.wait()
        width = target.shape[1]
        for j in range(blocks(27 * f0, lanes)):
            value = (source[j * width : (j + 1) * width].astype(F32) * scale).T
            rows = min(lanes, 27 * f0 - j * lanes)
            target[j * lanes : j * lanes + rows] = value[:rows]
        send(target, out)
    for copy in stores:
        copy.wait()


def local(features, cotangent, w_stem, w_middle, w_bottom, w_rise, w_final):
    f0, w, d, h = features.shape
    f1, f2 = w_middle.shape[4], w_bottom.shape[4]
    f = (f0, f1, f2)
    spans = {0: (w, d), 1: (w // 2, d // 2), 2: (w // 4, d // 4)}
    near = neighbours()
    sets = 1 + max(group for _, _, group in HALOS.values())
    flat = w * d * f0
    inputs = dict(
        feat=features.reshape(flat, h),
        cot=cotangent.reshape(flat, h),
        stem=w_stem.reshape(27, f0, f0),
        fin=w_final.transpose(0, 1, 2, 4, 3).reshape(27, f0, f1 + f0),
        mid=w_middle.reshape(27, f0, f1),
        bot=w_bottom.reshape(27, f1, f2),
        rise=w_rise.transpose(0, 1, 2, 4, 3).reshape(27, f1, f2 + f1),
    )
    outs = dict(output=jax.ShapeDtypeStruct((flat, h), BF), half=jax.ShapeDtypeStruct((flat // 4, h), F32))
    halos, sums = {}, {}
    for name, (c, level, _) in HALOS.items():
        a, b = spans[level]
        tall = edge_rows(f[c], a * b, h)
        halos[name] = dict(
            rows=pltpu.VMEM((a + 2, b + 2, f[c], h), BF),
            edges=pltpu.VMEM((2, 3, 3, tall, h), BF),
            own=pltpu.VMEM((tall, h), BF),
        )
        fold = lane_parts(f[c], tall, h >> level, h)
        if fold > 1:
            halos[name][0] = pltpu.VMEM((a + 2, b + 2, f[c] // fold, h), BF)
    place = segments(f, h)
    for name, order in orders().items():
        unit = TILE * math.prod(lax.axis_size(axis) for axis in GROUP)
        rows = -(-sum(a * b for a, b in place[name]) // unit) * unit
        outs[name] = jax.ShapeDtypeStruct((rows, h), BF)
        levels = {}
        for i, axes in enumerate(order):
            for j, kind in enumerate((F32, BF, BF)):
                levels[3 * i + j] = pltpu.VMEM((rows, h), kind)
            rows //= math.prod(lax.axis_size(axis) for axis in axes)
        several = pltpu.SemaphoreType.DMA((2 * len(order),))
        sums[name] = dict(levels=levels, send=several, recv=several)

    def cells_of(c, level, kind=F32):
        return pltpu.VMEM((*spans[level], c, h), kind)

    def taps(a, b):
        return pltpu.VMEM((a, 27 * b), BF)

    scratch = dict(
        send=pltpu.SemaphoreType.DMA((sets * near,)),
        recv=pltpu.SemaphoreType.DMA((sets * near,)),
        load=pltpu.SemaphoreType.DMA((len(inputs),)),
        inside={name: pltpu.VMEM(v.shape, BF) for name, v in inputs.items()},
        halos=halos,
        sums=sums,
        stacks={
            name: pltpu.VMEM((spans[level][0] + 2, spans[level][1] + 2, 3 * f[c], h), BF)
            for name, (c, level) in STACKS.items()
        },
        stem_pre=cells_of(f0, 0), mid_pre=cells_of(f1, 1), deep_pre=cells_of(f2, 2), rise_pre=cells_of(f1, 1),
        fb_pool=cells_of(f1, 1), fb_skip=cells_of(f0, 0), rb_skip=cells_of(f1, 1), fin_part=cells_of(f0, 0),
        stem_grad=cells_of(f0, 0, BF),
        wide=pltpu.VMEM((flat, h), F32), half_wide=pltpu.VMEM((flat // 4, h), F32),
        w_stem=taps(f0, f0), w_mid=taps(f1, f0), w_bot=taps(f2, f1), w_rise_up=taps(f1, f2), w_rise_low=taps(f1, f1),
        w_fin_up=taps(f0, f1), w_fin_low=taps(f0, f0), b_mid=taps(f0, f1), b_bot=taps(f1, f2),
        b_rise=taps(f2 + f1, f1), b_fin=taps(f1 + f0, f0),
    )
    vmem = pl.BlockSpec(memory_space=pltpu.VMEM)
    anywhere = pl.BlockSpec(memory_space=pl.ANY)
    leaves, back = spread_out(dict(ins=inputs, outs=outs, **scratch))
    done = pl.pallas_call(
        functools.partial(step_kernel, (f0, f1, f2, w, d, h), back),
        out_shape=tuple(outs.values()),
        in_specs=[anywhere] * len(inputs),
        out_specs=(vmem,) * len(outs),
        scratch_shapes=leaves[len(inputs) + len(outs) :],
        compiler_params=pltpu.CompilerParams(collective_id=0, has_side_effects=True, vmem_limit_bytes=60 << 20),
        name="unet_step",
    )(*inputs.values())
    packed = dict(zip(outs, done))
    cells = w * d * h * math.prod(lax.axis_size(axis) for axis in GROUP)
    fine, mid, deep = (1.0 / math.sqrt(cells / k) for k in (1.0, 8.0, 64.0))
    scales = Names(stem=fine, mid=mid, bot=deep, rise=mid, fin=fine)

    results = dict(
        output=jax.ShapeDtypeStruct((flat, h), BF),
        stem=jax.ShapeDtypeStruct((27 * f0, f0), F32),
        mid=jax.ShapeDtypeStruct((27 * f0, f1), F32),
        bot=jax.ShapeDtypeStruct((27 * f1, f2), F32),
        rise=jax.ShapeDtypeStruct((27, f1, f2 + f1), F32),
        fin=jax.ShapeDtypeStruct((27, f0, f1 + f0), F32),
        half=jax.ShapeDtypeStruct((flat // 4, h // 2), F32),
    )
    hold = dict(
        inside={n: pltpu.VMEM(v.shape, v.dtype) for n, v in packed.items()},
        ready={n: pltpu.VMEM(v.shape, v.dtype) for n, v in results.items()},
        load=pltpu.SemaphoreType.DMA((len(packed),)),
        store=pltpu.SemaphoreType.DMA((len(results),)),
    )
    leaves, back = spread_out(dict(ins=packed, outs=results, **hold))
    final = pl.pallas_call(
        functools.partial(unpack_kernel, (f0, f1, f2, h, scales), back),
        out_shape=tuple(results.values()),
        in_specs=[anywhere] * len(packed),
        out_specs=(anywhere,) * len(results),
        scratch_shapes=leaves[len(packed) + len(results) :],
        compiler_params=pltpu.CompilerParams(vmem_limit_bytes=60 << 20),
        name="unpack",
    )(*packed.values())
    final = Names(zip(results, final))
    return (
        final.output.reshape(f0, w, d, h),
        final.stem.reshape(w_stem.shape),
        final.mid.reshape(w_middle.shape),
        final.bot.reshape(w_bottom.shape),
        final.rise.reshape(3, 3, 3, f1, f2 + f1).transpose(0, 1, 2, 4, 3),
        final.fin.reshape(3, 3, 3, f0, f1 + f0).transpose(0, 1, 2, 4, 3),
        final.half.reshape(f0, w // 2, d // 2, h // 2),
    )


def solution(mesh):
    placed = (P("grp", "wid", "dep", "hgt"), P("grp", "wid", "dep", "hgt"), P(), P(), P(), P(), P())
    grad = P("grp", None, None, None, None)
    return jax.shard_map(
        local,
        mesh=mesh,
        in_specs=placed,
        out_specs=(P("grp", "wid", "dep", "hgt"), grad, grad, grad, grad, grad, P("grp", "wid", "dep", "hgt")),
        check_vma=False,
    )
```

```python
import functools
import math

import jax
import jax.numpy as jnp
from jax import lax
from jax.experimental import pallas as pl
from jax.experimental.pallas import tpu as pltpu
from jax.sharding import PartitionSpec as P

BF, F32 = jnp.bfloat16, jnp.float32
AXES = ("grp", "dep", "hgt", "wid")
GROUP = ("wid", "hgt", "dep")
TILE = 16


class Names(dict):
    __getattr__ = dict.__getitem__


def spread_out(tree):
    if not isinstance(tree, dict):
        return [tree], lambda leaves: next(leaves)
    parts = {k: spread_out(v) for k, v in tree.items()}
    leaves = [leaf for some, _ in parts.values() for leaf in some]
    return leaves, lambda leaves: Names({k: back(leaves) for k, (_, back) in parts.items()})


def mm(a, b):
    return lax.dot_general(a, b, (((1,), (0,)), ((), ())), preferred_element_type=F32)


def mm_nt(a, b):
    return lax.dot_general(a, b, (((1,), (1,)), ((), ())), preferred_element_type=F32)


def mm_split(a, b):
    high = a.astype(BF)
    low = (a - high.astype(F32)).astype(BF)
    return mm(high, b) + mm(low, b)


def silu(v):
    return v * jax.nn.sigmoid(v)


def slope(v):
    g = jax.nn.sigmoid(v)
    return g * (1.0 + v * (1.0 - g))


def pattern(lanes, test):
    row = lax.broadcasted_iota(jnp.int32, (lanes, lanes), 0)
    col = lax.broadcasted_iota(jnp.int32, (lanes, lanes), 1)
    return jnp.where(test(row, col), 1.0, 0.0)


def neighbours():
    count = 1
    for name in GROUP:
        count *= min(lax.axis_size(name), 3)
    return count - 1


def edge_rows(channels, rows, lanes):
    size = TILE
    while channels % size or rows * (channels // size) > lanes // 2:
        size += TILE
    return size


def lane_parts(channels, tall, h, lanes):
    count = lanes // h
    while channels % (tall * count):
        count -= 1
    return count


class Halo:
    def __init__(self, group, rows, packed, edges, own, span, sems):
        self.rows, self.edges, self.own = rows, edges, own
        self.packed = packed
        self.fold = rows.shape[2] // packed.shape[2]
        self.base, self.sent_base = group * neighbours(), group // 2 * neighbours()
        self.w, self.d, self.h = span
        self.send, self.recv = sems
        self.before = None
        self.unsent = False
        self.side = own.shape[1] // 2
        self.tall = own.shape[0]
        self.per = rows.shape[2] // self.tall

    def outer(self, a, b):
        return a in (0, self.w + 1) or b in (0, self.d + 1)

    def clear(self):
        moving = self.rows if self.fold == 1 else self.packed
        blank = jnp.zeros(moving.shape[2:], BF)
        for a in range(self.w + 2):
            for b in range(self.d + 2):
                if self.outer(a, b):
                    moving[a, b] = blank
        self.edges[...] = jnp.zeros(self.edges.shape, BF)

    def fill_edges(self):
        lane = lax.broadcasted_iota(jnp.int32, self.own.shape, 1)
        tile = jnp.zeros(self.own.shape, F32)
        for a in range(self.w):
            for b in range(self.d):
                row = self.rows[a + 1, b + 1].astype(F32)
                for g in range(self.per):
                    r = (a * self.d + b) * self.per + g
                    part_of = row[g * self.tall : (g + 1) * self.tall]
                    tile = jnp.where(lane == r, part_of[:, 0:1], tile)
                    tile = jnp.where(lane == self.side + r, part_of[:, self.h - 1 : self.h], tile)
        self.own[...] = tile.astype(BF)

    def pack(self):
        tall = self.packed.shape[2]
        for a in range(1, self.w + 1):
            for b in range(1, self.d + 1):
                wide = self.rows[a, b].astype(F32)
                total = wide[:tall]
                for g in range(1, self.fold):
                    total = total + pltpu.roll(wide[g * tall : (g + 1) * tall], g * self.h, 1)
                self.packed[a, b] = total.astype(BF)

    def copies(self):
        moving = self.rows if self.fold == 1 else self.packed
        place = {name: lax.axis_index(name) for name in AXES}
        size = {name: lax.axis_size(name) for name in AXES}

        def choices(name):
            i, n = place[name], size[name]
            if n == 1:
                return [(0, 0, True, True)]
            if n == 2:
                return [(0, 0, True, True), (1, 1 - 2 * i, True, True)]
            return [(0, 0, True, True), (1, 1, i < n - 1, i > 0), (2, -1, i > 0, i < n - 1)]

        def cells(step, code, count):
            if code == 0:
                return pl.ds(1, count), pl.ds(1, count)
            up = (1 + step) // 2
            return pl.ds(1 + (count - 1) * up, 1), pl.ds((count + 1) * (1 - up), 1)

        out = []
        for cw, sw, ow, iw in choices("wid"):
            for cd, sd, od, id_ in choices("dep"):
                for ch, sh, oh, ih in choices("hgt"):
                    if cw == 0 and cd == 0 and ch == 0:
                        continue
                    slot = self.base + len(out)
                    target = {"wid": place["wid"] + sw, "dep": place["dep"] + sd, "hgt": place["hgt"] + sh}
                    if ch == 0:
                        from_w, to_w = cells(sw, cw, self.w)
                        from_d, to_d = cells(sd, cd, self.d)
                        source = moving.at[from_w, from_d]
                        dest = moving.at[to_w, to_d]
                    else:
                        source = self.own
                        dest = self.edges.at[(1 - sh) // 2, 1 - sw, 1 - sd]
                    copy = pltpu.make_async_remote_copy(
                        src_ref=source,
                        dst_ref=dest,
                        send_sem=self.send.at[self.sent_base + len(out)],
                        recv_sem=self.recv.at[slot],
                        device_id=target,
                        device_id_type=pl.DeviceIdType.MESH,
                    )
                    steps = 2 * (cd > 0) + 2 * (ch > 0) + (cw > 0)
                    out.append((copy, [c for c in (ow, od, oh) if c is not True], [c for c in (iw, id_, ih) if c is not True], steps))
        return out

    @staticmethod
    def guarded(conditions, action):
        if not conditions:
            action()
        else:
            pl.when(functools.reduce(jnp.logical_and, conditions))(action)

    def start(self):
        if self.before is not None:
            self.before.finish()
        self.fill_edges()
        if self.fold > 1:
            self.pack()
        for copy, can_send, _, _ in sorted(self.copies(), key=lambda entry: -entry[3]):
            self.guarded(can_send, copy.start)
        self.unsent = True

    def wait(self):
        for copy, _, can_take, _ in self.copies():
            self.guarded(can_take, copy.wait_recv)

    def finish(self):
        if self.unsent:
            for copy, can_send, _, _ in self.copies():
                self.guarded(can_send, copy.wait_send)
        self.unsent = False

    def shifted(self, a, b, spread=None):
        lanes = self.own.shape[1]
        h = self.h if spread is None else 2 * self.h
        folded = self.fold > 1 and self.outer(a, b)
        tall = self.packed.shape[2] if folded else self.rows.shape[2]
        row = self.packed[a, b] if folded else self.rows[a, b]
        if spread is not None:
            pieces = [mm(row, spread[g]) for g in range(self.fold if folded else 1)]
            wide = pieces[0] if len(pieces) == 1 else jnp.concatenate(pieces, axis=0)
            row = wide.astype(BF)
            folded = False
        else:
            wide = row.astype(F32)
        dw = 0 if a == 0 else 2 if a == self.w + 1 else 1
        dd = 0 if b == 0 else 2 if b == self.d + 1 else 1
        r = ((self.w - 1, a - 1, 0)[dw] * self.d + (self.d - 1, b - 1, 0)[dd]) * self.per
        lane = lax.broadcasted_iota(jnp.int32, (self.tall, lanes), 1)
        low, high = self.edges[0, dw, dd].astype(F32), self.edges[1, dw, dd].astype(F32)
        befores, centres, afters = [], [], []
        for g in range(self.per):
            turn, from_row = divmod(g * self.tall, tall) if folded else (0, g * self.tall)
            here = wide[from_row : from_row + self.tall]
            left = low[:, self.side + r + g : self.side + r + g + 1]
            right = high[:, r + g : r + g + 1]
            before = jnp.where(lane == 0, left, pltpu.roll(here, (lanes + 1 - turn * h) % lanes, 1))
            after = jnp.where(lane == h - 1, right, pltpu.roll(here, lanes - 1 - turn * h, 1))
            if h < lanes:
                before = jnp.where(lane < h, before, 0.0)
                after = jnp.where(lane < h, after, 0.0)
            befores.append(before.astype(BF))
            afters.append(after.astype(BF))
            if folded:
                centre = pltpu.roll(here, lanes - turn * h, 1) if turn else here
                centres.append(jnp.where(lane < h, centre, 0.0).astype(BF))
        if folded:
            row = jnp.concatenate(centres, axis=0)
        return jnp.concatenate(befores, axis=0), row, jnp.concatenate(afters, axis=0)


def part(i, m):
    return pl.ds(pl.multiple_of(i * m, TILE), m)


def axis_part(axis):
    return (axis, 1, lax.axis_size(axis)) if isinstance(axis, str) else axis


def members(axes):
    return math.prod(axis_part(axis)[2] for axis in axes)


def position(axes):
    place, count = 0, 1
    for axis in axes:
        name, stride, n = axis_part(axis)
        index = lax.axis_index(name)
        if (stride, n) != (1, lax.axis_size(name)):
            index = lax.rem(lax.div(index, stride), n)
        place = place * n + index
        count *= n
    return place, count


def device_at(axes, place):
    where = {name: lax.axis_index(name) for name in GROUP}
    for axis in axes[::-1]:
        name, stride, n = axis_part(axis)
        to = place if axis == axes[0] else lax.rem(place, n)
        if n == lax.axis_size(name):
            where[name] = to
        else:
            where[name] = where[name] + (to - lax.rem(lax.div(where[name], stride), n)) * stride
        place = lax.div(place, n)
    return where


class Summed:
    def __init__(self, order, full, buffers, send, recv):
        self.order, self.full = order, full
        self.levels = [buffers[3 * i : 3 * i + 3] for i in range(len(order))]
        self.total = buffers[0]
        self.send, self.recv = send, recv
        self.stage, self.open, self.last = 0, None, None

    def copy(self, stage, axes, source, dest, to):
        return pltpu.make_async_remote_copy(
            src_ref=source,
            dst_ref=dest,
            send_sem=self.send.at[0],
            recv_sem=self.recv.at[stage],
            device_id=device_at(axes, to),
            device_id_type=pl.DeviceIdType.MESH,
        )

    def exchange(self, stage, axes, pieces, whole, m):
        i, n = position(axes)
        if n == 1:
            return
        self.settle()
        for k in sorted(range(1, n), key=lambda k: -min(k, n - k)):
            to = lax.rem(i + k, n)
            source, dest = pieces(to, i)
            self.copy(stage, axes, source, dest, to).start()
        every = whole.at[pl.ds(0, (n - 1) * m)]
        self.open = self.copy(stage, axes, every, every, lax.rem(i + 1, n))
        self.last = self.open

    def settle(self):
        if self.last is not None:
            self.last.wait_send()
            self.last = None

    def step(self):
        stage, deep = self.stage, len(self.order)
        self.stage += 1
        if self.open is not None:
            self.open.wait_recv()
            self.open = None
        if 0 < stage <= deep:
            i, n = position(self.order[stage - 1])
            held, _, came = self.levels[stage - 1]
            m = held.shape[0] // n
            value = held[part(i, m)]
            for k in range(1, n):
                value = value + came[part(lax.rem(i + k, n), m)].astype(F32)
            if stage < deep:
                self.levels[stage][0][...] = value
            else:
                place, _ = position([axis for axes in self.order for axis in axes])
                self.full[part(place, m)] = value.astype(BF)
        if stage < deep:
            held, wire, came = self.levels[stage]
            i, n = position(self.order[stage])
            m = held.shape[0] // n
            for k in range(1, n):
                there = part(lax.rem(i + k, n), m)
                wire[there] = held[there].astype(BF)
            self.exchange(stage, self.order[stage], lambda to, me: (wire.at[part(to, m)], came.at[part(me, m)]), came, m)
        elif stage < 2 * deep:
            depth = 2 * deep - stage
            place, count = position([axis for axes in self.order[:depth] for axis in axes])
            m = self.full.shape[0] // count
            piece = self.full.at[part(place, m)]
            self.exchange(stage, self.order[depth - 1], lambda to, me: (piece, piece), self.full, m)

    def finish(self):
        while self.stage <= 2 * len(self.order):
            self.step()
        self.settle()


HALOS = dict(
    feat=(0, 0, 0), half=(0, 1, 1), quarter=(1, 2, 0), deep=(2, 2, 1), rg=(1, 1, 0), dg=(2, 2, 1),
    mg=(1, 1, 0), cot=(0, 0, 2), stem=(0, 0, 3), mid=(1, 1, 2), ra=(1, 1, 3),
)
STACKS = dict(
    feat=(0, 0), cot=(0, 0), half=(0, 1), quarter=(1, 2), up2=(2, 1), mid=(1, 1), up1=(1, 0),
    stem=(0, 0), rg=(1, 1), dg=(2, 2), mg=(1, 1),
)


def blocks(size, lanes):
    return -(-size // lanes)


def split_at(count):
    return count * 4 // 9


def segments(f, lanes):
    f0, f1, f2 = f
    return dict(
        low=[(f1, blocks(27 * f1, lanes))],
        upa=[(f1, split_at(blocks(27 * f2, lanes)))],
        upb=[(f1, blocks(27 * f2, lanes) - split_at(blocks(27 * f2, lanes)))],
        bot=[(27 * f1, blocks(f2, lanes))],
        early=[(3 * f0, blocks(9 * f0, lanes))],
        fin=[(3 * f0, blocks(9 * f1, lanes))],
        mid=[(f1, blocks(27 * f0, lanes))],
        stem=[(f0, blocks(27 * f0, lanes))],
    )


STAGED = (("wid",), ("hgt",), ("dep",))


def orders():
    near = (GROUP[:1], GROUP[1:]) if members(GROUP) <= 16 else STAGED
    n = lax.axis_size("dep")
    one, swap = ((GROUP,) if members(GROUP) <= 16 else STAGED), (STAGED[0], STAGED[2], STAGED[1])
    pairs = (*STAGED[:2], (("dep", 1, 2),), (("dep", 2, n // 2),)) if n % 2 == 0 else STAGED
    return dict(low=STAGED, upa=STAGED, upb=STAGED, bot=pairs, early=STAGED, fin=STAGED, mid=STAGED, stem=near)


def step_kernel(cfg, back, *refs):
    (f0, f1, f2, w, d, h) = cfg
    ref = back(iter(refs))
    spans = {0: (w, d, h), 1: (w // 2, d // 2, h // 2), 2: (w // 4, d // 4, h // 4)}
    lanes = h
    halo = Names()
    last = {}
    for name, (_, level, group) in HALOS.items():
        own = ref.halos[name]
        halo[name] = Halo(group, own.rows, own.get(0, own.rows), own.edges, own.own, spans[level], (ref.send, ref.recv))
        halo[name].before = last.get(group // 2)
        last[group // 2] = halo[name]
    stacks = ref.stacks
    sums = Names()
    for name, order in orders().items():
        own = ref.sums[name]
        sums[name] = Summed(order, ref.outs[name], list(own.levels.values()), own.send, own.recv)

    loads = Names()
    for i, name in enumerate(ref.ins):
        loads[name] = pltpu.make_async_copy(ref.ins[name], ref.inside[name], ref.load.at[i])
        loads[name].start()
    halo.feat.clear()
    halo.cot.clear()

    def take(load, source, item):
        load.wait()
        ref.wide[...] = source[...].astype(F32)
        for a in range(w):
            for b in range(d):
                item.rows[a + 1, b + 1] = ref.wide[pl.ds(a * d + b, f0, stride=w * d), :].astype(BF)

    barrier = pltpu.get_barrier_semaphore()
    me, everyone = position(GROUP)
    for k in range(1, everyone):
        pl.semaphore_signal(
            barrier, 1, device_id=device_at(GROUP, lax.rem(me + k, everyone)), device_id_type=pl.DeviceIdType.MESH
        )
    take(loads.feat, ref.inside.feat, halo.feat)
    halo.half.clear()
    halo.stem.clear()
    pl.semaphore_wait(barrier, everyone - 1)

    halo.feat.start()
    take(loads.cot, ref.inside.cot, halo.cot)
    halo.cot.start()
    for item in (halo.quarter, halo.deep, halo.rg, halo.dg, halo.mg, halo.mid, halo.ra):
        item.clear()
    pool = pattern(lanes, lambda r, c: r // 2 == c)
    pool_mean = (pool / 8.0).astype(BF)
    pool_sum = pool.astype(BF)
    spread = pattern(lanes, lambda r, c: c // 2 == r)
    spread_mean = (spread / 8.0).astype(BF)

    def spreads(item):
        full = 2 * item.h
        each = [pattern(lanes, lambda r, c: (c < full) & (c // 2 == r - g * item.h)) for g in range(item.fold)]
        return [v.astype(BF) for v in each]

    def forward(raw, target):
        target[...] = raw[...].reshape(-1, raw.shape[2]).T

    def side_by_side(raw, target, low, high):
        width = high - low
        for k in range(raw.shape[0]):
            target[:, k * width : (k + 1) * width] = raw[k][:, low:high]

    loads.stem.wait()
    forward(ref.inside.stem, ref.w_stem)
    loads.fin.wait()
    forward(ref.inside.fin, ref.b_fin)
    side_by_side(ref.inside.fin, ref.w_fin_up, 0, f1)
    side_by_side(ref.inside.fin, ref.w_fin_low, f1, f1 + f0)
    loads.mid.wait()
    forward(ref.inside.mid, ref.w_mid)
    side_by_side(ref.inside.mid, ref.b_mid, 0, f1)
    loads.bot.wait()
    forward(ref.inside.bot, ref.w_bot)
    side_by_side(ref.inside.bot, ref.b_bot, 0, f2)
    loads.rise.wait()
    forward(ref.inside.rise, ref.b_rise)
    side_by_side(ref.inside.rise, ref.w_rise_up, 0, f2)
    side_by_side(ref.inside.rise, ref.w_rise_low, f2, f2 + f1)

    def stack(item, target, back=False):
        for a in range(item.w + 2):
            for b in range(item.d + 2):
                parts = item.shifted(a, b)
                target[a, b] = jnp.concatenate(parts[::-1] if back else parts, axis=0)

    def stack_up(up, target):
        spread = spreads(up)
        for i in range(up.w + 2):
            for j in range(up.d + 2):
                value = jnp.concatenate(up.shifted(i, j, spread), axis=0)
                for a in range(max(2 * i - 1, 0), min(2 * i + 1, target.shape[0])):
                    for b in range(max(2 * j - 1, 0), min(2 * j + 1, target.shape[1])):
                        target[a, b] = value

    def patch(source, a, b, pair, back=False, middle=False):
        third = source.shape[2] // 3
        rows = slice(third, 2 * third) if middle else slice(0, 3 * third)
        parts = []
        for q in range(pair):
            taps = [(ka, kb) for ka in range(3) for kb in range(3)]
            parts.append(
                jnp.concatenate([source[a + ka, b + kb + q, rows] for ka, kb in (taps[::-1] if back else taps)], axis=0)
            )
        return parts[0] if pair == 1 else jnp.concatenate(parts, axis=1)

    def over_rows(span, body):
        pair = 4 if span[1] % 4 == 0 else 2 if span[1] % 2 == 0 else 1
        across = span[1] // pair

        def trip(i, _):
            body(i // across, (i % across) * pair, pair)
            return 0

        count = span[0] * across
        if count <= 2:
            for i in range(count):
                trip(i, 0)
        else:
            lax.fori_loop(0, count, trip, 0)

    def conv(source, weight, span, store, back=False):
        def body(a, b, pair):
            result = mm(weight[...], patch(source, a, b, pair, back))
            for q in range(pair):
                store(a, b + q, result[:, q * lanes : (q + 1) * lanes])

        over_rows(span, body)

    def put_blocks(where, base, value):
        rows, width = value.shape
        count = blocks(width, lanes)
        if count * lanes > width:
            value = jnp.concatenate([value, jnp.zeros((rows, count * lanes - width), value.dtype)], axis=1)
        for j in range(count):
            where[base + j * rows : base + (j + 1) * rows] = value[:, j * lanes : (j + 1) * lanes]

    def beside(span, pick):
        return jnp.concatenate([pick(a, b) for a in range(span[0]) for b in range(span[1])], axis=1)

    halo.feat.wait()
    stack(halo.feat, stacks.feat)

    def stem_store(a, b, value):
        ref.stem_pre[a, b] = value
        halo.stem.rows[a + 1, b + 1] = silu(value).astype(BF)

    conv(stacks.feat, ref.w_stem, spans[0], stem_store)

    def pooled(fine, coarse):
        low, up = fine, coarse
        for a in range(up.w):
            for b in range(up.d):
                cat = [low.rows[2 * a + 1 + i, 2 * b + 1 + j] for i in range(2) for j in range(2)]
                total = mm(cat[0], pool_mean) + mm(cat[1], pool_mean) + mm(cat[2], pool_mean) + mm(cat[3], pool_mean)
                up.rows[a + 1, b + 1] = total.astype(BF)

    pooled(halo.stem, halo.half)
    halo.cot.wait()
    halo.half.start()
    halo.stem.start()
    stack(halo.cot, stacks.cot, back=True)
    ref.fb_pool[...] = jnp.zeros(ref.fb_pool.shape, F32)

    def back_store(a, b, value):
        ref.fb_pool[a // 2, b // 2] += value[:f1]
        ref.fb_skip[a, b] = value[f1:]

    conv(stacks.cot, ref.b_fin, spans[0], back_store, back=True)
    for a in range(spans[1][0]):
        for b in range(spans[1][1]):
            ref.fb_pool[a, b] = mm_split(ref.fb_pool[a, b], pool_sum)
    halo.half.wait()
    stack(halo.half, stacks.half)

    def mid_store(a, b, value):
        ref.mid_pre[a, b] = value
        halo.mid.rows[a + 1, b + 1] = silu(value).astype(BF)

    conv(stacks.half, ref.w_mid, spans[1], mid_store)
    pooled(halo.mid, halo.quarter)
    halo.quarter.start()
    halo.mid.start()
    halo.stem.wait()
    stack(halo.stem, stacks.stem)

    def final_low(a, b, value):
        ref.fin_part[a, b] = value

    conv(stacks.stem, ref.w_fin_low, spans[0], final_low)
    cot_cells = lambda: beside(spans[0], lambda a, b: stacks.cot[a + 1, b + 1])
    low_cells = beside(spans[0], lambda a, b: patch(stacks.stem, a, b, 1, middle=True))
    put_blocks(sums.early.total, 0, mm_nt(cot_cells(), low_cells))
    sums.early.step()
    halo.quarter.wait()
    stack(halo.quarter, stacks.quarter)

    def deep_store(a, b, value):
        ref.deep_pre[a, b] = value
        halo.deep.rows[a + 1, b + 1] = silu(value).astype(BF)

    conv(stacks.quarter, ref.w_bot, spans[2], deep_store)
    halo.deep.start()
    halo.mid.wait()
    stack(halo.mid, stacks.mid)

    def rise_low(a, b, value):
        ref.rise_pre[a, b] = value

    conv(stacks.mid, ref.w_rise_low, spans[1], rise_low)
    sums.early.step()
    halo.deep.wait()
    stack_up(halo.deep, stacks.up2)

    def rise_store(a, b, value):
        value = value + ref.rise_pre[a, b]
        halo.ra.rows[a + 1, b + 1] = silu(value).astype(BF)
        grad = ref.fb_pool[a, b] * slope(value)
        halo.rg.rows[a + 1, b + 1] = grad.astype(BF)

    conv(stacks.up2, ref.w_rise_up, spans[1], rise_store)
    halo.rg.start()
    halo.ra.start()
    sums.early.step()

    grad1 = lambda item: beside(spans[1], lambda a, b: item.rows[a + 1, b + 1])

    def wide_wgrad(segment, grad, source, span, low=None, high=None):
        cells = beside(span, lambda a, b: patch(source, a, b, 1)[low:high])
        put_blocks(segment.total, 0, mm_nt(grad, cells))

    wide_wgrad(sums.low, grad1(halo.rg), stacks.mid, spans[1])
    sums.low.step()
    cut = split_at(blocks(27 * f2, lanes)) * lanes
    wide_wgrad(sums.upa, grad1(halo.rg), stacks.up2, spans[1], None, cut)
    sums.upa.step()
    wide_wgrad(sums.upb, grad1(halo.rg), stacks.up2, spans[1], cut, None)
    sums.low.step()
    sums.upb.step()
    sums.upa.step()
    halo.rg.wait()
    stack(halo.rg, stacks.rg, back=True)
    deep_sum = [[None] * spans[2][1] for _ in range(spans[2][0])]
    pair1 = 2 if spans[1][1] % 2 == 0 else 1
    for a in range(spans[1][0]):
        for b in range(0, spans[1][1], pair1):
            result = mm(ref.b_rise[...], patch(stacks.rg, a, b, pair1, back=True))
            for q in range(pair1):
                value = result[:, q * lanes : (q + 1) * lanes]
                ref.rb_skip[a, b + q] = value[f2:]
                ap, bt = a // 2, (b + q) // 2
                old = deep_sum[ap][bt]
                deep_sum[ap][bt] = value[:f2] if old is None else old + value[:f2]
    for a in range(spans[2][0]):
        for b in range(spans[2][1]):
            grad = mm_split(deep_sum[a][b], pool_sum) * slope(ref.deep_pre[a, b])
            halo.dg.rows[a + 1, b + 1] = grad.astype(BF)
    halo.dg.start()
    sums.upb.step()
    cells2 = beside(spans[2], lambda a, b: patch(stacks.quarter, a, b, 1))
    grad2 = beside(spans[2], lambda a, b: halo.dg.rows[a + 1, b + 1])
    bot = mm_nt(cells2, grad2)
    put_blocks(sums.bot.total, 0, bot)
    sums.bot.step()
    sums.early.step()
    halo.ra.wait()
    stack_up(halo.ra, stacks.up1)
    sums.low.step()
    sums.bot.step()
    up_cells = beside(spans[0], lambda a, b: patch(stacks.up1, a, b, 1, middle=True))
    put_blocks(sums.fin.total, 0, mm_nt(cot_cells(), up_cells))
    sums.upa.step()
    sums.fin.step()
    halo.dg.wait()
    stack(halo.dg, stacks.dg, back=True)

    def quarter_store(a, b, value):
        wide = mm_split(value, spread_mean)
        for i in range(2):
            for j in range(2):
                at_, bt = 2 * a + i, 2 * b + j
                grad = (ref.rb_skip[at_, bt] + wide) * slope(ref.mid_pre[at_, bt])
                halo.mg.rows[at_ + 1, bt + 1] = grad.astype(BF)

    conv(stacks.dg, ref.b_bot, spans[2], quarter_store, back=True)
    halo.mg.start()
    sums.fin.step()
    sums.upb.step()

    def final_row(a):
        result = mm(ref.w_fin_up[...], patch(stacks.up1, a, 0, d))
        for b in range(d):
            value = ref.fin_part[a, b] + result[:, b * lanes : (b + 1) * lanes]
            ref.wide[pl.ds(a * d + b, f0, stride=w * d), :] = value

    wide_wgrad(sums.mid, grad1(halo.mg), stacks.half, spans[1])
    sums.mid.step()
    sums.low.step()
    sums.early.step()
    final_row(0)
    final_row(1)
    sums.upa.step()
    sums.bot.step()
    final_row(2)
    sums.mid.step()
    final_row(3)
    ref.outs.output[...] = ref.wide[...].astype(BF)
    sums.fin.step()
    halo.mg.wait()
    stack(halo.mg, stacks.mg, back=True)

    def half_store(a, b, value):
        ref.half_wide[pl.ds(a * spans[1][1] + b, f0, stride=spans[1][0] * spans[1][1]), :] = value
        wide = mm_split(value, spread_mean)
        for i in range(2):
            for j in range(2):
                at_, bt = 2 * a + i, 2 * b + j
                grad = (ref.fb_skip[at_, bt] + wide) * slope(ref.stem_pre[at_, bt])
                ref.stem_grad[at_, bt] = grad.astype(BF)

    conv(stacks.mg, ref.b_mid, spans[1], half_store, back=True)
    ref.outs.half[...] = ref.half_wide[...]
    sums.bot.step()
    sums.low.step()
    sums.upb.step()
    wide_wgrad(sums.stem, beside(spans[0], lambda a, b: ref.stem_grad[a, b]), stacks.feat, spans[0])
    sums.stem.step()
    sums.upa.step()

    sums.mid.step()
    sums.fin.step()
    sums.stem.step()
    sums.low.step()
    sums.early.step()
    sums.upb.step()
    sums.bot.step()
    sums.upa.step()
    sums.fin.step()
    sums.mid.step()
    sums.stem.step()
    sums.bot.step()
    sums.low.step()
    sums.upa.step()
    sums.upb.step()
    sums.stem.step()
    sums.bot.step()
    sums.fin.step()
    sums.mid.step()
    sums.upb.step()
    sums.stem.step()
    sums.bot.step()
    sums.mid.step()
    sums.fin.step()
    sums.early.step()
    sums.bot.step()
    sums.mid.step()
    for item in sums.values():
        item.finish()
    for item in halo.values():
        item.finish()


def unpack_kernel(cfg, back, *refs):
    (f0, f1, f2, lanes, scales) = cfg
    ref = back(iter(refs))
    stores = []

    def send(source, target):
        copy = pltpu.make_async_copy(source, target, ref.store.at[len(stores)])
        copy.start()
        stores.append(copy)

    def side(source, base, rows, width, scale):
        count = blocks(width, lanes)
        value = [source[base + j * rows : base + (j + 1) * rows].astype(F32) * scale for j in range(count)]
        return jnp.concatenate(value, axis=1)

    send(ref.ins.output, ref.outs.output)
    ref.ready.half[...] = ref.ins.half[:, : lanes // 2]
    send(ref.ready.half, ref.outs.half)
    ref.ready.bot[...] = side(ref.ins.bot, 0, 27 * f1, f2, scales.bot)[:, :f2]
    send(ref.ready.bot, ref.outs.bot)
    low = side(ref.ins.low, 0, f1, 27 * f1, scales.rise)
    first = split_at(blocks(27 * f2, lanes))
    up = [side(ref.ins.upa, 0, f1, first * lanes, scales.rise)]
    up.append(side(ref.ins.upb, 0, f1, 27 * f2 - first * lanes, scales.rise))
    up = jnp.concatenate(up, axis=1)
    for k in range(27):
        ref.ready.rise[k] = jnp.concatenate([up[:, k * f2 : (k + 1) * f2], low[:, k * f1 : (k + 1) * f1]], axis=1)
    send(ref.ready.rise, ref.outs.rise)
    up = side(ref.ins.fin, 0, 3 * f0, 9 * f1, scales.fin)
    low = side(ref.ins.early, 0, 3 * f0, 9 * f0, scales.fin)
    for k in range(27):
        at_, rows = k // 3, slice((k % 3) * f0, (k % 3 + 1) * f0)
        ref.ready.fin[k] = jnp.concatenate([up[rows, at_ * f1 : (at_ + 1) * f1], low[rows, at_ * f0 : (at_ + 1) * f0]], axis=1)
    send(ref.ready.fin, ref.outs.fin)
    for source, target, out, scale in (
        (ref.ins.mid, ref.ready.mid, ref.outs.mid, scales.mid),
        (ref.ins.stem, ref.ready.stem, ref.outs.stem, scales.stem),
    ):
        width = target.shape[1]
        for j in range(blocks(27 * f0, lanes)):
            value = (source[j * width : (j + 1) * width].astype(F32) * scale).T
            rows = min(lanes, 27 * f0 - j * lanes)
            target[j * lanes : j * lanes + rows] = value[:rows]
        send(target, out)
    for copy in stores:
        copy.wait()


def local(features, cotangent, w_stem, w_middle, w_bottom, w_rise, w_final):
    f0, w, d, h = features.shape
    f1, f2 = w_middle.shape[4], w_bottom.shape[4]
    f = (f0, f1, f2)
    spans = {0: (w, d), 1: (w // 2, d // 2), 2: (w // 4, d // 4)}
    near = neighbours()
    sets = 1 + max(group for _, _, group in HALOS.values())
    flat = w * d * f0
    inputs = dict(
        feat=features.reshape(flat, h),
        cot=cotangent.reshape(flat, h),
        stem=w_stem.reshape(27, f0, f0),
        fin=w_final.transpose(0, 1, 2, 4, 3).reshape(27, f0, f1 + f0),
        mid=w_middle.reshape(27, f0, f1),
        bot=w_bottom.reshape(27, f1, f2),
        rise=w_rise.transpose(0, 1, 2, 4, 3).reshape(27, f1, f2 + f1),
    )
    outs = dict(output=jax.ShapeDtypeStruct((flat, h), BF), half=jax.ShapeDtypeStruct((flat // 4, h), F32))
    halos, sums = {}, {}
    for name, (c, level, _) in HALOS.items():
        a, b = spans[level]
        tall = edge_rows(f[c], a * b, h)
        halos[name] = dict(
            rows=pltpu.VMEM((a + 2, b + 2, f[c], h), BF),
            edges=pltpu.VMEM((2, 3, 3, tall, h), BF),
            own=pltpu.VMEM((tall, h), BF),
        )
        fold = lane_parts(f[c], tall, h >> level, h)
        if fold > 1:
            halos[name][0] = pltpu.VMEM((a + 2, b + 2, f[c] // fold, h), BF)
    place = segments(f, h)
    for name, order in orders().items():
        unit = TILE * members(GROUP)
        rows = -(-sum(a * b for a, b in place[name]) // unit) * unit
        outs[name] = jax.ShapeDtypeStruct((rows, h), BF)
        levels = {}
        for i, axes in enumerate(order):
            for j, kind in enumerate((F32, BF, BF)):
                levels[3 * i + j] = pltpu.VMEM((rows, h), kind)
            rows //= members(axes)
        sums[name] = dict(levels=levels, send=pltpu.SemaphoreType.DMA((1,)), recv=pltpu.SemaphoreType.DMA((2 * len(order),)))

    def cells_of(c, level, kind=F32):
        return pltpu.VMEM((*spans[level], c, h), kind)

    def taps(a, b):
        return pltpu.VMEM((a, 27 * b), BF)

    scratch = dict(
        send=pltpu.SemaphoreType.DMA((blocks(sets, 2) * near,)),
        recv=pltpu.SemaphoreType.DMA((sets * near,)),
        load=pltpu.SemaphoreType.DMA((len(inputs),)),
        inside={name: pltpu.VMEM(v.shape, BF) for name, v in inputs.items()},
        halos=halos,
        sums=sums,
        stacks={
            name: pltpu.VMEM((spans[level][0] + 2, spans[level][1] + 2, 3 * f[c], h), BF)
            for name, (c, level) in STACKS.items()
        },
        stem_pre=cells_of(f0, 0), mid_pre=cells_of(f1, 1), deep_pre=cells_of(f2, 2), rise_pre=cells_of(f1, 1),
        fb_pool=cells_of(f1, 1), fb_skip=cells_of(f0, 0), rb_skip=cells_of(f1, 1), fin_part=cells_of(f0, 0),
        stem_grad=cells_of(f0, 0, BF),
        wide=pltpu.VMEM((flat, h), F32), half_wide=pltpu.VMEM((flat // 4, h), F32),
        w_stem=taps(f0, f0), w_mid=taps(f1, f0), w_bot=taps(f2, f1), w_rise_up=taps(f1, f2), w_rise_low=taps(f1, f1),
        w_fin_up=taps(f0, f1), w_fin_low=taps(f0, f0), b_mid=taps(f0, f1), b_bot=taps(f1, f2),
        b_rise=taps(f2 + f1, f1), b_fin=taps(f1 + f0, f0),
    )
    vmem = pl.BlockSpec(memory_space=pltpu.VMEM)
    anywhere = pl.BlockSpec(memory_space=pl.ANY)
    leaves, back = spread_out(dict(ins=inputs, outs=outs, **scratch))
    done = pl.pallas_call(
        functools.partial(step_kernel, (f0, f1, f2, w, d, h), back),
        out_shape=tuple(outs.values()),
        in_specs=[anywhere] * len(inputs),
        out_specs=(vmem,) * len(outs),
        scratch_shapes=leaves[len(inputs) + len(outs) :],
        compiler_params=pltpu.CompilerParams(collective_id=0, has_side_effects=True, vmem_limit_bytes=52 << 20),
        name="unet_step",
    )(*[pltpu.with_memory_space_constraint(v, pltpu.HBM) for v in inputs.values()])
    packed = dict(zip(outs, done))
    cells = w * d * h * members(GROUP)
    fine, mid, deep = (1.0 / math.sqrt(cells / k) for k in (1.0, 8.0, 64.0))
    scales = Names(stem=fine, mid=mid, bot=deep, rise=mid, fin=fine)

    results = dict(
        output=jax.ShapeDtypeStruct((flat, h), BF),
        stem=jax.ShapeDtypeStruct((27 * f0, f0), F32),
        mid=jax.ShapeDtypeStruct((27 * f0, f1), F32),
        bot=jax.ShapeDtypeStruct((27 * f1, f2), F32),
        rise=jax.ShapeDtypeStruct((27, f1, f2 + f1), F32),
        fin=jax.ShapeDtypeStruct((27, f0, f1 + f0), F32),
        half=jax.ShapeDtypeStruct((flat // 4, h // 2), F32),
    )
    hold = dict(
        ready={n: pltpu.VMEM(v.shape, v.dtype) for n, v in results.items()},
        store=pltpu.SemaphoreType.DMA((len(results),)),
    )
    leaves, back = spread_out(dict(ins=packed, outs=results, **hold))
    final = pl.pallas_call(
        functools.partial(unpack_kernel, (f0, f1, f2, h, scales), back),
        out_shape=tuple(results.values()),
        in_specs=[vmem] * len(packed),
        out_specs=(anywhere,) * len(results),
        scratch_shapes=leaves[len(packed) + len(results) :],
        compiler_params=pltpu.CompilerParams(vmem_limit_bytes=46 << 20),
        name="unpack",
    )(*packed.values())
    final = Names(zip(results, final))
    return (
        final.output.reshape(f0, w, d, h),
        final.stem.reshape(w_stem.shape),
        final.mid.reshape(w_middle.shape),
        final.bot.reshape(w_bottom.shape),
        final.rise.reshape(3, 3, 3, f1, f2 + f1).transpose(0, 1, 2, 4, 3),
        final.fin.reshape(3, 3, 3, f0, f1 + f0).transpose(0, 1, 2, 4, 3),
        final.half.reshape(f0, w // 2, d // 2, h // 2),
    )


def solution(mesh):
    placed = (P("grp", "wid", "dep", "hgt"), P("grp", "wid", "dep", "hgt"), P(), P(), P(), P(), P())
    grad = P("grp", None, None, None, None)
    return jax.shard_map(
        local,
        mesh=mesh,
        in_specs=placed,
        out_specs=(P("grp", "wid", "dep", "hgt"), grad, grad, grad, grad, grad, P("grp", "wid", "dep", "hgt")),
        check_vma=False,
    )
```

```python
import functools
import math

import jax
import jax.numpy as jnp
from jax import lax
from jax.experimental import pallas as pl
from jax.experimental.pallas import tpu as pltpu
from jax.sharding import PartitionSpec as P

BF, F32 = jnp.bfloat16, jnp.float32
AXES = ("grp", "dep", "hgt", "wid")
GROUP = ("wid", "hgt", "dep")
TILE = 16


class Names(dict):
    __getattr__ = dict.__getitem__


def spread_out(tree):
    if not isinstance(tree, dict):
        return [tree], lambda leaves: next(leaves)
    parts = {k: spread_out(v) for k, v in tree.items()}
    leaves = [leaf for some, _ in parts.values() for leaf in some]
    return leaves, lambda leaves: Names({k: back(leaves) for k, (_, back) in parts.items()})


def mm(a, b):
    return lax.dot_general(a, b, (((1,), (0,)), ((), ())), preferred_element_type=F32)


def mm_nt(a, b):
    return lax.dot_general(a, b, (((1,), (1,)), ((), ())), preferred_element_type=F32)


def mm_split(a, b):
    high = a.astype(BF)
    low = (a - high.astype(F32)).astype(BF)
    return mm(high, b) + mm(low, b)


def silu(v):
    return v * jax.nn.sigmoid(v)


def slope(v):
    g = jax.nn.sigmoid(v)
    return g * (1.0 + v * (1.0 - g))


def pattern(lanes, test):
    row = lax.broadcasted_iota(jnp.int32, (lanes, lanes), 0)
    col = lax.broadcasted_iota(jnp.int32, (lanes, lanes), 1)
    return jnp.where(test(row, col), 1.0, 0.0)


def neighbours():
    count = 1
    for name in GROUP:
        count *= min(lax.axis_size(name), 3)
    return count - 1


def edge_rows(channels, rows, lanes):
    size = TILE
    while channels % size or rows * (channels // size) > lanes // 2:
        size += TILE
    return size


def lane_parts(channels, tall, h, lanes):
    count = lanes // h
    while channels % (tall * count):
        count -= 1
    return count


class Halo:
    def __init__(self, group, rows, packed, edges, own, span, sems):
        self.rows, self.edges, self.own = rows, edges, own
        self.packed = packed
        self.fold = rows.shape[2] // packed.shape[2]
        self.base, self.sent_base = group * neighbours(), group // 2 * neighbours()
        self.w, self.d, self.h = span
        self.send, self.recv = sems
        self.before = None
        self.unsent = False
        self.side = own.shape[1] // 2
        self.tall = own.shape[0]
        self.per = rows.shape[2] // self.tall

    def outer(self, a, b):
        return a in (0, self.w + 1) or b in (0, self.d + 1)

    def clear(self):
        moving = self.rows if self.fold == 1 else self.packed
        blank = jnp.zeros(moving.shape[2:], BF)
        for a in range(self.w + 2):
            for b in range(self.d + 2):
                if self.outer(a, b):
                    moving[a, b] = blank
        self.edges[...] = jnp.zeros(self.edges.shape, BF)

    def fill_edges(self):
        lane = lax.broadcasted_iota(jnp.int32, self.own.shape, 1)
        tile = jnp.zeros(self.own.shape, F32)
        for a in range(self.w):
            for b in range(self.d):
                row = self.rows[a + 1, b + 1].astype(F32)
                for g in range(self.per):
                    r = (a * self.d + b) * self.per + g
                    part_of = row[g * self.tall : (g + 1) * self.tall]
                    tile = jnp.where(lane == r, part_of[:, 0:1], tile)
                    tile = jnp.where(lane == self.side + r, part_of[:, self.h - 1 : self.h], tile)
        self.own[...] = tile.astype(BF)

    def pack(self):
        tall = self.packed.shape[2]
        for a in range(1, self.w + 1):
            for b in range(1, self.d + 1):
                wide = self.rows[a, b].astype(F32)
                total = wide[:tall]
                for g in range(1, self.fold):
                    total = total + pltpu.roll(wide[g * tall : (g + 1) * tall], g * self.h, 1)
                self.packed[a, b] = total.astype(BF)

    def copies(self):
        moving = self.rows if self.fold == 1 else self.packed
        place = {name: lax.axis_index(name) for name in AXES}
        size = {name: lax.axis_size(name) for name in AXES}

        def choices(name):
            i, n = place[name], size[name]
            if n == 1:
                return [(0, 0, True, True)]
            if n == 2:
                return [(0, 0, True, True), (1, 1 - 2 * i, True, True)]
            return [(0, 0, True, True), (1, 1, i < n - 1, i > 0), (2, -1, i > 0, i < n - 1)]

        def cells(step, code, count):
            if code == 0:
                return pl.ds(1, count), pl.ds(1, count)
            up = (1 + step) // 2
            return pl.ds(1 + (count - 1) * up, 1), pl.ds((count + 1) * (1 - up), 1)

        out = []
        for cw, sw, ow, iw in choices("wid"):
            for cd, sd, od, id_ in choices("dep"):
                for ch, sh, oh, ih in choices("hgt"):
                    if cw == 0 and cd == 0 and ch == 0:
                        continue
                    slot = self.base + len(out)
                    target = {"wid": place["wid"] + sw, "dep": place["dep"] + sd, "hgt": place["hgt"] + sh}
                    if ch == 0:
                        from_w, to_w = cells(sw, cw, self.w)
                        from_d, to_d = cells(sd, cd, self.d)
                        source = moving.at[from_w, from_d]
                        dest = moving.at[to_w, to_d]
                    else:
                        source = self.own
                        dest = self.edges.at[(1 - sh) // 2, 1 - sw, 1 - sd]
                    copy = pltpu.make_async_remote_copy(
                        src_ref=source,
                        dst_ref=dest,
                        send_sem=self.send.at[self.sent_base + len(out)],
                        recv_sem=self.recv.at[slot],
                        device_id=target,
                        device_id_type=pl.DeviceIdType.MESH,
                    )
                    steps = 2 * (cd > 0) + 2 * (ch > 0) + (cw > 0)
                    out.append((copy, [c for c in (ow, od, oh) if c is not True], [c for c in (iw, id_, ih) if c is not True], steps))
        return out

    @staticmethod
    def guarded(conditions, action):
        if not conditions:
            action()
        else:
            pl.when(functools.reduce(jnp.logical_and, conditions))(action)

    def start(self):
        if self.before is not None:
            self.before.finish()
        self.fill_edges()
        if self.fold > 1:
            self.pack()
        for copy, can_send, _, _ in sorted(self.copies(), key=lambda entry: -entry[3]):
            self.guarded(can_send, copy.start)
        self.unsent = True

    def wait(self):
        for copy, _, can_take, _ in self.copies():
            self.guarded(can_take, copy.wait_recv)

    def finish(self):
        if self.unsent:
            for copy, can_send, _, _ in self.copies():
                self.guarded(can_send, copy.wait_send)
        self.unsent = False

    def shifted(self, a, b, spread=None):
        lanes = self.own.shape[1]
        h = self.h if spread is None else 2 * self.h
        folded = self.fold > 1 and self.outer(a, b)
        tall = self.packed.shape[2] if folded else self.rows.shape[2]
        row = self.packed[a, b] if folded else self.rows[a, b]
        if spread is not None:
            pieces = [mm(row, spread[g]) for g in range(self.fold if folded else 1)]
            wide = pieces[0] if len(pieces) == 1 else jnp.concatenate(pieces, axis=0)
            row = wide.astype(BF)
            folded = False
        else:
            wide = row.astype(F32)
        dw = 0 if a == 0 else 2 if a == self.w + 1 else 1
        dd = 0 if b == 0 else 2 if b == self.d + 1 else 1
        r = ((self.w - 1, a - 1, 0)[dw] * self.d + (self.d - 1, b - 1, 0)[dd]) * self.per
        lane = lax.broadcasted_iota(jnp.int32, (self.tall, lanes), 1)
        low, high = self.edges[0, dw, dd].astype(F32), self.edges[1, dw, dd].astype(F32)
        befores, centres, afters = [], [], []
        for g in range(self.per):
            turn, from_row = divmod(g * self.tall, tall) if folded else (0, g * self.tall)
            here = wide[from_row : from_row + self.tall]
            left = low[:, self.side + r + g : self.side + r + g + 1]
            right = high[:, r + g : r + g + 1]
            before = jnp.where(lane == 0, left, pltpu.roll(here, (lanes + 1 - turn * h) % lanes, 1))
            after = jnp.where(lane == h - 1, right, pltpu.roll(here, lanes - 1 - turn * h, 1))
            if h < lanes:
                before = jnp.where(lane < h, before, 0.0)
                after = jnp.where(lane < h, after, 0.0)
            befores.append(before.astype(BF))
            afters.append(after.astype(BF))
            if folded:
                centre = pltpu.roll(here, lanes - turn * h, 1) if turn else here
                centres.append(jnp.where(lane < h, centre, 0.0).astype(BF))
        if folded:
            row = jnp.concatenate(centres, axis=0)
        return jnp.concatenate(befores, axis=0), row, jnp.concatenate(afters, axis=0)


def part(i, m):
    return pl.ds(pl.multiple_of(i * m, TILE), m)


def axis_part(axis):
    return (axis, 1, lax.axis_size(axis)) if isinstance(axis, str) else axis


def members(axes):
    return math.prod(axis_part(axis)[2] for axis in axes)


def position(axes):
    place, count = 0, 1
    for axis in axes:
        name, stride, n = axis_part(axis)
        index = lax.axis_index(name)
        if (stride, n) != (1, lax.axis_size(name)):
            index = lax.rem(lax.div(index, stride), n)
        place = place * n + index
        count *= n
    return place, count


def device_at(axes, place):
    where = {name: lax.axis_index(name) for name in GROUP}
    for axis in axes[::-1]:
        name, stride, n = axis_part(axis)
        to = place if axis == axes[0] else lax.rem(place, n)
        if n == lax.axis_size(name):
            where[name] = to
        else:
            where[name] = where[name] + (to - lax.rem(lax.div(where[name], stride), n)) * stride
        place = lax.div(place, n)
    return where


class Summed:
    def __init__(self, order, full, buffers, send, recv):
        self.order, self.full = order, full
        self.levels = [buffers[3 * i : 3 * i + 3] for i in range(len(order))]
        self.total = buffers[0]
        self.send, self.recv = send, recv
        self.stage, self.open, self.last = 0, None, None

    def copy(self, stage, axes, source, dest, to):
        return pltpu.make_async_remote_copy(
            src_ref=source,
            dst_ref=dest,
            send_sem=self.send.at[0],
            recv_sem=self.recv.at[stage],
            device_id=device_at(axes, to),
            device_id_type=pl.DeviceIdType.MESH,
        )

    def exchange(self, stage, axes, pieces, whole, m):
        i, n = position(axes)
        if n == 1:
            return
        self.settle()
        for k in sorted(range(1, n), key=lambda k: -min(k, n - k)):
            to = lax.rem(i + k, n)
            source, dest = pieces(to, i)
            self.copy(stage, axes, source, dest, to).start()
        every = whole.at[pl.ds(0, (n - 1) * m)]
        self.open = self.copy(stage, axes, every, every, lax.rem(i + 1, n))
        self.last = self.open

    def settle(self):
        if self.last is not None:
            self.last.wait_send()
            self.last = None

    def step(self):
        stage, deep = self.stage, len(self.order)
        self.stage += 1
        if self.open is not None:
            self.open.wait_recv()
            self.open = None
        if 0 < stage <= deep:
            i, n = position(self.order[stage - 1])
            held, _, came = self.levels[stage - 1]
            m = held.shape[0] // n
            value = held[part(i, m)]
            for k in range(1, n):
                value = value + came[part(lax.rem(i + k, n), m)].astype(F32)
            if stage < deep:
                self.levels[stage][0][...] = value
            else:
                place, _ = position([axis for axes in self.order for axis in axes])
                self.full[part(place, m)] = value.astype(BF)
        if stage < deep:
            held, wire, came = self.levels[stage]
            i, n = position(self.order[stage])
            m = held.shape[0] // n
            for k in range(1, n):
                there = part(lax.rem(i + k, n), m)
                wire[there] = held[there].astype(BF)
            self.exchange(stage, self.order[stage], lambda to, me: (wire.at[part(to, m)], came.at[part(me, m)]), came, m)
        elif stage < 2 * deep:
            depth = 2 * deep - stage
            place, count = position([axis for axes in self.order[:depth] for axis in axes])
            m = self.full.shape[0] // count
            piece = self.full.at[part(place, m)]
            self.exchange(stage, self.order[depth - 1], lambda to, me: (piece, piece), self.full, m)

    def finish(self):
        while self.stage <= 2 * len(self.order):
            self.step()
        self.settle()


HALOS = dict(
    feat=(0, 0, 0), half=(0, 1, 1), quarter=(1, 2, 0), deep=(2, 2, 1), rg=(1, 1, 0), dg=(2, 2, 1),
    mg=(1, 1, 0), cot=(0, 0, 2), stem=(0, 0, 3), mid=(1, 1, 2), ra=(1, 1, 3),
)
STACKS = dict(
    feat=(0, 0), cot=(0, 0), half=(0, 1), quarter=(1, 2), up2=(2, 1), mid=(1, 1), up1=(1, 0),
    stem=(0, 0), rg=(1, 1), dg=(2, 2), mg=(1, 1),
)


def blocks(size, lanes):
    return -(-size // lanes)


def split_at(count):
    return count * 4 // 9


def segments(f, lanes):
    f0, f1, f2 = f
    return dict(
        low=[(f1, blocks(27 * f1, lanes))],
        upa=[(f1, split_at(blocks(27 * f2, lanes)))],
        upb=[(f1, blocks(27 * f2, lanes) - split_at(blocks(27 * f2, lanes)))],
        bota=[(16 * f1, blocks(f2, lanes))],
        botb=[(11 * f1, blocks(f2, lanes))],
        early=[(3 * f0, blocks(9 * f0, lanes))],
        fin=[(3 * f0, blocks(9 * f1, lanes))],
        mid=[(f1, blocks(27 * f0, lanes))],
        stem=[(f0, blocks(27 * f0, lanes))],
    )


STAGED = (("wid",), ("hgt",), ("dep",))


def orders():
    near = (GROUP[:1], GROUP[1:]) if members(GROUP) <= 16 else STAGED
    n = lax.axis_size("dep")
    one, swap = ((GROUP,) if members(GROUP) <= 16 else STAGED), (STAGED[0], STAGED[2], STAGED[1])
    pairs = (*STAGED[:2], (("dep", 1, 2),), (("dep", 2, n // 2),)) if n % 2 == 0 else STAGED
    return dict(low=STAGED, upa=STAGED, upb=STAGED, bota=pairs, botb=pairs, early=STAGED, fin=STAGED, mid=STAGED, stem=near)


def step_kernel(cfg, back, *refs):
    (f0, f1, f2, w, d, h) = cfg
    ref = back(iter(refs))
    spans = {0: (w, d, h), 1: (w // 2, d // 2, h // 2), 2: (w // 4, d // 4, h // 4)}
    lanes = h
    halo = Names()
    last = {}
    for name, (_, level, group) in HALOS.items():
        own = ref.halos[name]
        halo[name] = Halo(group, own.rows, own.get(0, own.rows), own.edges, own.own, spans[level], (ref.send, ref.recv))
        halo[name].before = last.get(group // 2)
        last[group // 2] = halo[name]
    stacks = ref.stacks
    sums = Names()
    for name, order in orders().items():
        own = ref.sums[name]
        sums[name] = Summed(order, ref.outs[name], list(own.levels.values()), own.send, own.recv)

    loads = Names()
    for i, name in enumerate(ref.ins):
        loads[name] = pltpu.make_async_copy(ref.ins[name], ref.inside[name], ref.load.at[i])
        loads[name].start()
    halo.feat.clear()
    halo.cot.clear()

    def take(load, source, item):
        load.wait()
        ref.wide[...] = source[...].astype(F32)
        for a in range(w):
            for b in range(d):
                item.rows[a + 1, b + 1] = ref.wide[pl.ds(a * d + b, f0, stride=w * d), :].astype(BF)

    barrier = pltpu.get_barrier_semaphore()
    me, everyone = position(GROUP)
    for k in range(1, everyone):
        pl.semaphore_signal(
            barrier, 1, device_id=device_at(GROUP, lax.rem(me + k, everyone)), device_id_type=pl.DeviceIdType.MESH
        )
    take(loads.feat, ref.inside.feat, halo.feat)
    halo.half.clear()
    halo.stem.clear()
    pl.semaphore_wait(barrier, everyone - 1)

    halo.feat.start()
    take(loads.cot, ref.inside.cot, halo.cot)
    halo.cot.start()
    for item in (halo.quarter, halo.deep, halo.rg, halo.dg, halo.mg, halo.mid, halo.ra):
        item.clear()
    pool = pattern(lanes, lambda r, c: r // 2 == c)
    pool_mean = (pool / 8.0).astype(BF)
    pool_sum = pool.astype(BF)
    spread = pattern(lanes, lambda r, c: c // 2 == r)
    spread_mean = (spread / 8.0).astype(BF)

    def spreads(item):
        full = 2 * item.h
        each = [pattern(lanes, lambda r, c: (c < full) & (c // 2 == r - g * item.h)) for g in range(item.fold)]
        return [v.astype(BF) for v in each]

    def forward(raw, target):
        target[...] = raw[...].reshape(-1, raw.shape[2]).T

    def side_by_side(raw, target, low, high):
        width = high - low
        for k in range(raw.shape[0]):
            target[:, k * width : (k + 1) * width] = raw[k][:, low:high]

    loads.stem.wait()
    forward(ref.inside.stem, ref.w_stem)
    loads.fin.wait()
    forward(ref.inside.fin, ref.b_fin)
    side_by_side(ref.inside.fin, ref.w_fin_up, 0, f1)
    side_by_side(ref.inside.fin, ref.w_fin_low, f1, f1 + f0)
    loads.mid.wait()
    forward(ref.inside.mid, ref.w_mid)
    side_by_side(ref.inside.mid, ref.b_mid, 0, f1)
    loads.bot.wait()
    forward(ref.inside.bot, ref.w_bot)
    side_by_side(ref.inside.bot, ref.b_bot, 0, f2)
    loads.rise.wait()
    forward(ref.inside.rise, ref.b_rise)
    side_by_side(ref.inside.rise, ref.w_rise_up, 0, f2)
    side_by_side(ref.inside.rise, ref.w_rise_low, f2, f2 + f1)

    def stack(item, target, back=False):
        for a in range(item.w + 2):
            for b in range(item.d + 2):
                parts = item.shifted(a, b)
                target[a, b] = jnp.concatenate(parts[::-1] if back else parts, axis=0)

    def stack_up(up, target):
        spread = spreads(up)
        for i in range(up.w + 2):
            for j in range(up.d + 2):
                value = jnp.concatenate(up.shifted(i, j, spread), axis=0)
                for a in range(max(2 * i - 1, 0), min(2 * i + 1, target.shape[0])):
                    for b in range(max(2 * j - 1, 0), min(2 * j + 1, target.shape[1])):
                        target[a, b] = value

    def patch(source, a, b, pair, back=False, middle=False):
        third = source.shape[2] // 3
        rows = slice(third, 2 * third) if middle else slice(0, 3 * third)
        parts = []
        for q in range(pair):
            taps = [(ka, kb) for ka in range(3) for kb in range(3)]
            parts.append(
                jnp.concatenate([source[a + ka, b + kb + q, rows] for ka, kb in (taps[::-1] if back else taps)], axis=0)
            )
        return parts[0] if pair == 1 else jnp.concatenate(parts, axis=1)

    def over_rows(span, body):
        pair = 4 if span[1] % 4 == 0 else 2 if span[1] % 2 == 0 else 1
        across = span[1] // pair

        def trip(i, _):
            body(i // across, (i % across) * pair, pair)
            return 0

        count = span[0] * across
        if count <= 2:
            for i in range(count):
                trip(i, 0)
        else:
            lax.fori_loop(0, count, trip, 0)

    def conv(source, weight, span, store, back=False):
        def body(a, b, pair):
            result = mm(weight[...], patch(source, a, b, pair, back))
            for q in range(pair):
                store(a, b + q, result[:, q * lanes : (q + 1) * lanes])

        over_rows(span, body)

    def put_blocks(where, base, value):
        rows, width = value.shape
        count = blocks(width, lanes)
        if count * lanes > width:
            value = jnp.concatenate([value, jnp.zeros((rows, count * lanes - width), value.dtype)], axis=1)
        for j in range(count):
            where[base + j * rows : base + (j + 1) * rows] = value[:, j * lanes : (j + 1) * lanes]

    def beside(span, pick):
        return jnp.concatenate([pick(a, b) for a in range(span[0]) for b in range(span[1])], axis=1)

    halo.feat.wait()
    stack(halo.feat, stacks.feat)

    def stem_store(a, b, value):
        ref.stem_pre[a, b] = value
        halo.stem.rows[a + 1, b + 1] = silu(value).astype(BF)

    conv(stacks.feat, ref.w_stem, spans[0], stem_store)

    def pooled(fine, coarse):
        low, up = fine, coarse
        for a in range(up.w):
            for b in range(up.d):
                cat = [low.rows[2 * a + 1 + i, 2 * b + 1 + j] for i in range(2) for j in range(2)]
                total = mm(cat[0], pool_mean) + mm(cat[1], pool_mean) + mm(cat[2], pool_mean) + mm(cat[3], pool_mean)
                up.rows[a + 1, b + 1] = total.astype(BF)

    pooled(halo.stem, halo.half)
    halo.cot.wait()
    halo.half.start()
    halo.stem.start()
    stack(halo.cot, stacks.cot, back=True)
    ref.fb_pool[...] = jnp.zeros(ref.fb_pool.shape, F32)

    def back_store(a, b, value):
        ref.fb_pool[a // 2, b // 2] += value[:f1]
        ref.fb_skip[a, b] = value[f1:]

    conv(stacks.cot, ref.b_fin, spans[0], back_store, back=True)
    for a in range(spans[1][0]):
        for b in range(spans[1][1]):
            ref.fb_pool[a, b] = mm_split(ref.fb_pool[a, b], pool_sum)
    halo.half.wait()
    stack(halo.half, stacks.half)

    def mid_store(a, b, value):
        ref.mid_pre[a, b] = value
        halo.mid.rows[a + 1, b + 1] = silu(value).astype(BF)

    conv(stacks.half, ref.w_mid, spans[1], mid_store)
    pooled(halo.mid, halo.quarter)
    halo.quarter.start()
    halo.mid.start()
    halo.stem.wait()
    stack(halo.stem, stacks.stem)

    def final_low(a, b, value):
        ref.fin_part[a, b] = value

    conv(stacks.stem, ref.w_fin_low, spans[0], final_low)
    cot_cells = lambda: beside(spans[0], lambda a, b: stacks.cot[a + 1, b + 1])
    low_cells = beside(spans[0], lambda a, b: patch(stacks.stem, a, b, 1, middle=True))
    put_blocks(sums.early.total, 0, mm_nt(cot_cells(), low_cells))
    sums.early.step()
    halo.quarter.wait()
    stack(halo.quarter, stacks.quarter)

    def deep_store(a, b, value):
        ref.deep_pre[a, b] = value
        halo.deep.rows[a + 1, b + 1] = silu(value).astype(BF)

    conv(stacks.quarter, ref.w_bot, spans[2], deep_store)
    halo.deep.start()
    halo.mid.wait()
    stack(halo.mid, stacks.mid)

    def rise_low(a, b, value):
        ref.rise_pre[a, b] = value

    conv(stacks.mid, ref.w_rise_low, spans[1], rise_low)
    sums.early.step()
    for held in (ref.stem_pre, ref.mid_pre, ref.deep_pre):
        for a in range(held.shape[0]):
            for b in range(held.shape[1]):
                held[a, b] = slope(held[a, b])
    halo.deep.wait()
    stack_up(halo.deep, stacks.up2)

    def rise_store(a, b, value):
        value = value + ref.rise_pre[a, b]
        halo.ra.rows[a + 1, b + 1] = silu(value).astype(BF)
        grad = ref.fb_pool[a, b] * slope(value)
        halo.rg.rows[a + 1, b + 1] = grad.astype(BF)

    conv(stacks.up2, ref.w_rise_up, spans[1], rise_store)
    halo.rg.start()
    halo.ra.start()
    sums.early.step()

    grad1 = lambda item: beside(spans[1], lambda a, b: item.rows[a + 1, b + 1])

    def wide_wgrad(segment, grad, source, span, low=None, high=None):
        cells = beside(span, lambda a, b: patch(source, a, b, 1)[low:high])
        put_blocks(segment.total, 0, mm_nt(grad, cells))

    wide_wgrad(sums.low, grad1(halo.rg), stacks.mid, spans[1])
    sums.low.step()
    cut = split_at(blocks(27 * f2, lanes)) * lanes
    wide_wgrad(sums.upa, grad1(halo.rg), stacks.up2, spans[1], None, cut)
    sums.upa.step()
    wide_wgrad(sums.upb, grad1(halo.rg), stacks.up2, spans[1], cut, None)
    sums.low.step()
    sums.upb.step()
    sums.upa.step()
    halo.rg.wait()
    stack(halo.rg, stacks.rg, back=True)
    deep_sum = [[None] * spans[2][1] for _ in range(spans[2][0])]
    pair1 = 2 if spans[1][1] % 2 == 0 else 1
    for a in range(spans[1][0]):
        for b in range(0, spans[1][1], pair1):
            result = mm(ref.b_rise[...], patch(stacks.rg, a, b, pair1, back=True))
            for q in range(pair1):
                value = result[:, q * lanes : (q + 1) * lanes]
                ref.rb_skip[a, b + q] = value[f2:]
                ap, bt = a // 2, (b + q) // 2
                old = deep_sum[ap][bt]
                deep_sum[ap][bt] = value[:f2] if old is None else old + value[:f2]
    for a in range(spans[2][0]):
        for b in range(spans[2][1]):
            grad = mm_split(deep_sum[a][b], pool_sum) * ref.deep_pre[a, b]
            halo.dg.rows[a + 1, b + 1] = grad.astype(BF)
    halo.dg.start()
    sums.upb.step()
    cells2 = beside(spans[2], lambda a, b: patch(stacks.quarter, a, b, 1))
    grad2 = beside(spans[2], lambda a, b: halo.dg.rows[a + 1, b + 1])
    bot = mm_nt(cells2, grad2)
    put_blocks(sums.bota.total, 0, bot[: 16 * f1])
    put_blocks(sums.botb.total, 0, bot[16 * f1 :])
    sums.bota.step()
    sums.botb.step()
    sums.early.step()
    halo.ra.wait()
    stack_up(halo.ra, stacks.up1)
    sums.low.step()
    up_cells = beside(spans[0], lambda a, b: patch(stacks.up1, a, b, 1, middle=True))
    put_blocks(sums.fin.total, 0, mm_nt(cot_cells(), up_cells))
    sums.bota.step()
    sums.botb.step()
    sums.upa.step()
    sums.fin.step()
    halo.dg.wait()
    stack(halo.dg, stacks.dg, back=True)

    def quarter_store(a, b, value):
        wide = mm_split(value, spread_mean)
        for i in range(2):
            for j in range(2):
                at_, bt = 2 * a + i, 2 * b + j
                grad = (ref.rb_skip[at_, bt] + wide) * ref.mid_pre[at_, bt]
                halo.mg.rows[at_ + 1, bt + 1] = grad.astype(BF)

    conv(stacks.dg, ref.b_bot, spans[2], quarter_store, back=True)
    halo.mg.start()
    sums.fin.step()
    sums.upb.step()

    def final_row(a):
        result = mm(ref.w_fin_up[...], patch(stacks.up1, a, 0, d))
        for b in range(d):
            value = ref.fin_part[a, b] + result[:, b * lanes : (b + 1) * lanes]
            ref.wide[pl.ds(a * d + b, f0, stride=w * d), :] = value

    wide_wgrad(sums.mid, grad1(halo.mg), stacks.half, spans[1])
    sums.mid.step()
    sums.low.step()
    sums.early.step()
    sums.bota.step()
    final_row(0)
    final_row(1)
    sums.botb.step()
    sums.upa.step()
    final_row(2)
    sums.mid.step()
    final_row(3)
    ref.outs.output[...] = ref.wide[...].astype(BF)
    sums.fin.step()
    halo.mg.wait()
    stack(halo.mg, stacks.mg, back=True)

    def half_store(a, b, value):
        ref.half_wide[pl.ds(a * spans[1][1] + b, f0, stride=spans[1][0] * spans[1][1]), :] = value
        wide = mm_split(value, spread_mean)
        for i in range(2):
            for j in range(2):
                at_, bt = 2 * a + i, 2 * b + j
                grad = (ref.fb_skip[at_, bt] + wide) * ref.stem_pre[at_, bt]
                ref.stem_grad[at_, bt] = grad.astype(BF)

    conv(stacks.mg, ref.b_mid, spans[1], half_store, back=True)
    ref.outs.half[...] = ref.half_wide[...]
    sums.low.step()
    sums.bota.step()
    sums.upb.step()
    wide_wgrad(sums.stem, beside(spans[0], lambda a, b: ref.stem_grad[a, b]), stacks.feat, spans[0])
    sums.stem.step()
    sums.botb.step()
    sums.upa.step()

    sums.mid.step()
    sums.fin.step()
    sums.stem.step()
    sums.bota.step()
    sums.low.step()
    sums.early.step()
    sums.upb.step()
    sums.botb.step()
    sums.upa.step()
    sums.mid.step()
    sums.fin.step()
    sums.bota.step()
    sums.low.step()
    sums.upa.step()
    sums.upb.step()
    sums.botb.step()
    sums.stem.step()
    sums.mid.step()
    sums.fin.step()
    sums.bota.step()
    sums.upb.step()
    sums.botb.step()
    sums.stem.step()
    sums.mid.step()
    sums.bota.step()
    sums.fin.step()
    sums.early.step()
    sums.stem.step()
    sums.botb.step()
    sums.bota.step()
    sums.mid.step()
    sums.botb.step()
    for item in sums.values():
        item.finish()
    for item in halo.values():
        item.finish()


def unpack_kernel(cfg, back, *refs):
    (f0, f1, f2, lanes, scales) = cfg
    ref = back(iter(refs))
    stores = []

    def send(source, target):
        copy = pltpu.make_async_copy(source, target, ref.store.at[len(stores)])
        copy.start()
        stores.append(copy)

    def side(source, base, rows, width, scale):
        count = blocks(width, lanes)
        value = [source[base + j * rows : base + (j + 1) * rows].astype(F32) * scale for j in range(count)]
        return jnp.concatenate(value, axis=1)

    send(ref.ins.output, ref.outs.output)
    ref.ready.half[...] = ref.ins.half[:, : lanes // 2]
    send(ref.ready.half, ref.outs.half)
    ref.ready.bot[: 16 * f1] = side(ref.ins.bota, 0, 16 * f1, f2, scales.bot)[:, :f2]
    ref.ready.bot[16 * f1 :] = side(ref.ins.botb, 0, 11 * f1, f2, scales.bot)[:, :f2]
    send(ref.ready.bot, ref.outs.bot)
    low = side(ref.ins.low, 0, f1, 27 * f1, scales.rise)
    first = split_at(blocks(27 * f2, lanes))
    up = [side(ref.ins.upa, 0, f1, first * lanes, scales.rise)]
    up.append(side(ref.ins.upb, 0, f1, 27 * f2 - first * lanes, scales.rise))
    up = jnp.concatenate(up, axis=1)
    for k in range(27):
        ref.ready.rise[k] = jnp.concatenate([up[:, k * f2 : (k + 1) * f2], low[:, k * f1 : (k + 1) * f1]], axis=1)
    send(ref.ready.rise, ref.outs.rise)
    up = side(ref.ins.fin, 0, 3 * f0, 9 * f1, scales.fin)
    low = side(ref.ins.early, 0, 3 * f0, 9 * f0, scales.fin)
    for k in range(27):
        at_, rows = k // 3, slice((k % 3) * f0, (k % 3 + 1) * f0)
        ref.ready.fin[k] = jnp.concatenate([up[rows, at_ * f1 : (at_ + 1) * f1], low[rows, at_ * f0 : (at_ + 1) * f0]], axis=1)
    send(ref.ready.fin, ref.outs.fin)
    for source, target, out, scale in (
        (ref.ins.mid, ref.ready.mid, ref.outs.mid, scales.mid),
        (ref.ins.stem, ref.ready.stem, ref.outs.stem, scales.stem),
    ):
        width = target.shape[1]
        for j in range(blocks(27 * f0, lanes)):
            value = (source[j * width : (j + 1) * width].astype(F32) * scale).T
            rows = min(lanes, 27 * f0 - j * lanes)
            target[j * lanes : j * lanes + rows] = value[:rows]
        send(target, out)
    for copy in stores:
        copy.wait()


def local(features, cotangent, w_stem, w_middle, w_bottom, w_rise, w_final):
    f0, w, d, h = features.shape
    f1, f2 = w_middle.shape[4], w_bottom.shape[4]
    f = (f0, f1, f2)
    spans = {0: (w, d), 1: (w // 2, d // 2), 2: (w // 4, d // 4)}
    near = neighbours()
    sets = 1 + max(group for _, _, group in HALOS.values())
    flat = w * d * f0
    inputs = dict(
        feat=features.reshape(flat, h),
        cot=cotangent.reshape(flat, h),
        stem=w_stem.reshape(27, f0, f0),
        fin=w_final.transpose(0, 1, 2, 4, 3).reshape(27, f0, f1 + f0),
        mid=w_middle.reshape(27, f0, f1),
        bot=w_bottom.reshape(27, f1, f2),
        rise=w_rise.transpose(0, 1, 2, 4, 3).reshape(27, f1, f2 + f1),
    )
    outs = dict(output=jax.ShapeDtypeStruct((flat, h), BF), half=jax.ShapeDtypeStruct((flat // 4, h), F32))
    halos, sums = {}, {}
    for name, (c, level, _) in HALOS.items():
        a, b = spans[level]
        tall = edge_rows(f[c], a * b, h)
        halos[name] = dict(
            rows=pltpu.VMEM((a + 2, b + 2, f[c], h), BF),
            edges=pltpu.VMEM((2, 3, 3, tall, h), BF),
            own=pltpu.VMEM((tall, h), BF),
        )
        fold = lane_parts(f[c], tall, h >> level, h)
        if fold > 1:
            halos[name][0] = pltpu.VMEM((a + 2, b + 2, f[c] // fold, h), BF)
    place = segments(f, h)
    for name, order in orders().items():
        unit = TILE * members(GROUP)
        rows = -(-sum(a * b for a, b in place[name]) // unit) * unit
        outs[name] = jax.ShapeDtypeStruct((rows, h), BF)
        levels = {}
        for i, axes in enumerate(order):
            for j, kind in enumerate((F32, BF, BF)):
                levels[3 * i + j] = pltpu.VMEM((rows, h), kind)
            rows //= members(axes)
        sums[name] = dict(levels=levels, send=pltpu.SemaphoreType.DMA((1,)), recv=pltpu.SemaphoreType.DMA((2 * len(order),)))

    def cells_of(c, level, kind=F32):
        return pltpu.VMEM((*spans[level], c, h), kind)

    def taps(a, b):
        return pltpu.VMEM((a, 27 * b), BF)

    scratch = dict(
        send=pltpu.SemaphoreType.DMA((blocks(sets, 2) * near,)),
        recv=pltpu.SemaphoreType.DMA((sets * near,)),
        load=pltpu.SemaphoreType.DMA((len(inputs),)),
        inside={name: pltpu.VMEM(v.shape, BF) for name, v in inputs.items()},
        halos=halos,
        sums=sums,
        stacks={
            name: pltpu.VMEM((spans[level][0] + 2, spans[level][1] + 2, 3 * f[c], h), BF)
            for name, (c, level) in STACKS.items()
        },
        stem_pre=cells_of(f0, 0), mid_pre=cells_of(f1, 1), deep_pre=cells_of(f2, 2), rise_pre=cells_of(f1, 1),
        fb_pool=cells_of(f1, 1), fb_skip=cells_of(f0, 0), rb_skip=cells_of(f1, 1), fin_part=cells_of(f0, 0),
        stem_grad=cells_of(f0, 0, BF),
        wide=pltpu.VMEM((flat, h), F32), half_wide=pltpu.VMEM((flat // 4, h), F32),
        w_stem=taps(f0, f0), w_mid=taps(f1, f0), w_bot=taps(f2, f1), w_rise_up=taps(f1, f2), w_rise_low=taps(f1, f1),
        w_fin_up=taps(f0, f1), w_fin_low=taps(f0, f0), b_mid=taps(f0, f1), b_bot=taps(f1, f2),
        b_rise=taps(f2 + f1, f1), b_fin=taps(f1 + f0, f0),
    )
    vmem = pl.BlockSpec(memory_space=pltpu.VMEM)
    anywhere = pl.BlockSpec(memory_space=pl.ANY)
    leaves, back = spread_out(dict(ins=inputs, outs=outs, **scratch))
    done = pl.pallas_call(
        functools.partial(step_kernel, (f0, f1, f2, w, d, h), back),
        out_shape=tuple(outs.values()),
        in_specs=[anywhere] * len(inputs),
        out_specs=(vmem,) * len(outs),
        scratch_shapes=leaves[len(inputs) + len(outs) :],
        compiler_params=pltpu.CompilerParams(collective_id=0, has_side_effects=True, vmem_limit_bytes=58 << 20),
        name="unet_step",
    )(*[pltpu.with_memory_space_constraint(v, pltpu.HBM) for v in inputs.values()])
    packed = dict(zip(outs, done))
    cells = w * d * h * members(GROUP)
    fine, mid, deep = (1.0 / math.sqrt(cells / k) for k in (1.0, 8.0, 64.0))
    scales = Names(stem=fine, mid=mid, bot=deep, rise=mid, fin=fine)

    results = dict(
        output=jax.ShapeDtypeStruct((flat, h), BF),
        stem=jax.ShapeDtypeStruct((27 * f0, f0), F32),
        mid=jax.ShapeDtypeStruct((27 * f0, f1), F32),
        bot=jax.ShapeDtypeStruct((27 * f1, f2), F32),
        rise=jax.ShapeDtypeStruct((27, f1, f2 + f1), F32),
        fin=jax.ShapeDtypeStruct((27, f0, f1 + f0), F32),
        half=jax.ShapeDtypeStruct((flat // 4, h // 2), F32),
    )
    hold = dict(
        ready={n: pltpu.VMEM(v.shape, v.dtype) for n, v in results.items()},
        store=pltpu.SemaphoreType.DMA((len(results),)),
    )
    leaves, back = spread_out(dict(ins=packed, outs=results, **hold))
    final = pl.pallas_call(
        functools.partial(unpack_kernel, (f0, f1, f2, h, scales), back),
        out_shape=tuple(results.values()),
        in_specs=[vmem] * len(packed),
        out_specs=(anywhere,) * len(results),
        scratch_shapes=leaves[len(packed) + len(results) :],
        compiler_params=pltpu.CompilerParams(vmem_limit_bytes=46 << 20),
        name="unpack",
    )(*packed.values())
    final = Names(zip(results, final))
    return (
        final.output.reshape(f0, w, d, h),
        final.stem.reshape(w_stem.shape),
        final.mid.reshape(w_middle.shape),
        final.bot.reshape(w_bottom.shape),
        final.rise.reshape(3, 3, 3, f1, f2 + f1).transpose(0, 1, 2, 4, 3),
        final.fin.reshape(3, 3, 3, f0, f1 + f0).transpose(0, 1, 2, 4, 3),
        final.half.reshape(f0, w // 2, d // 2, h // 2),
    )


def solution(mesh):
    placed = (P("grp", "wid", "dep", "hgt"), P("grp", "wid", "dep", "hgt"), P(), P(), P(), P(), P())
    grad = P("grp", None, None, None, None)
    return jax.shard_map(
        local,
        mesh=mesh,
        in_specs=placed,
        out_specs=(P("grp", "wid", "dep", "hgt"), grad, grad, grad, grad, grad, P("grp", "wid", "dep", "hgt")),
        check_vma=False,
    )
```

```python
import functools
import math

import jax
import jax.numpy as jnp
from jax import lax
from jax.experimental import pallas as pl
from jax.experimental.pallas import tpu as pltpu
from jax.sharding import PartitionSpec as P

BF, F32 = jnp.bfloat16, jnp.float32
AXES = ("grp", "dep", "hgt", "wid")
GROUP = ("wid", "hgt", "dep")
TILE = 16


class Names(dict):
    __getattr__ = dict.__getitem__


def spread_out(tree):
    if not isinstance(tree, dict):
        return [tree], lambda leaves: next(leaves)
    parts = {k: spread_out(v) for k, v in tree.items()}
    leaves = [leaf for some, _ in parts.values() for leaf in some]
    return leaves, lambda leaves: Names({k: back(leaves) for k, (_, back) in parts.items()})


def mm(a, b):
    return lax.dot_general(a, b, (((1,), (0,)), ((), ())), preferred_element_type=F32)


def mm_nt(a, b):
    return lax.dot_general(a, b, (((1,), (1,)), ((), ())), preferred_element_type=F32)


def mm_split(a, b):
    high = a.astype(BF)
    low = (a - high.astype(F32)).astype(BF)
    return mm(high, b) + mm(low, b)


def silu(v):
    return v * jax.nn.sigmoid(v)


def slope(v):
    g = jax.nn.sigmoid(v)
    return g * (1.0 + v * (1.0 - g))


def pattern(lanes, test):
    row = lax.broadcasted_iota(jnp.int32, (lanes, lanes), 0)
    col = lax.broadcasted_iota(jnp.int32, (lanes, lanes), 1)
    return jnp.where(test(row, col), 1.0, 0.0)


def neighbours():
    count = 1
    for name in GROUP:
        count *= min(lax.axis_size(name), 3)
    return count - 1


def edge_rows(channels, rows, lanes):
    size = TILE
    while channels % size or rows * (channels // size) > lanes // 2:
        size += TILE
    return size


def lane_parts(channels, tall, h, lanes):
    count = lanes // h
    while channels % (tall * count):
        count -= 1
    return count


class Halo:
    def __init__(self, group, rows, packed, edges, own, span, sems):
        self.rows, self.edges, self.own = rows, edges, own
        self.packed = packed
        self.fold = rows.shape[2] // packed.shape[2]
        self.base, self.sent_base = group * neighbours(), group // 2 * neighbours()
        self.w, self.d, self.h = span
        self.send, self.recv = sems
        self.before = None
        self.unsent = False
        self.side = own.shape[1] // 2
        self.tall = own.shape[0]
        self.per = rows.shape[2] // self.tall

    def outer(self, a, b):
        return a in (0, self.w + 1) or b in (0, self.d + 1)

    def clear(self):
        moving = self.rows if self.fold == 1 else self.packed
        blank = jnp.zeros(moving.shape[2:], BF)
        for a in range(self.w + 2):
            for b in range(self.d + 2):
                if self.outer(a, b):
                    moving[a, b] = blank
        self.edges[...] = jnp.zeros(self.edges.shape, BF)

    def fill_edges(self):
        lane = lax.broadcasted_iota(jnp.int32, self.own.shape, 1)
        tile = jnp.zeros(self.own.shape, F32)
        for a in range(self.w):
            for b in range(self.d):
                row = self.rows[a + 1, b + 1].astype(F32)
                for g in range(self.per):
                    r = (a * self.d + b) * self.per + g
                    part_of = row[g * self.tall : (g + 1) * self.tall]
                    tile = jnp.where(lane == r, part_of[:, 0:1], tile)
                    tile = jnp.where(lane == self.side + r, part_of[:, self.h - 1 : self.h], tile)
        self.own[...] = tile.astype(BF)

    def pack(self):
        tall = self.packed.shape[2]
        for a in range(1, self.w + 1):
            for b in range(1, self.d + 1):
                wide = self.rows[a, b].astype(F32)
                total = wide[:tall]
                for g in range(1, self.fold):
                    total = total + pltpu.roll(wide[g * tall : (g + 1) * tall], g * self.h, 1)
                self.packed[a, b] = total.astype(BF)

    def copies(self):
        moving = self.rows if self.fold == 1 else self.packed
        place = {name: lax.axis_index(name) for name in AXES}
        size = {name: lax.axis_size(name) for name in AXES}

        def choices(name):
            i, n = place[name], size[name]
            if n == 1:
                return [(0, 0, True, True)]
            if n == 2:
                return [(0, 0, True, True), (1, 1 - 2 * i, True, True)]
            return [(0, 0, True, True), (1, 1, i < n - 1, i > 0), (2, -1, i > 0, i < n - 1)]

        def cells(step, code, count):
            if code == 0:
                return pl.ds(1, count), pl.ds(1, count)
            up = (1 + step) // 2
            return pl.ds(1 + (count - 1) * up, 1), pl.ds((count + 1) * (1 - up), 1)

        out = []
        for cw, sw, ow, iw in choices("wid"):
            for cd, sd, od, id_ in choices("dep"):
                for ch, sh, oh, ih in choices("hgt"):
                    if cw == 0 and cd == 0 and ch == 0:
                        continue
                    slot = self.base + len(out)
                    target = {"wid": place["wid"] + sw, "dep": place["dep"] + sd, "hgt": place["hgt"] + sh}
                    if ch == 0:
                        from_w, to_w = cells(sw, cw, self.w)
                        from_d, to_d = cells(sd, cd, self.d)
                        source = moving.at[from_w, from_d]
                        dest = moving.at[to_w, to_d]
                    else:
                        source = self.own
                        dest = self.edges.at[(1 - sh) // 2, 1 - sw, 1 - sd]
                    copy = pltpu.make_async_remote_copy(
                        src_ref=source,
                        dst_ref=dest,
                        send_sem=self.send.at[self.sent_base + len(out)],
                        recv_sem=self.recv.at[slot],
                        device_id=target,
                        device_id_type=pl.DeviceIdType.MESH,
                    )
                    steps = 2 * (cd > 0) + 2 * (ch > 0) + (cw > 0)
                    out.append((copy, [c for c in (ow, od, oh) if c is not True], [c for c in (iw, id_, ih) if c is not True], steps))
        return out

    @staticmethod
    def guarded(conditions, action):
        if not conditions:
            action()
        else:
            pl.when(functools.reduce(jnp.logical_and, conditions))(action)

    def start(self):
        if self.before is not None:
            self.before.finish()
        self.fill_edges()
        if self.fold > 1:
            self.pack()
        for copy, can_send, _, _ in sorted(self.copies(), key=lambda entry: -entry[3]):
            self.guarded(can_send, copy.start)
        self.unsent = True

    def wait(self):
        for copy, _, can_take, _ in self.copies():
            self.guarded(can_take, copy.wait_recv)

    def finish(self):
        if self.unsent:
            for copy, can_send, _, _ in self.copies():
                self.guarded(can_send, copy.wait_send)
        self.unsent = False

    def shifted(self, a, b, spread=None):
        lanes = self.own.shape[1]
        h = self.h if spread is None else 2 * self.h
        folded = self.fold > 1 and self.outer(a, b)
        tall = self.packed.shape[2] if folded else self.rows.shape[2]
        row = self.packed[a, b] if folded else self.rows[a, b]
        if spread is not None:
            pieces = [mm(row, spread[g]) for g in range(self.fold if folded else 1)]
            wide = pieces[0] if len(pieces) == 1 else jnp.concatenate(pieces, axis=0)
            row = wide.astype(BF)
            folded = False
        else:
            wide = row.astype(F32)
        dw = 0 if a == 0 else 2 if a == self.w + 1 else 1
        dd = 0 if b == 0 else 2 if b == self.d + 1 else 1
        r = ((self.w - 1, a - 1, 0)[dw] * self.d + (self.d - 1, b - 1, 0)[dd]) * self.per
        lane = lax.broadcasted_iota(jnp.int32, (self.tall, lanes), 1)
        low, high = self.edges[0, dw, dd].astype(F32), self.edges[1, dw, dd].astype(F32)
        befores, centres, afters = [], [], []
        for g in range(self.per):
            turn, from_row = divmod(g * self.tall, tall) if folded else (0, g * self.tall)
            here = wide[from_row : from_row + self.tall]
            left = low[:, self.side + r + g : self.side + r + g + 1]
            right = high[:, r + g : r + g + 1]
            before = jnp.where(lane == 0, left, pltpu.roll(here, (lanes + 1 - turn * h) % lanes, 1))
            after = jnp.where(lane == h - 1, right, pltpu.roll(here, lanes - 1 - turn * h, 1))
            if h < lanes:
                before = jnp.where(lane < h, before, 0.0)
                after = jnp.where(lane < h, after, 0.0)
            befores.append(before.astype(BF))
            afters.append(after.astype(BF))
            if folded:
                centre = pltpu.roll(here, lanes - turn * h, 1) if turn else here
                centres.append(jnp.where(lane < h, centre, 0.0).astype(BF))
        if folded:
            row = jnp.concatenate(centres, axis=0)
        return jnp.concatenate(befores, axis=0), row, jnp.concatenate(afters, axis=0)


def part(i, m):
    return pl.ds(pl.multiple_of(i * m, TILE), m)


def axis_part(axis):
    return (axis, 1, lax.axis_size(axis)) if isinstance(axis, str) else axis


def members(axes):
    return math.prod(axis_part(axis)[2] for axis in axes)


def position(axes):
    place, count = 0, 1
    for axis in axes:
        name, stride, n = axis_part(axis)
        index = lax.axis_index(name)
        if (stride, n) != (1, lax.axis_size(name)):
            index = lax.rem(lax.div(index, stride), n)
        place = place * n + index
        count *= n
    return place, count


def device_at(axes, place):
    where = {name: lax.axis_index(name) for name in GROUP}
    for axis in axes[::-1]:
        name, stride, n = axis_part(axis)
        to = place if axis == axes[0] else lax.rem(place, n)
        if n == lax.axis_size(name):
            where[name] = to
        else:
            where[name] = where[name] + (to - lax.rem(lax.div(where[name], stride), n)) * stride
        place = lax.div(place, n)
    return where


class Summed:
    def __init__(self, order, full, buffers, send, recv):
        self.order, self.full = order, full
        self.levels = [buffers[3 * i : 3 * i + 3] for i in range(len(order))]
        self.total = buffers[0]
        self.send, self.recv = send, recv
        self.stage, self.open, self.last = 0, None, None

    def copy(self, stage, axes, source, dest, to):
        return pltpu.make_async_remote_copy(
            src_ref=source,
            dst_ref=dest,
            send_sem=self.send.at[0],
            recv_sem=self.recv.at[stage],
            device_id=device_at(axes, to),
            device_id_type=pl.DeviceIdType.MESH,
        )

    def exchange(self, stage, axes, pieces, whole, m):
        i, n = position(axes)
        if n == 1:
            return
        self.settle()
        for k in sorted(range(1, n), key=lambda k: -min(k, n - k)):
            to = lax.rem(i + k, n)
            source, dest = pieces(to, i)
            self.copy(stage, axes, source, dest, to).start()
        every = whole.at[pl.ds(0, (n - 1) * m)]
        self.open = self.copy(stage, axes, every, every, lax.rem(i + 1, n))
        self.last = self.open

    def settle(self):
        if self.last is not None:
            self.last.wait_send()
            self.last = None

    def step(self):
        stage, deep = self.stage, len(self.order)
        self.stage += 1
        if self.open is not None:
            self.open.wait_recv()
            self.open = None
        if 0 < stage <= deep:
            i, n = position(self.order[stage - 1])
            held, _, came = self.levels[stage - 1]
            m = held.shape[0] // n
            value = held[part(i, m)]
            for k in range(1, n):
                value = value + came[part(lax.rem(i + k, n), m)].astype(F32)
            if stage < deep:
                self.levels[stage][0][...] = value
            else:
                place, _ = position([axis for axes in self.order for axis in axes])
                self.full[part(place, m)] = value.astype(BF)
        if stage < deep:
            held, wire, came = self.levels[stage]
            i, n = position(self.order[stage])
            m = held.shape[0] // n
            for k in range(1, n):
                there = part(lax.rem(i + k, n), m)
                wire[there] = held[there].astype(BF)
            self.exchange(stage, self.order[stage], lambda to, me: (wire.at[part(to, m)], came.at[part(me, m)]), came, m)
        elif stage < 2 * deep:
            depth = 2 * deep - stage
            place, count = position([axis for axes in self.order[:depth] for axis in axes])
            m = self.full.shape[0] // count
            piece = self.full.at[part(place, m)]
            self.exchange(stage, self.order[depth - 1], lambda to, me: (piece, piece), self.full, m)

    def finish(self):
        while self.stage <= 2 * len(self.order):
            self.step()
        self.settle()


HALOS = dict(
    feat=(0, 0, 0), half=(0, 1, 1), quarter=(1, 2, 0), deep=(2, 2, 1), rg=(1, 1, 0), dg=(2, 2, 1),
    mg=(1, 1, 0), cot=(0, 0, 2), stem=(0, 0, 3), mid=(1, 1, 2), ra=(1, 1, 3),
)
STACKS = dict(
    feat=(0, 0), cot=(0, 0), half=(0, 1), quarter=(1, 2), up2=(2, 1), mid=(1, 1), up1=(1, 0),
    stem=(0, 0), rg=(1, 1), dg=(2, 2), mg=(1, 1),
)


def blocks(size, lanes):
    return -(-size // lanes)


def split_at(count):
    return count * 4 // 9


def segments(f, lanes):
    f0, f1, f2 = f
    return dict(
        low=[(f1, blocks(27 * f1, lanes))],
        upa=[(f1, split_at(blocks(27 * f2, lanes)))],
        upb=[(f1, blocks(27 * f2, lanes) - split_at(blocks(27 * f2, lanes)))],
        bota=[(16 * f1, blocks(f2, lanes))],
        botb=[(11 * f1, blocks(f2, lanes))],
        early=[(3 * f0, blocks(9 * f0, lanes))],
        fin=[(3 * f0, blocks(9 * f1, lanes))],
        mid=[(f1, blocks(27 * f0, lanes))],
        stem=[(f0, blocks(27 * f0, lanes))],
    )


STAGED = (("wid",), ("hgt",), ("dep",))


def orders():
    near = (GROUP[:1], GROUP[1:]) if members(GROUP) <= 16 else STAGED
    n = lax.axis_size("dep")
    one, swap = ((GROUP,) if members(GROUP) <= 16 else STAGED), (STAGED[0], STAGED[2], STAGED[1])
    pairs = (*STAGED[:2], (("dep", 1, 2),), (("dep", 2, n // 2),)) if n % 2 == 0 else STAGED
    return dict(low=STAGED, upa=STAGED, upb=STAGED, bota=pairs, botb=pairs, early=STAGED, fin=STAGED, mid=STAGED, stem=near)


def step_kernel(cfg, back, *refs):
    (f0, f1, f2, w, d, h) = cfg
    ref = back(iter(refs))
    spans = {0: (w, d, h), 1: (w // 2, d // 2, h // 2), 2: (w // 4, d // 4, h // 4)}
    lanes = h
    halo = Names()
    last = {}
    for name, (_, level, group) in HALOS.items():
        own = ref.halos[name]
        halo[name] = Halo(group, own.rows, own.get(0, own.rows), own.edges, own.own, spans[level], (ref.send, ref.recv))
        halo[name].before = last.get(group // 2)
        last[group // 2] = halo[name]
    stacks = ref.stacks
    sums = Names()
    for name, order in orders().items():
        own = ref.sums[name]
        sums[name] = Summed(order, ref.outs[name], list(own.levels.values()), own.send, own.recv)

    loads = Names()
    for i, name in enumerate(ref.ins):
        loads[name] = pltpu.make_async_copy(ref.ins[name], ref.inside[name], ref.load.at[i])
        loads[name].start()
    halo.feat.clear()
    halo.cot.clear()

    def take(load, source, item):
        load.wait()
        ref.wide[...] = source[...].astype(F32)
        for a in range(w):
            for b in range(d):
                item.rows[a + 1, b + 1] = ref.wide[pl.ds(a * d + b, f0, stride=w * d), :].astype(BF)

    barrier = pltpu.get_barrier_semaphore()
    me, everyone = position(GROUP)
    for k in range(1, everyone):
        pl.semaphore_signal(
            barrier, 1, device_id=device_at(GROUP, lax.rem(me + k, everyone)), device_id_type=pl.DeviceIdType.MESH
        )
    take(loads.feat, ref.inside.feat, halo.feat)
    halo.half.clear()
    halo.stem.clear()
    pl.semaphore_wait(barrier, everyone - 1)

    halo.feat.start()
    take(loads.cot, ref.inside.cot, halo.cot)
    halo.cot.start()
    for item in (halo.quarter, halo.deep, halo.rg, halo.dg, halo.mg, halo.mid, halo.ra):
        item.clear()
    pool = pattern(lanes, lambda r, c: r // 2 == c)
    pool_mean = (pool / 8.0).astype(BF)
    pool_sum = pool.astype(BF)
    spread = pattern(lanes, lambda r, c: c // 2 == r)
    spread_mean = (spread / 8.0).astype(BF)

    def spreads(item):
        full = 2 * item.h
        each = [pattern(lanes, lambda r, c: (c < full) & (c // 2 == r - g * item.h)) for g in range(item.fold)]
        return [v.astype(BF) for v in each]

    def forward(raw, target):
        target[...] = raw[...].reshape(-1, raw.shape[2]).T

    def side_by_side(raw, target, low, high):
        width = high - low
        for k in range(raw.shape[0]):
            target[:, k * width : (k + 1) * width] = raw[k][:, low:high]

    loads.stem.wait()
    forward(ref.inside.stem, ref.w_stem)
    loads.fin.wait()
    forward(ref.inside.fin, ref.b_fin)
    side_by_side(ref.inside.fin, ref.w_fin_up, 0, f1)
    side_by_side(ref.inside.fin, ref.w_fin_low, f1, f1 + f0)
    loads.mid.wait()
    forward(ref.inside.mid, ref.w_mid)
    side_by_side(ref.inside.mid, ref.b_mid, 0, f1)
    loads.bot.wait()
    forward(ref.inside.bot, ref.w_bot)
    side_by_side(ref.inside.bot, ref.b_bot, 0, f2)
    loads.rise.wait()
    forward(ref.inside.rise, ref.b_rise)
    side_by_side(ref.inside.rise, ref.w_rise_up, 0, f2)
    side_by_side(ref.inside.rise, ref.w_rise_low, f2, f2 + f1)

    def stack(item, target, back=False):
        for a in range(item.w + 2):
            for b in range(item.d + 2):
                parts = item.shifted(a, b)
                target[a, b] = jnp.concatenate(parts[::-1] if back else parts, axis=0)

    def stack_up(up, target):
        spread = spreads(up)
        for i in range(up.w + 2):
            for j in range(up.d + 2):
                value = jnp.concatenate(up.shifted(i, j, spread), axis=0)
                for a in range(max(2 * i - 1, 0), min(2 * i + 1, target.shape[0])):
                    for b in range(max(2 * j - 1, 0), min(2 * j + 1, target.shape[1])):
                        target[a, b] = value

    def patch(source, a, b, pair, back=False, middle=False):
        third = source.shape[2] // 3
        rows = slice(third, 2 * third) if middle else slice(0, 3 * third)
        parts = []
        for q in range(pair):
            taps = [(ka, kb) for ka in range(3) for kb in range(3)]
            parts.append(
                jnp.concatenate([source[a + ka, b + kb + q, rows] for ka, kb in (taps[::-1] if back else taps)], axis=0)
            )
        return parts[0] if pair == 1 else jnp.concatenate(parts, axis=1)

    def over_rows(span, body):
        pair = 4 if span[1] % 4 == 0 else 2 if span[1] % 2 == 0 else 1
        across = span[1] // pair

        def trip(i, _):
            body(i // across, (i % across) * pair, pair)
            return 0

        count = span[0] * across
        if count <= 2:
            for i in range(count):
                trip(i, 0)
        else:
            lax.fori_loop(0, count, trip, 0)

    def conv(source, weight, span, store, back=False):
        def body(a, b, pair):
            result = mm(weight[...], patch(source, a, b, pair, back))
            for q in range(pair):
                store(a, b + q, result[:, q * lanes : (q + 1) * lanes])

        over_rows(span, body)

    def put_blocks(where, base, value):
        rows, width = value.shape
        count = blocks(width, lanes)
        if count * lanes > width:
            value = jnp.concatenate([value, jnp.zeros((rows, count * lanes - width), value.dtype)], axis=1)
        for j in range(count):
            where[base + j * rows : base + (j + 1) * rows] = value[:, j * lanes : (j + 1) * lanes]

    def beside(span, pick):
        return jnp.concatenate([pick(a, b) for a in range(span[0]) for b in range(span[1])], axis=1)

    halo.feat.wait()
    stack(halo.feat, stacks.feat)

    def stem_store(a, b, value):
        ref.stem_pre[a, b] = value
        halo.stem.rows[a + 1, b + 1] = silu(value).astype(BF)

    conv(stacks.feat, ref.w_stem, spans[0], stem_store)

    def pooled(fine, coarse):
        low, up = fine, coarse
        for a in range(up.w):
            for b in range(up.d):
                cat = [low.rows[2 * a + 1 + i, 2 * b + 1 + j] for i in range(2) for j in range(2)]
                total = mm(cat[0], pool_mean) + mm(cat[1], pool_mean) + mm(cat[2], pool_mean) + mm(cat[3], pool_mean)
                up.rows[a + 1, b + 1] = total.astype(BF)

    pooled(halo.stem, halo.half)
    halo.cot.wait()
    halo.half.start()
    halo.stem.start()
    stack(halo.cot, stacks.cot, back=True)
    ref.fb_pool[...] = jnp.zeros(ref.fb_pool.shape, F32)

    def back_store(a, b, value):
        ref.fb_pool[a // 2, b // 2] += value[:f1]
        ref.fb_skip[a, b] = value[f1:]

    conv(stacks.cot, ref.b_fin, spans[0], back_store, back=True)
    for a in range(spans[1][0]):
        for b in range(spans[1][1]):
            ref.fb_pool[a, b] = mm_split(ref.fb_pool[a, b], pool_sum)
    halo.half.wait()
    stack(halo.half, stacks.half)

    def mid_store(a, b, value):
        ref.mid_pre[a, b] = value
        halo.mid.rows[a + 1, b + 1] = silu(value).astype(BF)

    conv(stacks.half, ref.w_mid, spans[1], mid_store)
    pooled(halo.mid, halo.quarter)
    halo.quarter.start()
    halo.mid.start()
    halo.stem.wait()
    stack(halo.stem, stacks.stem)

    def final_low(a, b, value):
        ref.fin_part[a, b] = value

    conv(stacks.stem, ref.w_fin_low, spans[0], final_low)
    cot_cells = lambda: beside(spans[0], lambda a, b: stacks.cot[a + 1, b + 1])
    low_cells = beside(spans[0], lambda a, b: patch(stacks.stem, a, b, 1, middle=True))
    put_blocks(sums.early.total, 0, mm_nt(cot_cells(), low_cells))
    sums.early.step()
    halo.quarter.wait()
    stack(halo.quarter, stacks.quarter)

    def deep_store(a, b, value):
        ref.deep_pre[a, b] = value
        halo.deep.rows[a + 1, b + 1] = silu(value).astype(BF)

    conv(stacks.quarter, ref.w_bot, spans[2], deep_store)
    halo.deep.start()
    halo.mid.wait()
    stack(halo.mid, stacks.mid)

    def rise_low(a, b, value):
        ref.rise_pre[a, b] = value

    conv(stacks.mid, ref.w_rise_low, spans[1], rise_low)
    sums.early.step()
    for held in (ref.stem_pre, ref.mid_pre, ref.deep_pre):
        for a in range(held.shape[0]):
            for b in range(held.shape[1]):
                held[a, b] = slope(held[a, b])
    halo.deep.wait()
    stack_up(halo.deep, stacks.up2)

    def rise_store(a, b, value):
        value = value + ref.rise_pre[a, b]
        halo.ra.rows[a + 1, b + 1] = silu(value).astype(BF)
        grad = ref.fb_pool[a, b] * slope(value)
        halo.rg.rows[a + 1, b + 1] = grad.astype(BF)

    conv(stacks.up2, ref.w_rise_up, spans[1], rise_store)
    halo.rg.start()
    halo.ra.start()
    sums.early.step()

    grad1 = lambda item: beside(spans[1], lambda a, b: item.rows[a + 1, b + 1])

    def wide_wgrad(segment, grad, source, span, low=None, high=None):
        cells = beside(span, lambda a, b: patch(source, a, b, 1)[low:high])
        put_blocks(segment.total, 0, mm_nt(grad, cells))

    wide_wgrad(sums.low, grad1(halo.rg), stacks.mid, spans[1])
    sums.low.step()
    cut = split_at(blocks(27 * f2, lanes)) * lanes
    wide_wgrad(sums.upa, grad1(halo.rg), stacks.up2, spans[1], None, cut)
    sums.upa.step()
    wide_wgrad(sums.upb, grad1(halo.rg), stacks.up2, spans[1], cut, None)
    sums.low.step()
    sums.upb.step()
    sums.upa.step()
    halo.rg.wait()
    stack(halo.rg, stacks.rg, back=True)
    deep_sum = [[None] * spans[2][1] for _ in range(spans[2][0])]
    pair1 = 2 if spans[1][1] % 2 == 0 else 1
    for a in range(spans[1][0]):
        for b in range(0, spans[1][1], pair1):
            result = mm(ref.b_rise[...], patch(stacks.rg, a, b, pair1, back=True))
            for q in range(pair1):
                value = result[:, q * lanes : (q + 1) * lanes]
                ref.rb_skip[a, b + q] = value[f2:]
                ap, bt = a // 2, (b + q) // 2
                old = deep_sum[ap][bt]
                deep_sum[ap][bt] = value[:f2] if old is None else old + value[:f2]
    for a in range(spans[2][0]):
        for b in range(spans[2][1]):
            grad = mm_split(deep_sum[a][b], pool_sum) * ref.deep_pre[a, b]
            halo.dg.rows[a + 1, b + 1] = grad.astype(BF)
    halo.dg.start()
    sums.upb.step()
    cells2 = beside(spans[2], lambda a, b: patch(stacks.quarter, a, b, 1))
    grad2 = beside(spans[2], lambda a, b: halo.dg.rows[a + 1, b + 1])
    bot = mm_nt(cells2, grad2)
    put_blocks(sums.bota.total, 0, bot[: 16 * f1])
    put_blocks(sums.botb.total, 0, bot[16 * f1 :])
    sums.bota.step()
    sums.botb.step()
    sums.early.step()
    halo.ra.wait()
    stack_up(halo.ra, stacks.up1)
    sums.low.step()
    up_cells = beside(spans[0], lambda a, b: patch(stacks.up1, a, b, 1, middle=True))
    put_blocks(sums.fin.total, 0, mm_nt(cot_cells(), up_cells))
    sums.bota.step()
    sums.botb.step()
    sums.upa.step()
    sums.fin.step()
    halo.dg.wait()
    stack(halo.dg, stacks.dg, back=True)

    def quarter_store(a, b, value):
        wide = mm_split(value, spread_mean)
        for i in range(2):
            for j in range(2):
                at_, bt = 2 * a + i, 2 * b + j
                grad = (ref.rb_skip[at_, bt] + wide) * ref.mid_pre[at_, bt]
                halo.mg.rows[at_ + 1, bt + 1] = grad.astype(BF)

    conv(stacks.dg, ref.b_bot, spans[2], quarter_store, back=True)
    halo.mg.start()
    sums.fin.step()
    sums.upb.step()

    def final_row(a):
        result = mm(ref.w_fin_up[...], patch(stacks.up1, a, 0, d))
        for b in range(d):
            value = ref.fin_part[a, b] + result[:, b * lanes : (b + 1) * lanes]
            ref.wide[pl.ds(a * d + b, f0, stride=w * d), :] = value

    wide_wgrad(sums.mid, grad1(halo.mg), stacks.half, spans[1])
    sums.mid.step()
    sums.low.step()
    sums.early.step()
    sums.bota.step()
    final_row(0)
    final_row(1)
    sums.botb.step()
    sums.upa.step()
    final_row(2)
    sums.mid.step()
    final_row(3)
    ref.outs.output[...] = ref.wide[...].astype(BF)
    sums.fin.step()
    halo.mg.wait()
    stack(halo.mg, stacks.mg, back=True)

    def half_store(a, b, value):
        ref.half_wide[pl.ds(a * spans[1][1] + b, f0, stride=spans[1][0] * spans[1][1]), :] = value
        wide = mm_split(value, spread_mean)
        for i in range(2):
            for j in range(2):
                at_, bt = 2 * a + i, 2 * b + j
                grad = (ref.fb_skip[at_, bt] + wide) * ref.stem_pre[at_, bt]
                ref.stem_grad[at_, bt] = grad.astype(BF)

    conv(stacks.mg, ref.b_mid, spans[1], half_store, back=True)
    ref.outs.half[...] = ref.half_wide[...]
    sums.low.step()
    sums.bota.step()
    sums.upb.step()
    wide_wgrad(sums.stem, beside(spans[0], lambda a, b: ref.stem_grad[a, b]), stacks.feat, spans[0])
    sums.stem.step()
    sums.botb.step()
    sums.upa.step()

    sums.mid.step()
    sums.fin.step()
    sums.stem.step()
    sums.bota.step()
    sums.low.step()
    sums.early.step()
    sums.upb.step()
    sums.botb.step()
    sums.upa.step()
    sums.mid.step()
    sums.fin.step()
    sums.bota.step()
    sums.low.step()
    sums.upa.step()
    sums.upb.step()
    sums.botb.step()
    sums.stem.step()
    sums.mid.step()
    sums.fin.step()
    sums.bota.step()
    sums.upb.step()
    sums.botb.step()
    sums.stem.step()
    sums.mid.step()
    sums.bota.step()
    sums.fin.step()
    sums.early.step()
    sums.stem.step()
    sums.botb.step()
    sums.bota.step()
    sums.mid.step()
    sums.botb.step()
    for item in sums.values():
        item.finish()
    for item in halo.values():
        item.finish()


def unpack_kernel(cfg, back, *refs):
    (f0, f1, f2, lanes, scales) = cfg
    ref = back(iter(refs))
    stores = []

    def send(source, target):
        copy = pltpu.make_async_copy(source, target, ref.store.at[len(stores)])
        copy.start()
        stores.append(copy)

    def side(source, base, rows, width, scale):
        count = blocks(width, lanes)
        value = [source[base + j * rows : base + (j + 1) * rows].astype(F32) * scale for j in range(count)]
        return jnp.concatenate(value, axis=1)

    send(ref.ins.output, ref.outs.output)
    ref.ready.half[...] = ref.ins.half[:, : lanes // 2]
    send(ref.ready.half, ref.outs.half)
    ref.ready.bot[: 16 * f1] = side(ref.ins.bota, 0, 16 * f1, f2, scales.bot)[:, :f2]
    ref.ready.bot[16 * f1 :] = side(ref.ins.botb, 0, 11 * f1, f2, scales.bot)[:, :f2]
    send(ref.ready.bot, ref.outs.bot)
    low = side(ref.ins.low, 0, f1, 27 * f1, scales.rise)
    first = split_at(blocks(27 * f2, lanes))
    up = [side(ref.ins.upa, 0, f1, first * lanes, scales.rise)]
    up.append(side(ref.ins.upb, 0, f1, 27 * f2 - first * lanes, scales.rise))
    up = jnp.concatenate(up, axis=1)
    for k in range(27):
        ref.ready.rise[k] = jnp.concatenate([up[:, k * f2 : (k + 1) * f2], low[:, k * f1 : (k + 1) * f1]], axis=1)
    send(ref.ready.rise, ref.outs.rise)
    up = side(ref.ins.fin, 0, 3 * f0, 9 * f1, scales.fin)
    low = side(ref.ins.early, 0, 3 * f0, 9 * f0, scales.fin)
    for k in range(27):
        at_, rows = k // 3, slice((k % 3) * f0, (k % 3 + 1) * f0)
        ref.ready.fin[k] = jnp.concatenate([up[rows, at_ * f1 : (at_ + 1) * f1], low[rows, at_ * f0 : (at_ + 1) * f0]], axis=1)
    send(ref.ready.fin, ref.outs.fin)
    for source, target, out, scale in (
        (ref.ins.mid, ref.ready.mid, ref.outs.mid, scales.mid),
        (ref.ins.stem, ref.ready.stem, ref.outs.stem, scales.stem),
    ):
        width = target.shape[1]
        for j in range(blocks(27 * f0, lanes)):
            value = (source[j * width : (j + 1) * width].astype(F32) * scale).T
            rows = min(lanes, 27 * f0 - j * lanes)
            target[j * lanes : j * lanes + rows] = value[:rows]
        send(target, out)
    for copy in stores:
        copy.wait()


def local(features, cotangent, w_stem, w_middle, w_bottom, w_rise, w_final):
    f0, w, d, h = features.shape
    f1, f2 = w_middle.shape[4], w_bottom.shape[4]
    f = (f0, f1, f2)
    spans = {0: (w, d), 1: (w // 2, d // 2), 2: (w // 4, d // 4)}
    near = neighbours()
    sets = 1 + max(group for _, _, group in HALOS.values())
    flat = w * d * f0
    inputs = dict(
        feat=features.reshape(flat, h),
        cot=cotangent.reshape(flat, h),
        stem=w_stem.reshape(27, f0, f0),
        fin=w_final.transpose(0, 1, 2, 4, 3).reshape(27, f0, f1 + f0),
        mid=w_middle.reshape(27, f0, f1),
        bot=w_bottom.reshape(27, f1, f2),
        rise=w_rise.transpose(0, 1, 2, 4, 3).reshape(27, f1, f2 + f1),
    )
    outs = dict(output=jax.ShapeDtypeStruct((flat, h), BF), half=jax.ShapeDtypeStruct((flat // 4, h), F32))
    halos, sums = {}, {}
    for name, (c, level, _) in HALOS.items():
        a, b = spans[level]
        tall = edge_rows(f[c], a * b, h)
        halos[name] = dict(
            rows=pltpu.VMEM((a + 2, b + 2, f[c], h), BF),
            edges=pltpu.VMEM((2, 3, 3, tall, h), BF),
            own=pltpu.VMEM((tall, h), BF),
        )
        fold = lane_parts(f[c], tall, h >> level, h)
        if fold > 1:
            halos[name][0] = pltpu.VMEM((a + 2, b + 2, f[c] // fold, h), BF)
    place = segments(f, h)
    for name, order in orders().items():
        unit = TILE * members(GROUP)
        rows = -(-sum(a * b for a, b in place[name]) // unit) * unit
        outs[name] = jax.ShapeDtypeStruct((rows, h), BF)
        levels = {}
        for i, axes in enumerate(order):
            for j, kind in enumerate((F32, BF, BF)):
                levels[3 * i + j] = pltpu.VMEM((rows, h), kind)
            rows //= members(axes)
        sums[name] = dict(levels=levels, send=pltpu.SemaphoreType.DMA((1,)), recv=pltpu.SemaphoreType.DMA((2 * len(order),)))

    def cells_of(c, level, kind=F32):
        return pltpu.VMEM((*spans[level], c, h), kind)

    def taps(a, b):
        return pltpu.VMEM((a, 27 * b), BF)

    scratch = dict(
        send=pltpu.SemaphoreType.DMA((blocks(sets, 2) * near,)),
        recv=pltpu.SemaphoreType.DMA((sets * near,)),
        load=pltpu.SemaphoreType.DMA((len(inputs),)),
        inside={name: pltpu.VMEM(v.shape, BF) for name, v in inputs.items()},
        halos=halos,
        sums=sums,
        stacks={
            name: pltpu.VMEM((spans[level][0] + 2, spans[level][1] + 2, 3 * f[c], h), BF)
            for name, (c, level) in STACKS.items()
        },
        stem_pre=cells_of(f0, 0), mid_pre=cells_of(f1, 1), deep_pre=cells_of(f2, 2), rise_pre=cells_of(f1, 1),
        fb_pool=cells_of(f1, 1), fb_skip=cells_of(f0, 0), rb_skip=cells_of(f1, 1), fin_part=cells_of(f0, 0),
        stem_grad=cells_of(f0, 0, BF),
        wide=pltpu.VMEM((flat, h), F32), half_wide=pltpu.VMEM((flat // 4, h), F32),
        w_stem=taps(f0, f0), w_mid=taps(f1, f0), w_bot=taps(f2, f1), w_rise_up=taps(f1, f2), w_rise_low=taps(f1, f1),
        w_fin_up=taps(f0, f1), w_fin_low=taps(f0, f0), b_mid=taps(f0, f1), b_bot=taps(f1, f2),
        b_rise=taps(f2 + f1, f1), b_fin=taps(f1 + f0, f0),
    )
    grant = 46 if members(GROUP) <= 16 else 60
    vmem = pl.BlockSpec(memory_space=pltpu.VMEM)
    anywhere = pl.BlockSpec(memory_space=pl.ANY)
    leaves, back = spread_out(dict(ins=inputs, outs=outs, **scratch))
    done = pl.pallas_call(
        functools.partial(step_kernel, (f0, f1, f2, w, d, h), back),
        out_shape=tuple(outs.values()),
        in_specs=[anywhere] * len(inputs),
        out_specs=(vmem,) * len(outs),
        scratch_shapes=leaves[len(inputs) + len(outs) :],
        compiler_params=pltpu.CompilerParams(collective_id=0, has_side_effects=True, vmem_limit_bytes=grant << 20),
        name="unet_step",
    )(*[pltpu.with_memory_space_constraint(v, pltpu.HBM) for v in inputs.values()])
    packed = dict(zip(outs, done))
    cells = w * d * h * members(GROUP)
    fine, mid, deep = (1.0 / math.sqrt(cells / k) for k in (1.0, 8.0, 64.0))
    scales = Names(stem=fine, mid=mid, bot=deep, rise=mid, fin=fine)

    results = dict(
        output=jax.ShapeDtypeStruct((flat, h), BF),
        stem=jax.ShapeDtypeStruct((27 * f0, f0), F32),
        mid=jax.ShapeDtypeStruct((27 * f0, f1), F32),
        bot=jax.ShapeDtypeStruct((27 * f1, f2), F32),
        rise=jax.ShapeDtypeStruct((27, f1, f2 + f1), F32),
        fin=jax.ShapeDtypeStruct((27, f0, f1 + f0), F32),
        half=jax.ShapeDtypeStruct((flat // 4, h // 2), F32),
    )
    hold = dict(
        ready={n: pltpu.VMEM(v.shape, v.dtype) for n, v in results.items()},
        store=pltpu.SemaphoreType.DMA((len(results),)),
    )
    leaves, back = spread_out(dict(ins=packed, outs=results, **hold))
    final = pl.pallas_call(
        functools.partial(unpack_kernel, (f0, f1, f2, h, scales), back),
        out_shape=tuple(results.values()),
        in_specs=[vmem] * len(packed),
        out_specs=(anywhere,) * len(results),
        scratch_shapes=leaves[len(packed) + len(results) :],
        compiler_params=pltpu.CompilerParams(vmem_limit_bytes=46 << 20),
        name="unpack",
    )(*packed.values())
    final = Names(zip(results, final))
    return (
        final.output.reshape(f0, w, d, h),
        final.stem.reshape(w_stem.shape),
        final.mid.reshape(w_middle.shape),
        final.bot.reshape(w_bottom.shape),
        final.rise.reshape(3, 3, 3, f1, f2 + f1).transpose(0, 1, 2, 4, 3),
        final.fin.reshape(3, 3, 3, f0, f1 + f0).transpose(0, 1, 2, 4, 3),
        final.half.reshape(f0, w // 2, d // 2, h // 2),
    )


def solution(mesh):
    placed = (P("grp", "wid", "dep", "hgt"), P("grp", "wid", "dep", "hgt"), P(), P(), P(), P(), P())
    grad = P("grp", None, None, None, None)
    return jax.shard_map(
        local,
        mesh=mesh,
        in_specs=placed,
        out_specs=(P("grp", "wid", "dep", "hgt"), grad, grad, grad, grad, grad, P("grp", "wid", "dep", "hgt")),
        check_vma=False,
    )
```

```python
import functools
import math

import jax
import jax.numpy as jnp
from jax import lax
from jax.experimental import pallas as pl
from jax.experimental.pallas import tpu as pltpu
from jax.sharding import PartitionSpec as P

BF, F32 = jnp.bfloat16, jnp.float32
AXES = ("grp", "dep", "hgt", "wid")
GROUP = ("wid", "hgt", "dep")
TILE = 16


class Names(dict):
    __getattr__ = dict.__getitem__


def spread_out(tree):
    if not isinstance(tree, dict):
        return [tree], lambda leaves: next(leaves)
    parts = {k: spread_out(v) for k, v in tree.items()}
    leaves = [leaf for some, _ in parts.values() for leaf in some]
    return leaves, lambda leaves: Names({k: back(leaves) for k, (_, back) in parts.items()})


def mm(a, b):
    return lax.dot_general(a, b, (((1,), (0,)), ((), ())), preferred_element_type=F32)


def mm_nt(a, b):
    return lax.dot_general(a, b, (((1,), (1,)), ((), ())), preferred_element_type=F32)


def mm_split(a, b):
    high = a.astype(BF)
    low = (a - high.astype(F32)).astype(BF)
    return mm(high, b) + mm(low, b)


def silu(v):
    return v * jax.nn.sigmoid(v)


def slope(v):
    g = jax.nn.sigmoid(v)
    return g * (1.0 + v * (1.0 - g))


def pattern(lanes, test):
    row = lax.broadcasted_iota(jnp.int32, (lanes, lanes), 0)
    col = lax.broadcasted_iota(jnp.int32, (lanes, lanes), 1)
    return jnp.where(test(row, col), 1.0, 0.0)


def neighbours():
    count = 1
    for name in GROUP:
        count *= min(lax.axis_size(name), 3)
    return count - 1


def edge_rows(channels, rows, lanes):
    size = TILE
    while channels % size or rows * (channels // size) > lanes // 2:
        size += TILE
    return size


def lane_parts(channels, tall, h, lanes):
    count = lanes // h
    while channels % (tall * count):
        count -= 1
    return count


class Halo:
    def __init__(self, group, rows, packed, edges, own, span, sems):
        self.rows, self.edges, self.own = rows, edges, own
        self.packed = packed
        self.fold = rows.shape[2] // packed.shape[2]
        self.base, self.sent_base = group * neighbours(), group // 2 * neighbours()
        self.w, self.d, self.h = span
        self.send, self.recv = sems
        self.before = None
        self.unsent = False
        self.side = own.shape[1] // 2
        self.tall = own.shape[0]
        self.per = rows.shape[2] // self.tall

    def outer(self, a, b):
        return a in (0, self.w + 1) or b in (0, self.d + 1)

    def clear(self):
        moving = self.rows if self.fold == 1 else self.packed
        blank = jnp.zeros(moving.shape[2:], BF)
        for a in range(self.w + 2):
            for b in range(self.d + 2):
                if self.outer(a, b):
                    moving[a, b] = blank
        self.edges[...] = jnp.zeros(self.edges.shape, BF)

    def fill_edges(self):
        lane = lax.broadcasted_iota(jnp.int32, self.own.shape, 1)
        tile = jnp.zeros(self.own.shape, F32)
        for a in range(self.w):
            for b in range(self.d):
                row = self.rows[a + 1, b + 1].astype(F32)
                for g in range(self.per):
                    r = (a * self.d + b) * self.per + g
                    part_of = row[g * self.tall : (g + 1) * self.tall]
                    tile = jnp.where(lane == r, part_of[:, 0:1], tile)
                    tile = jnp.where(lane == self.side + r, part_of[:, self.h - 1 : self.h], tile)
        self.own[...] = tile.astype(BF)

    def pack(self):
        tall = self.packed.shape[2]
        for a in range(1, self.w + 1):
            for b in range(1, self.d + 1):
                wide = self.rows[a, b].astype(F32)
                total = wide[:tall]
                for g in range(1, self.fold):
                    total = total + pltpu.roll(wide[g * tall : (g + 1) * tall], g * self.h, 1)
                self.packed[a, b] = total.astype(BF)

    def copies(self):
        moving = self.rows if self.fold == 1 else self.packed
        place = {name: lax.axis_index(name) for name in AXES}
        size = {name: lax.axis_size(name) for name in AXES}

        def choices(name):
            i, n = place[name], size[name]
            if n == 1:
                return [(0, 0, True, True)]
            if n == 2:
                return [(0, 0, True, True), (1, 1 - 2 * i, True, True)]
            return [(0, 0, True, True), (1, 1, i < n - 1, i > 0), (2, -1, i > 0, i < n - 1)]

        def cells(step, code, count):
            if code == 0:
                return pl.ds(1, count), pl.ds(1, count)
            up = (1 + step) // 2
            return pl.ds(1 + (count - 1) * up, 1), pl.ds((count + 1) * (1 - up), 1)

        out = []
        for cw, sw, ow, iw in choices("wid"):
            for cd, sd, od, id_ in choices("dep"):
                for ch, sh, oh, ih in choices("hgt"):
                    if cw == 0 and cd == 0 and ch == 0:
                        continue
                    slot = self.base + len(out)
                    target = {"wid": place["wid"] + sw, "dep": place["dep"] + sd, "hgt": place["hgt"] + sh}
                    if ch == 0:
                        from_w, to_w = cells(sw, cw, self.w)
                        from_d, to_d = cells(sd, cd, self.d)
                        source = moving.at[from_w, from_d]
                        dest = moving.at[to_w, to_d]
                    else:
                        source = self.own
                        dest = self.edges.at[(1 - sh) // 2, 1 - sw, 1 - sd]
                    copy = pltpu.make_async_remote_copy(
                        src_ref=source,
                        dst_ref=dest,
                        send_sem=self.send.at[self.sent_base + len(out)],
                        recv_sem=self.recv.at[slot],
                        device_id=target,
                        device_id_type=pl.DeviceIdType.MESH,
                    )
                    steps = 2 * (cd > 0) + 2 * (ch > 0) + (cw > 0)
                    out.append((copy, [c for c in (ow, od, oh) if c is not True], [c for c in (iw, id_, ih) if c is not True], steps))
        return out

    @staticmethod
    def guarded(conditions, action):
        if not conditions:
            action()
        else:
            pl.when(functools.reduce(jnp.logical_and, conditions))(action)

    def start(self):
        if self.before is not None:
            self.before.finish()
        self.fill_edges()
        if self.fold > 1:
            self.pack()
        for copy, can_send, _, _ in sorted(self.copies(), key=lambda entry: -entry[3]):
            self.guarded(can_send, copy.start)
        self.unsent = True

    def wait(self):
        for copy, _, can_take, _ in self.copies():
            self.guarded(can_take, copy.wait_recv)

    def finish(self):
        if self.unsent:
            for copy, can_send, _, _ in self.copies():
                self.guarded(can_send, copy.wait_send)
        self.unsent = False

    def shifted(self, a, b, spread=None):
        lanes = self.own.shape[1]
        h = self.h if spread is None else 2 * self.h
        folded = self.fold > 1 and self.outer(a, b)
        tall = self.packed.shape[2] if folded else self.rows.shape[2]
        row = self.packed[a, b] if folded else self.rows[a, b]
        if spread is not None:
            pieces = [mm(row, spread[g]) for g in range(self.fold if folded else 1)]
            wide = pieces[0] if len(pieces) == 1 else jnp.concatenate(pieces, axis=0)
            row = wide.astype(BF)
            folded = False
        else:
            wide = row.astype(F32)
        dw = 0 if a == 0 else 2 if a == self.w + 1 else 1
        dd = 0 if b == 0 else 2 if b == self.d + 1 else 1
        r = ((self.w - 1, a - 1, 0)[dw] * self.d + (self.d - 1, b - 1, 0)[dd]) * self.per
        lane = lax.broadcasted_iota(jnp.int32, (self.tall, lanes), 1)
        low, high = self.edges[0, dw, dd].astype(F32), self.edges[1, dw, dd].astype(F32)
        befores, centres, afters = [], [], []
        for g in range(self.per):
            turn, from_row = divmod(g * self.tall, tall) if folded else (0, g * self.tall)
            here = wide[from_row : from_row + self.tall]
            left = low[:, self.side + r + g : self.side + r + g + 1]
            right = high[:, r + g : r + g + 1]
            before = jnp.where(lane == 0, left, pltpu.roll(here, (lanes + 1 - turn * h) % lanes, 1))
            after = jnp.where(lane == h - 1, right, pltpu.roll(here, lanes - 1 - turn * h, 1))
            if h < lanes:
                before = jnp.where(lane < h, before, 0.0)
                after = jnp.where(lane < h, after, 0.0)
            befores.append(before.astype(BF))
            afters.append(after.astype(BF))
            if folded:
                centre = pltpu.roll(here, lanes - turn * h, 1) if turn else here
                centres.append(jnp.where(lane < h, centre, 0.0).astype(BF))
        if folded:
            row = jnp.concatenate(centres, axis=0)
        return jnp.concatenate(befores, axis=0), row, jnp.concatenate(afters, axis=0)


def part(i, m):
    return pl.ds(pl.multiple_of(i * m, TILE), m)


def axis_part(axis):
    return (axis, 1, lax.axis_size(axis)) if isinstance(axis, str) else axis


def members(axes):
    return math.prod(axis_part(axis)[2] for axis in axes)


def position(axes):
    place, count = 0, 1
    for axis in axes:
        name, stride, n = axis_part(axis)
        index = lax.axis_index(name)
        if (stride, n) != (1, lax.axis_size(name)):
            index = lax.rem(lax.div(index, stride), n)
        place = place * n + index
        count *= n
    return place, count


def device_at(axes, place):
    where = {name: lax.axis_index(name) for name in GROUP}
    for axis in axes[::-1]:
        name, stride, n = axis_part(axis)
        to = place if axis == axes[0] else lax.rem(place, n)
        if n == lax.axis_size(name):
            where[name] = to
        else:
            where[name] = where[name] + (to - lax.rem(lax.div(where[name], stride), n)) * stride
        place = lax.div(place, n)
    return where


class Summed:
    def __init__(self, order, full, buffers, send, recv):
        self.order, self.full = order, full
        self.levels = [buffers[3 * i : 3 * i + 3] for i in range(len(order))]
        self.total = buffers[0]
        self.send, self.recv = send, recv
        self.stage, self.open, self.last = 0, None, None

    def copy(self, stage, axes, source, dest, to):
        return pltpu.make_async_remote_copy(
            src_ref=source,
            dst_ref=dest,
            send_sem=self.send.at[0],
            recv_sem=self.recv.at[stage],
            device_id=device_at(axes, to),
            device_id_type=pl.DeviceIdType.MESH,
        )

    def exchange(self, stage, axes, pieces, whole, m):
        i, n = position(axes)
        if n == 1:
            return
        self.settle()
        for k in sorted(range(1, n), key=lambda k: -min(k, n - k)):
            to = lax.rem(i + k, n)
            source, dest = pieces(to, i)
            self.copy(stage, axes, source, dest, to).start()
        every = whole.at[pl.ds(0, (n - 1) * m)]
        self.open = self.copy(stage, axes, every, every, lax.rem(i + 1, n))
        self.last = self.open

    def settle(self):
        if self.last is not None:
            self.last.wait_send()
            self.last = None

    def step(self):
        stage, deep = self.stage, len(self.order)
        self.stage += 1
        if self.open is not None:
            self.open.wait_recv()
            self.open = None
        if 0 < stage <= deep:
            i, n = position(self.order[stage - 1])
            held, _, came = self.levels[stage - 1]
            m = held.shape[0] // n
            value = held[part(i, m)]
            for k in range(1, n):
                value = value + came[part(lax.rem(i + k, n), m)].astype(F32)
            if stage < deep:
                self.levels[stage][0][...] = value
            else:
                place, _ = position([axis for axes in self.order for axis in axes])
                self.full[part(place, m)] = value.astype(BF)
        if stage < deep:
            held, wire, came = self.levels[stage]
            i, n = position(self.order[stage])
            m = held.shape[0] // n
            for k in range(1, n):
                there = part(lax.rem(i + k, n), m)
                wire[there] = held[there].astype(BF)
            self.exchange(stage, self.order[stage], lambda to, me: (wire.at[part(to, m)], came.at[part(me, m)]), came, m)
        elif stage < 2 * deep:
            depth = 2 * deep - stage
            place, count = position([axis for axes in self.order[:depth] for axis in axes])
            m = self.full.shape[0] // count
            piece = self.full.at[part(place, m)]
            self.exchange(stage, self.order[depth - 1], lambda to, me: (piece, piece), self.full, m)

    def finish(self):
        while self.stage <= 2 * len(self.order):
            self.step()
        self.settle()


HALOS = dict(
    feat=(0, 0, 0), half=(0, 1, 1), quarter=(1, 2, 0), deep=(2, 2, 1), rg=(1, 1, 0), dg=(2, 2, 1),
    mg=(1, 1, 0), cot=(0, 0, 2), stem=(0, 0, 3), mid=(1, 1, 2), ra=(1, 1, 3),
)
STACKS = dict(
    feat=(0, 0), cot=(0, 0), half=(0, 1), quarter=(1, 2), up2=(2, 1), mid=(1, 1), up1=(1, 0),
    stem=(0, 0), rg=(1, 1), dg=(2, 2), mg=(1, 1),
)


def blocks(size, lanes):
    return -(-size // lanes)


def split_at(count):
    return count * 4 // 9


def segments(f, lanes):
    f0, f1, f2 = f
    return dict(
        low=[(f1, blocks(27 * f1, lanes))],
        upa=[(f1, split_at(blocks(27 * f2, lanes)))],
        upb=[(f1, blocks(27 * f2, lanes) - split_at(blocks(27 * f2, lanes)))],
        bota=[(16 * f1, blocks(f2, lanes))],
        botb=[(11 * f1, blocks(f2, lanes))],
        early=[(3 * f0, blocks(9 * f0, lanes))],
        fin=[(3 * f0, blocks(9 * f1, lanes))],
        mid=[(f1, blocks(27 * f0, lanes))],
        stem=[(f0, blocks(27 * f0, lanes))],
    )


STAGED = (("wid",), ("hgt",), ("dep",))


def orders():
    near = (GROUP[:1], GROUP[1:]) if members(GROUP) <= 16 else STAGED
    n = lax.axis_size("dep")
    one, swap = ((GROUP,) if members(GROUP) <= 16 else STAGED), (STAGED[0], STAGED[2], STAGED[1])
    pairs = (*STAGED[:2], (("dep", 1, 2),), (("dep", 2, n // 2),)) if n % 2 == 0 else STAGED
    return dict(low=STAGED, upa=STAGED, upb=STAGED, bota=pairs, botb=pairs, early=STAGED, fin=STAGED, mid=STAGED, stem=near)


def step_kernel(cfg, back, *refs):
    (f0, f1, f2, w, d, h) = cfg
    ref = back(iter(refs))
    spans = {0: (w, d, h), 1: (w // 2, d // 2, h // 2), 2: (w // 4, d // 4, h // 4)}
    lanes = h
    halo = Names()
    last = {}
    for name, (_, level, group) in HALOS.items():
        own = ref.halos[name]
        halo[name] = Halo(group, own.rows, own.get(0, own.rows), own.edges, own.own, spans[level], (ref.send, ref.recv))
        halo[name].before = last.get(group // 2)
        last[group // 2] = halo[name]
    stacks = ref.stacks
    sums = Names()
    for name, order in orders().items():
        own = ref.sums[name]
        sums[name] = Summed(order, ref.outs[name], list(own.levels.values()), own.send, own.recv)

    loads = Names()
    for i, name in enumerate(ref.ins):
        loads[name] = pltpu.make_async_copy(ref.ins[name], ref.inside[name], ref.load.at[i])
        loads[name].start()
    halo.feat.clear()
    halo.cot.clear()

    def take(load, source, item):
        load.wait()
        ref.wide[...] = source[...].astype(F32)
        for a in range(w):
            for b in range(d):
                item.rows[a + 1, b + 1] = ref.wide[pl.ds(a * d + b, f0, stride=w * d), :].astype(BF)

    barrier = pltpu.get_barrier_semaphore()
    me, everyone = position(GROUP)
    for k in range(1, everyone):
        pl.semaphore_signal(
            barrier, 1, device_id=device_at(GROUP, lax.rem(me + k, everyone)), device_id_type=pl.DeviceIdType.MESH
        )
    take(loads.feat, ref.inside.feat, halo.feat)
    halo.half.clear()
    halo.stem.clear()
    pl.semaphore_wait(barrier, everyone - 1)

    halo.feat.start()
    take(loads.cot, ref.inside.cot, halo.cot)
    halo.cot.start()
    for item in (halo.quarter, halo.deep, halo.rg, halo.dg, halo.mg, halo.mid, halo.ra):
        item.clear()
    pool = pattern(lanes, lambda r, c: r // 2 == c)
    pool_mean = (pool / 8.0).astype(BF)
    pool_sum = pool.astype(BF)
    spread = pattern(lanes, lambda r, c: c // 2 == r)
    spread_mean = (spread / 8.0).astype(BF)

    def spreads(item):
        full = 2 * item.h
        each = [pattern(lanes, lambda r, c: (c < full) & (c // 2 == r - g * item.h)) for g in range(item.fold)]
        return [v.astype(BF) for v in each]

    def forward(raw, target):
        target[...] = raw[...].reshape(-1, raw.shape[2]).T

    def side_by_side(raw, target, low, high):
        width = high - low
        for k in range(raw.shape[0]):
            target[:, k * width : (k + 1) * width] = raw[k][:, low:high]

    loads.stem.wait()
    forward(ref.inside.stem, ref.w_stem)
    loads.fin.wait()
    forward(ref.inside.fin, ref.b_fin)
    side_by_side(ref.inside.fin, ref.w_fin_up, 0, f1)
    side_by_side(ref.inside.fin, ref.w_fin_low, f1, f1 + f0)
    loads.mid.wait()
    forward(ref.inside.mid, ref.w_mid)
    side_by_side(ref.inside.mid, ref.b_mid, 0, f1)
    loads.bot.wait()
    forward(ref.inside.bot, ref.w_bot)
    side_by_side(ref.inside.bot, ref.b_bot, 0, f2)
    loads.rise.wait()
    forward(ref.inside.rise, ref.b_rise)
    side_by_side(ref.inside.rise, ref.w_rise_up, 0, f2)
    side_by_side(ref.inside.rise, ref.w_rise_low, f2, f2 + f1)

    def stack(item, target, back=False):
        for a in range(item.w + 2):
            for b in range(item.d + 2):
                parts = item.shifted(a, b)
                target[a, b] = jnp.concatenate(parts[::-1] if back else parts, axis=0)

    def stack_up(up, target):
        spread = spreads(up)
        for i in range(up.w + 2):
            for j in range(up.d + 2):
                value = jnp.concatenate(up.shifted(i, j, spread), axis=0)
                for a in range(max(2 * i - 1, 0), min(2 * i + 1, target.shape[0])):
                    for b in range(max(2 * j - 1, 0), min(2 * j + 1, target.shape[1])):
                        target[a, b] = value

    def patch(source, a, b, pair, back=False, middle=False):
        third = source.shape[2] // 3
        rows = slice(third, 2 * third) if middle else slice(0, 3 * third)
        parts = []
        for q in range(pair):
            taps = [(ka, kb) for ka in range(3) for kb in range(3)]
            parts.append(
                jnp.concatenate([source[a + ka, b + kb + q, rows] for ka, kb in (taps[::-1] if back else taps)], axis=0)
            )
        return parts[0] if pair == 1 else jnp.concatenate(parts, axis=1)

    def over_rows(span, body):
        pair = 4 if span[1] % 4 == 0 else 2 if span[1] % 2 == 0 else 1
        across = span[1] // pair

        def trip(i, _):
            body(i // across, (i % across) * pair, pair)
            return 0

        count = span[0] * across
        if count <= 2:
            for i in range(count):
                trip(i, 0)
        else:
            lax.fori_loop(0, count, trip, 0)

    def conv(source, weight, span, store, back=False):
        def body(a, b, pair):
            result = mm(weight[...], patch(source, a, b, pair, back))
            for q in range(pair):
                store(a, b + q, result[:, q * lanes : (q + 1) * lanes])

        over_rows(span, body)

    def put_blocks(where, base, value):
        rows, width = value.shape
        count = blocks(width, lanes)
        if count * lanes > width:
            value = jnp.concatenate([value, jnp.zeros((rows, count * lanes - width), value.dtype)], axis=1)
        for j in range(count):
            where[base + j * rows : base + (j + 1) * rows] = value[:, j * lanes : (j + 1) * lanes]

    def beside(span, pick):
        return jnp.concatenate([pick(a, b) for a in range(span[0]) for b in range(span[1])], axis=1)

    halo.feat.wait()
    stack(halo.feat, stacks.feat)

    def stem_store(a, b, value):
        ref.stem_pre[a, b] = value
        halo.stem.rows[a + 1, b + 1] = silu(value).astype(BF)

    conv(stacks.feat, ref.w_stem, spans[0], stem_store)

    def pooled(fine, coarse):
        low, up = fine, coarse
        for a in range(up.w):
            for b in range(up.d):
                cat = [low.rows[2 * a + 1 + i, 2 * b + 1 + j] for i in range(2) for j in range(2)]
                total = mm(cat[0], pool_mean) + mm(cat[1], pool_mean) + mm(cat[2], pool_mean) + mm(cat[3], pool_mean)
                up.rows[a + 1, b + 1] = total.astype(BF)

    pooled(halo.stem, halo.half)
    halo.cot.wait()
    halo.half.start()
    halo.stem.start()
    stack(halo.cot, stacks.cot, back=True)
    ref.fb_pool[...] = jnp.zeros(ref.fb_pool.shape, F32)

    def back_store(a, b, value):
        ref.fb_pool[a // 2, b // 2] += value[:f1]
        ref.fb_skip[a, b] = value[f1:]

    conv(stacks.cot, ref.b_fin, spans[0], back_store, back=True)
    for a in range(spans[1][0]):
        for b in range(spans[1][1]):
            ref.fb_pool[a, b] = mm_split(ref.fb_pool[a, b], pool_sum)
    halo.half.wait()
    stack(halo.half, stacks.half)

    def mid_store(a, b, value):
        ref.mid_pre[a, b] = value
        halo.mid.rows[a + 1, b + 1] = silu(value).astype(BF)

    conv(stacks.half, ref.w_mid, spans[1], mid_store)
    pooled(halo.mid, halo.quarter)
    halo.quarter.start()
    halo.mid.start()
    halo.stem.wait()
    stack(halo.stem, stacks.stem)

    def final_low(a, b, value):
        ref.fin_part[a, b] = value

    conv(stacks.stem, ref.w_fin_low, spans[0], final_low)
    cot_cells = lambda: beside(spans[0], lambda a, b: stacks.cot[a + 1, b + 1])
    low_cells = beside(spans[0], lambda a, b: patch(stacks.stem, a, b, 1, middle=True))
    put_blocks(sums.early.total, 0, mm_nt(cot_cells(), low_cells))
    sums.early.step()
    halo.quarter.wait()
    stack(halo.quarter, stacks.quarter)

    def deep_store(a, b, value):
        ref.deep_pre[a, b] = value
        halo.deep.rows[a + 1, b + 1] = silu(value).astype(BF)

    conv(stacks.quarter, ref.w_bot, spans[2], deep_store)
    halo.deep.start()
    halo.mid.wait()
    stack(halo.mid, stacks.mid)

    def rise_low(a, b, value):
        ref.rise_pre[a, b] = value

    conv(stacks.mid, ref.w_rise_low, spans[1], rise_low)
    sums.early.step()
    for held in (ref.stem_pre, ref.mid_pre, ref.deep_pre):
        for a in range(held.shape[0]):
            for b in range(held.shape[1]):
                held[a, b] = slope(held[a, b])
    halo.deep.wait()
    stack_up(halo.deep, stacks.up2)

    def rise_store(a, b, value):
        value = value + ref.rise_pre[a, b]
        halo.ra.rows[a + 1, b + 1] = silu(value).astype(BF)
        grad = ref.fb_pool[a, b] * slope(value)
        halo.rg.rows[a + 1, b + 1] = grad.astype(BF)

    conv(stacks.up2, ref.w_rise_up, spans[1], rise_store)
    halo.rg.start()
    halo.ra.start()
    sums.early.step()

    grad1 = lambda item: beside(spans[1], lambda a, b: item.rows[a + 1, b + 1])

    def wide_wgrad(segment, grad, source, span, low=None, high=None):
        cells = beside(span, lambda a, b: patch(source, a, b, 1)[low:high])
        put_blocks(segment.total, 0, mm_nt(grad, cells))

    wide_wgrad(sums.low, grad1(halo.rg), stacks.mid, spans[1])
    sums.low.step()
    cut = split_at(blocks(27 * f2, lanes)) * lanes
    wide_wgrad(sums.upa, grad1(halo.rg), stacks.up2, spans[1], None, cut)
    sums.upa.step()
    wide_wgrad(sums.upb, grad1(halo.rg), stacks.up2, spans[1], cut, None)
    sums.low.step()
    sums.upb.step()
    sums.upa.step()
    halo.rg.wait()
    stack(halo.rg, stacks.rg, back=True)
    deep_sum = [[None] * spans[2][1] for _ in range(spans[2][0])]
    pair1 = 2 if spans[1][1] % 2 == 0 else 1
    for a in range(spans[1][0]):
        for b in range(0, spans[1][1], pair1):
            result = mm(ref.b_rise[...], patch(stacks.rg, a, b, pair1, back=True))
            for q in range(pair1):
                value = result[:, q * lanes : (q + 1) * lanes]
                ref.rb_skip[a, b + q] = value[f2:]
                ap, bt = a // 2, (b + q) // 2
                old = deep_sum[ap][bt]
                deep_sum[ap][bt] = value[:f2] if old is None else old + value[:f2]
    for a in range(spans[2][0]):
        for b in range(spans[2][1]):
            grad = mm_split(deep_sum[a][b], pool_sum) * ref.deep_pre[a, b]
            halo.dg.rows[a + 1, b + 1] = grad.astype(BF)
    halo.dg.start()
    sums.upb.step()
    cells2 = beside(spans[2], lambda a, b: patch(stacks.quarter, a, b, 1))
    grad2 = beside(spans[2], lambda a, b: halo.dg.rows[a + 1, b + 1])
    bot = mm_nt(cells2, grad2)
    put_blocks(sums.bota.total, 0, bot[: 16 * f1])
    put_blocks(sums.botb.total, 0, bot[16 * f1 :])
    sums.bota.step()
    sums.botb.step()
    sums.early.step()
    halo.ra.wait()
    stack_up(halo.ra, stacks.up1)
    sums.low.step()
    up_cells = beside(spans[0], lambda a, b: patch(stacks.up1, a, b, 1, middle=True))
    put_blocks(sums.fin.total, 0, mm_nt(cot_cells(), up_cells))
    sums.bota.step()
    sums.botb.step()
    sums.upa.step()
    sums.fin.step()
    halo.dg.wait()
    stack(halo.dg, stacks.dg, back=True)

    def quarter_store(a, b, value):
        wide = mm_split(value, spread_mean)
        for i in range(2):
            for j in range(2):
                at_, bt = 2 * a + i, 2 * b + j
                grad = (ref.rb_skip[at_, bt] + wide) * ref.mid_pre[at_, bt]
                halo.mg.rows[at_ + 1, bt + 1] = grad.astype(BF)

    conv(stacks.dg, ref.b_bot, spans[2], quarter_store, back=True)
    halo.mg.start()
    sums.fin.step()
    sums.upb.step()

    def final_row(a):
        result = mm(ref.w_fin_up[...], patch(stacks.up1, a, 0, d))
        for b in range(d):
            value = ref.fin_part[a, b] + result[:, b * lanes : (b + 1) * lanes]
            ref.wide[pl.ds(a * d + b, f0, stride=w * d), :] = value

    wide_wgrad(sums.mid, grad1(halo.mg), stacks.half, spans[1])
    sums.mid.step()
    sums.low.step()
    sums.early.step()
    sums.bota.step()
    final_row(0)
    final_row(1)
    sums.botb.step()
    sums.upa.step()
    final_row(2)
    sums.mid.step()
    final_row(3)
    ref.outs.output[...] = ref.wide[...].astype(BF)
    sums.fin.step()
    halo.mg.wait()
    stack(halo.mg, stacks.mg, back=True)

    def half_store(a, b, value):
        ref.half_wide[pl.ds(a * spans[1][1] + b, f0, stride=spans[1][0] * spans[1][1]), :] = value
        wide = mm_split(value, spread_mean)
        for i in range(2):
            for j in range(2):
                at_, bt = 2 * a + i, 2 * b + j
                grad = (ref.fb_skip[at_, bt] + wide) * ref.stem_pre[at_, bt]
                ref.stem_grad[at_, bt] = grad.astype(BF)

    conv(stacks.mg, ref.b_mid, spans[1], half_store, back=True)
    ref.outs.half[...] = ref.half_wide[...]
    sums.bota.step()
    sums.upb.step()
    wide_wgrad(sums.stem, beside(spans[0], lambda a, b: ref.stem_grad[a, b]), stacks.feat, spans[0])
    sums.stem.step()
    sums.low.step()
    sums.botb.step()
    sums.upa.step()

    sums.mid.step()
    sums.fin.step()
    sums.stem.step()
    sums.bota.step()
    sums.low.step()
    sums.early.step()
    sums.upb.step()
    sums.botb.step()
    sums.upa.step()
    sums.mid.step()
    sums.fin.step()
    sums.bota.step()
    sums.low.step()
    sums.upa.step()
    sums.upb.step()
    sums.botb.step()
    sums.stem.step()
    sums.mid.step()
    sums.fin.step()
    sums.bota.step()
    sums.upb.step()
    sums.botb.step()
    sums.stem.step()
    sums.mid.step()
    sums.bota.step()
    sums.fin.step()
    sums.early.step()
    sums.stem.step()
    sums.botb.step()
    sums.bota.step()
    sums.mid.step()
    sums.botb.step()
    for item in sums.values():
        item.finish()
    for item in halo.values():
        item.finish()


def unpack_kernel(cfg, back, *refs):
    (f0, f1, f2, lanes, scales) = cfg
    ref = back(iter(refs))
    stores = []

    def send(source, target):
        copy = pltpu.make_async_copy(source, target, ref.store.at[len(stores)])
        copy.start()
        stores.append(copy)

    def side(source, base, rows, width, scale):
        count = blocks(width, lanes)
        value = [source[base + j * rows : base + (j + 1) * rows].astype(F32) * scale for j in range(count)]
        return jnp.concatenate(value, axis=1)

    send(ref.ins.output, ref.outs.output)
    ref.ready.half[...] = ref.ins.half[:, : lanes // 2]
    send(ref.ready.half, ref.outs.half)
    ref.ready.bot[: 16 * f1] = side(ref.ins.bota, 0, 16 * f1, f2, scales.bot)[:, :f2]
    ref.ready.bot[16 * f1 :] = side(ref.ins.botb, 0, 11 * f1, f2, scales.bot)[:, :f2]
    send(ref.ready.bot, ref.outs.bot)
    low = side(ref.ins.low, 0, f1, 27 * f1, scales.rise)
    first = split_at(blocks(27 * f2, lanes))
    up = [side(ref.ins.upa, 0, f1, first * lanes, scales.rise)]
    up.append(side(ref.ins.upb, 0, f1, 27 * f2 - first * lanes, scales.rise))
    up = jnp.concatenate(up, axis=1)
    for k in range(27):
        ref.ready.rise[k] = jnp.concatenate([up[:, k * f2 : (k + 1) * f2], low[:, k * f1 : (k + 1) * f1]], axis=1)
    send(ref.ready.rise, ref.outs.rise)
    up = side(ref.ins.fin, 0, 3 * f0, 9 * f1, scales.fin)
    low = side(ref.ins.early, 0, 3 * f0, 9 * f0, scales.fin)
    for k in range(27):
        at_, rows = k // 3, slice((k % 3) * f0, (k % 3 + 1) * f0)
        ref.ready.fin[k] = jnp.concatenate([up[rows, at_ * f1 : (at_ + 1) * f1], low[rows, at_ * f0 : (at_ + 1) * f0]], axis=1)
    send(ref.ready.fin, ref.outs.fin)
    for source, target, out, scale in (
        (ref.ins.mid, ref.ready.mid, ref.outs.mid, scales.mid),
        (ref.ins.stem, ref.ready.stem, ref.outs.stem, scales.stem),
    ):
        width = target.shape[1]
        for j in range(blocks(27 * f0, lanes)):
            value = (source[j * width : (j + 1) * width].astype(F32) * scale).T
            rows = min(lanes, 27 * f0 - j * lanes)
            target[j * lanes : j * lanes + rows] = value[:rows]
        send(target, out)
    for copy in stores:
        copy.wait()


def local(features, cotangent, w_stem, w_middle, w_bottom, w_rise, w_final):
    f0, w, d, h = features.shape
    f1, f2 = w_middle.shape[4], w_bottom.shape[4]
    f = (f0, f1, f2)
    spans = {0: (w, d), 1: (w // 2, d // 2), 2: (w // 4, d // 4)}
    near = neighbours()
    sets = 1 + max(group for _, _, group in HALOS.values())
    flat = w * d * f0
    inputs = dict(
        feat=features.reshape(flat, h),
        cot=cotangent.reshape(flat, h),
        stem=w_stem.reshape(27, f0, f0),
        fin=w_final.transpose(0, 1, 2, 4, 3).reshape(27, f0, f1 + f0),
        mid=w_middle.reshape(27, f0, f1),
        bot=w_bottom.reshape(27, f1, f2),
        rise=w_rise.transpose(0, 1, 2, 4, 3).reshape(27, f1, f2 + f1),
    )
    outs = dict(output=jax.ShapeDtypeStruct((flat, h), BF), half=jax.ShapeDtypeStruct((flat // 4, h), F32))
    halos, sums = {}, {}
    for name, (c, level, _) in HALOS.items():
        a, b = spans[level]
        tall = edge_rows(f[c], a * b, h)
        halos[name] = dict(
            rows=pltpu.VMEM((a + 2, b + 2, f[c], h), BF),
            edges=pltpu.VMEM((2, 3, 3, tall, h), BF),
            own=pltpu.VMEM((tall, h), BF),
        )
        fold = lane_parts(f[c], tall, h >> level, h)
        if fold > 1:
            halos[name][0] = pltpu.VMEM((a + 2, b + 2, f[c] // fold, h), BF)
    place = segments(f, h)
    for name, order in orders().items():
        unit = TILE * members(GROUP)
        rows = -(-sum(a * b for a, b in place[name]) // unit) * unit
        outs[name] = jax.ShapeDtypeStruct((rows, h), BF)
        levels = {}
        for i, axes in enumerate(order):
            for j, kind in enumerate((F32, BF, BF)):
                levels[3 * i + j] = pltpu.VMEM((rows, h), kind)
            rows //= members(axes)
        sums[name] = dict(levels=levels, send=pltpu.SemaphoreType.DMA((1,)), recv=pltpu.SemaphoreType.DMA((2 * len(order),)))

    def cells_of(c, level, kind=F32):
        return pltpu.VMEM((*spans[level], c, h), kind)

    def taps(a, b):
        return pltpu.VMEM((a, 27 * b), BF)

    scratch = dict(
        send=pltpu.SemaphoreType.DMA((blocks(sets, 2) * near,)),
        recv=pltpu.SemaphoreType.DMA((sets * near,)),
        load=pltpu.SemaphoreType.DMA((len(inputs),)),
        inside={name: pltpu.VMEM(v.shape, BF) for name, v in inputs.items()},
        halos=halos,
        sums=sums,
        stacks={
            name: pltpu.VMEM((spans[level][0] + 2, spans[level][1] + 2, 3 * f[c], h), BF)
            for name, (c, level) in STACKS.items()
        },
        stem_pre=cells_of(f0, 0), mid_pre=cells_of(f1, 1), deep_pre=cells_of(f2, 2), rise_pre=cells_of(f1, 1),
        fb_pool=cells_of(f1, 1), fb_skip=cells_of(f0, 0), rb_skip=cells_of(f1, 1), fin_part=cells_of(f0, 0),
        stem_grad=cells_of(f0, 0, BF),
        wide=pltpu.VMEM((flat, h), F32), half_wide=pltpu.VMEM((flat // 4, h), F32),
        w_stem=taps(f0, f0), w_mid=taps(f1, f0), w_bot=taps(f2, f1), w_rise_up=taps(f1, f2), w_rise_low=taps(f1, f1),
        w_fin_up=taps(f0, f1), w_fin_low=taps(f0, f0), b_mid=taps(f0, f1), b_bot=taps(f1, f2),
        b_rise=taps(f2 + f1, f1), b_fin=taps(f1 + f0, f0),
    )
    grant = 46 if members(GROUP) <= 16 else 60
    vmem = pl.BlockSpec(memory_space=pltpu.VMEM)
    anywhere = pl.BlockSpec(memory_space=pl.ANY)
    leaves, back = spread_out(dict(ins=inputs, outs=outs, **scratch))
    done = pl.pallas_call(
        functools.partial(step_kernel, (f0, f1, f2, w, d, h), back),
        out_shape=tuple(outs.values()),
        in_specs=[anywhere] * len(inputs),
        out_specs=(vmem,) * len(outs),
        scratch_shapes=leaves[len(inputs) + len(outs) :],
        compiler_params=pltpu.CompilerParams(collective_id=0, has_side_effects=True, vmem_limit_bytes=grant << 20),
        name="unet_step",
    )(*[pltpu.with_memory_space_constraint(v, pltpu.HBM) for v in inputs.values()])
    packed = dict(zip(outs, done))
    cells = w * d * h * members(GROUP)
    fine, mid, deep = (1.0 / math.sqrt(cells / k) for k in (1.0, 8.0, 64.0))
    scales = Names(stem=fine, mid=mid, bot=deep, rise=mid, fin=fine)

    results = dict(
        output=jax.ShapeDtypeStruct((flat, h), BF),
        stem=jax.ShapeDtypeStruct((27 * f0, f0), F32),
        mid=jax.ShapeDtypeStruct((27 * f0, f1), F32),
        bot=jax.ShapeDtypeStruct((27 * f1, f2), F32),
        rise=jax.ShapeDtypeStruct((27, f1, f2 + f1), F32),
        fin=jax.ShapeDtypeStruct((27, f0, f1 + f0), F32),
        half=jax.ShapeDtypeStruct((flat // 4, h // 2), F32),
    )
    hold = dict(
        ready={n: pltpu.VMEM(v.shape, v.dtype) for n, v in results.items()},
        store=pltpu.SemaphoreType.DMA((len(results),)),
    )
    leaves, back = spread_out(dict(ins=packed, outs=results, **hold))
    final = pl.pallas_call(
        functools.partial(unpack_kernel, (f0, f1, f2, h, scales), back),
        out_shape=tuple(results.values()),
        in_specs=[vmem] * len(packed),
        out_specs=(anywhere,) * len(results),
        scratch_shapes=leaves[len(packed) + len(results) :],
        compiler_params=pltpu.CompilerParams(vmem_limit_bytes=46 << 20),
        name="unpack",
    )(*packed.values())
    final = Names(zip(results, final))
    return (
        final.output.reshape(f0, w, d, h),
        final.stem.reshape(w_stem.shape),
        final.mid.reshape(w_middle.shape),
        final.bot.reshape(w_bottom.shape),
        final.rise.reshape(3, 3, 3, f1, f2 + f1).transpose(0, 1, 2, 4, 3),
        final.fin.reshape(3, 3, 3, f0, f1 + f0).transpose(0, 1, 2, 4, 3),
        final.half.reshape(f0, w // 2, d // 2, h // 2),
    )


def solution(mesh):
    placed = (P("grp", "wid", "dep", "hgt"), P("grp", "wid", "dep", "hgt"), P(), P(), P(), P(), P())
    grad = P("grp", None, None, None, None)
    return jax.shard_map(
        local,
        mesh=mesh,
        in_specs=placed,
        out_specs=(P("grp", "wid", "dep", "hgt"), grad, grad, grad, grad, grad, P("grp", "wid", "dep", "hgt")),
        check_vma=False,
    )
```
